32 devices in a mesh: dp: 2 (over x), fsdp: 16 (over z, y, core).
Axes of the slice: x: 2, y: 2, z: 4, core: 2. Of those that a mesh axis runs over, the one named last changes fastest.
Arguments:
- inputs: bfloat16 [16, 1024, 1024], P('fsdp', 'dp'), may hold values from -6 to 6
- segment_ids: int32 [16, 1024], P('fsdp', 'dp'), may hold values from 0 to 2, never falling along the last dimension, each value on 1 to 512 neighbouring positions
- key_mask: int32 [16, 1024], P('fsdp', 'dp'), may hold values 0 or 1
- lead_index: int32 [16, 2], P('fsdp'), may hold values from 0 to 7
- cotangent_first: bfloat16 [16, 1024, 1024], P('fsdp', 'dp'), may hold values from -6 to 6
- cotangent_second: bfloat16 [16, 1024, 1024], P('fsdp', 'dp'), may hold values from -6 to 6
- w_qkv: bfloat16 [1024, 3072], P(('dp', 'fsdp')), may hold values from -0.1875 to 0.1875
- w_out: bfloat16 [1024, 1024], P(('dp', 'fsdp')), may hold values from -3 to 3
- w_up: bfloat16 [1024, 4096], P(('dp', 'fsdp')), may hold values from -0.1875 to 0.1875
- w_down: bfloat16 [4096, 1024], P(('dp', 'fsdp')), may hold values from -0.09375 to 0.09375
- biases: bfloat16 [4, 1024], P(None, ('dp', 'fsdp')), may hold values from -3 to 3
- up_bias: bfloat16 [4096], P(('dp', 'fsdp')), may hold values from -3 to 3
- norm_gains: bfloat16 [2, 1024], P(None, ('dp', 'fsdp')), may hold values from 0.099609375 to 1.8984375
- norm_shifts: bfloat16 [2, 1024], P(None, ('dp', 'fsdp')), may hold values from -2 to 2
- lead_table: bfloat16 [8, 1024], P(None, ('dp', 'fsdp')), may hold values from -5 to 5
Outputs:
- first_out: bfloat16 [16, 1024, 1024], P('fsdp', 'dp')
- second_out: bfloat16 [16, 1024, 1024], P('fsdp', 'dp')
- input_grad: float32 [16, 1024, 1024], P('fsdp', 'dp')
- grad_qkv: float32 [1024, 3072], P(('dp', 'fsdp'))
- grad_out: float32 [1024, 1024], P(('dp', 'fsdp'))
- grad_up: float32 [1024, 4096], P(('dp', 'fsdp'))
- grad_down: float32 [4096, 1024], P(('dp', 'fsdp'))
- grad_biases: float32 [4, 1024], P(None, ('dp', 'fsdp'))
- grad_up_bias: float32 [4096], P(('dp', 'fsdp'))
- grad_gains: float32 [2, 1024], P(None, ('dp', 'fsdp'))
- grad_shifts: float32 [2, 1024], P(None, ('dp', 'fsdp'))
- grad_lead: float32 [8, 1024], P(None, ('dp', 'fsdp'))
The draws below stay inside these ranges and needn't reach their ends.
Inputs may be any that keep to these rules, and one draw needn't show every extreme that they name: `segment_ids`: sample numbers never fall along a group; each sample has 1 to min(2048, 512) patches, and one of each group has exactly min(2048, 512).
All inputs are finite; a program needn't handle non-finite values. No bound on the sum of `key_mask` on one device may be relied on, other than what follows from the above.
Results may differ from the reference program's by a relative error of at most 0.013.
Values may be sent and summed in bfloat16 or wider, within the bound.
No kernel may reach another device: no remote copies, remote signals or barrier semaphores. Data moves between devices by JAX's collectives and lax.ppermute only.
A program may use at most 256 MiB of HBM per device.

```python
import math
from functools import partial
import jax
import jax.numpy as jnp
import numpy as np
from jax import lax

D = 1024
HEADS = 16
HEAD = 64
FF = 4096
LEADS = 8
GROUP = 1024
GROUPS = 16


def plant(drawn, rng, least, top_value):
    dims = drawn.shape
    spot = [jax.random.randint(jax.random.fold_in(rng, axis), (), 0, dims[axis]) for axis in range(len(dims))]
    drawn = drawn.at[tuple(spot)].set(least)
    longest = dims.index(max(dims))
    spot[longest] = (spot[longest] + 1) % dims[longest]
    return drawn.at[tuple(spot)].set(top_value)


def steps_of(key, shape, shards, least, high):
    gain, own = 1.0, jax.random.fold_in(key, 6)
    for axis_at, shards_of in shards:
        steps = jnp.exp(jax.random.uniform(jax.random.fold_in(own, axis_at), (shards_of,), jnp.float32, least / len(shards), high / len(shards)))
        gain = gain * jnp.repeat(steps, shape[axis_at] // shards_of).reshape([-1 if axis == axis_at else 1 for axis in range(len(shape))])
    return gain


def length_profile(amount, total, most, slope):
    weights = [(1 << 20) // math.isqrt(standing ** slope) + 1 for standing in range(2, amount + 1)]
    surplus, counts = total - most - (amount - 1), [1] * (amount - 1)
    while surplus > 0:
        candidates = [i for i in range(amount - 1) if counts[i] < most]
        mass, budget = sum([weights[i] for i in candidates]), surplus
        for i in candidates:
            more = min(most - counts[i], max(1, budget * weights[i] // mass), surplus)
            counts[i] = counts[i] + more
            surplus = surplus - more
    return np.array([most] + counts)


def ragged_sizes(stream_key, amount, total, bound, slope):
    if amount == 2:
        one = jax.random.randint(stream_key, (), max(1, total - bound), min(bound, total - 1) + 1)
        return jnp.stack([one, total - one])
    tallies = jnp.asarray(length_profile(amount, total, bound, slope), jnp.int32)
    twos = (amount - 1) // 2
    giver, sink = tallies[1:1 + 2 * twos:2], tallies[2:2 + 2 * twos:2]
    slack = jnp.minimum(giver - 1, bound - sink)
    shifted = jax.random.randint(jax.random.fold_in(stream_key, 1), (twos,), 0, 1 << 20) % (slack + 1)
    tallies = tallies.at[1:1 + 2 * twos:2].set(giver - shifted).at[2:2 + 2 * twos:2].set(sink + shifted)
    return tallies[jax.random.permutation(jax.random.fold_in(stream_key, 2), amount)]


def scatter_about(rng, shape, width, reach, shards=(), kind=jnp.bfloat16):
    gain = steps_of(rng, shape, shards, -0.22, 0.18) if shards else 1.0
    values = jax.random.normal(rng, shape, jnp.float32) * width * gain
    return jnp.minimum(jnp.maximum(values, -reach), reach).astype(kind)


def setup_inputs(seed: int = 0) -> dict:
    seeds = jax.random.split(jax.random.key(seed), 16)
    inputs = scatter_about(seeds[0], (GROUPS, GROUP, D), 1.0, 6.0, ((0, 16), (1, 2)))
    segment_ids = jax.vmap(lambda own: jnp.searchsorted(jnp.cumsum(ragged_sizes(own, 3, GROUP, min(2048, GROUP // 2), 0)), jnp.arange(GROUP), side="right"))(jax.random.split(seeds[1], GROUPS)).reshape((GROUPS, GROUP)).astype(jnp.int32)
    key_mask = plant((jax.random.randint(seeds[2], (GROUPS, GROUP), 0, 8) < 7).astype(jnp.int32), jax.random.fold_in(seeds[2], 1), 0, 1)
    lead_index = plant(jax.random.randint(seeds[3], (GROUPS, 2), 0, LEADS), jax.random.fold_in(seeds[3], 1), 0, LEADS - 1).astype(jnp.int32)
    cotangent_first = scatter_about(seeds[4], (GROUPS, GROUP, D), 1.0, 6.0, ((0, 16), (1, 2)))
    cotangent_second = scatter_about(seeds[5], (GROUPS, GROUP, D), 1.0, 6.0, ((0, 16), (1, 2)))
    w_qkv = scatter_about(seeds[6], (D, 3 * D), D ** -0.5, 0.1875, ((0, 32),))
    w_out = scatter_about(seeds[7], (D, D), (max(D // 256, 1)) ** -0.5, 3.0, ((0, 32),))
    w_up = scatter_about(seeds[8], (D, FF), D ** -0.5, 0.1875, ((0, 32),))
    w_down = scatter_about(seeds[9], (FF, D), FF ** -0.5, 0.09375, ((0, 32),))
    biases = scatter_about(seeds[10], (4, D), 0.5, 3.0, ((1, 32),))
    up_bias = scatter_about(seeds[11], (FF,), 0.5, 3.0, ((0, 32),))
    norm_gains = jnp.clip(1.0 + 0.18 * jax.random.normal(seeds[12], (2, D), jnp.float32), 0.099609375, 1.8984375).astype(jnp.bfloat16)
    norm_shifts = scatter_about(seeds[13], (2, D), 0.3, 2.0, ((1, 32),))
    lead_table = scatter_about(seeds[14], (LEADS, D), 1.0, 5.0, ((1, 32),))
    return {"inputs": inputs, "segment_ids": segment_ids, "key_mask": key_mask, "lead_index": lead_index, "cotangent_first": cotangent_first, "cotangent_second": cotangent_second, "w_qkv": w_qkv, "w_out": w_out, "w_up": w_up, "w_down": w_down, "biases": biases, "up_bias": up_bias, "norm_gains": norm_gains, "norm_shifts": norm_shifts, "lead_table": lead_table}


@jax.custom_vjp
def low(v):
    return lax.optimization_barrier(v.astype(jnp.bfloat16)).astype(jnp.float32)

@jax.custom_vjp
def low_back(v):
    return v

def low_keep(v):
    return (low(v), None)

def low_pass(kept, grad):
    return (grad,)

def back_keep(v):
    return (v, None)

def back_low(kept, grad):
    return (low(grad),)
low.defvjp(low_keep, low_pass)
low_back.defvjp(back_keep, back_low)
SCALE = 0.125
EPSILON = 1e-06
NEGATIVE = -1e+30
PRECISE = lax.Precision.HIGHEST

def layer_norm(tensor, gain_row, shift_row):
    average = lax.optimization_barrier(jnp.mean(tensor, axis=-1, keepdims=True))
    centred = tensor - average
    variance = lax.optimization_barrier(jnp.mean(centred * centred, axis=-1, keepdims=True))
    return centred * lax.rsqrt(variance + EPSILON) * gain_row + shift_row

def product(left_side, right_side):
    return jnp.dot(left_side, right_side, precision=PRECISE, preferred_element_type=jnp.float32)

def round_both(tensor):
    return low(low_back(tensor))

def attend(query, keys, values, segment, opened):
    group = query.shape[0]
    stride = min(512, group)
    count = group // stride
    query_blocks = query.reshape(count, stride, HEADS, HEAD)
    segment_blocks = segment.reshape(count, stride)
    keys_heads = keys.reshape(group, HEADS, HEAD)
    values_heads = values.reshape(group, HEADS, HEAD)
    columns = jnp.arange(group, dtype=jnp.int32)

    def one_block(item):
        query_block, segment_block, first_row = item
        rows = first_row + jnp.arange(stride, dtype=jnp.int32)
        logits = jnp.einsum('bhd,khd->hbk', query_block, keys_heads, precision=PRECISE) * SCALE
        logits = low_back(logits)
        allowed = (segment_block[:, None] == segment[None, :]) & ((opened[None, :] == 1) | (rows[:, None] == columns[None, :]))
        masked = jnp.where(allowed[None], logits, NEGATIVE)
        highest = lax.optimization_barrier(jnp.max(masked, axis=-1, keepdims=True))
        denominator = lax.optimization_barrier(jnp.sum(jnp.exp(masked - highest), axis=-1, keepdims=True))
        probs = jnp.exp(masked - (highest + jnp.log(denominator)))
        output = jnp.einsum('hbk,khd->bhd', low(probs), values_heads, precision=PRECISE)
        return output.reshape(stride, HEADS * HEAD)
    starts = jnp.arange(count, dtype=jnp.int32) * stride
    output = lax.map(jax.checkpoint(one_block), (query_blocks, segment_blocks, starts))
    return output.reshape(group, HEADS * HEAD)

def block_layer(tensor, lead_row, segment, opened, params):
    weight_qkv, weight_out, weight_up, weight_down, bias_rows, bias_up, gain_rows, shift_rows, lead_rows = params
    hidden = tensor + lead_row[None, :]
    normed = low(layer_norm(hidden, gain_rows[0], shift_rows[0]))
    mixed = product(normed, weight_qkv)
    query = round_both(mixed[:, :D] + bias_rows[0])
    keys = round_both(mixed[:, D:2 * D])
    values = round_both(mixed[:, 2 * D:] + bias_rows[1])
    attn = round_both(attend(query, keys, values, segment, opened))
    branch = low_back(product(attn, weight_out) + bias_rows[2])
    middle = hidden + branch
    normed_mid = low(layer_norm(middle, gain_rows[1], shift_rows[1]))
    gate_in = low_back(product(normed_mid, weight_up) + bias_up)
    activated = low(jax.nn.gelu(gate_in, approximate=False))
    feed = low_back(product(activated, weight_down) + bias_rows[3])
    return middle + feed

def group_forward(params, item):
    tensor, segment, opened, leads = item
    lead_rows = params[8]
    first = low(block_layer(tensor, lead_rows[leads[0]], segment, opened, params))
    second = low(block_layer(first, lead_rows[leads[1]], segment, opened, params))
    return (first, second)

def reference(inputs, segment_ids, key_mask, lead_index, cotangent_first, cotangent_second, w_qkv, w_out, w_up, w_down, biases, up_bias, norm_gains, norm_shifts, lead_table):
    params = (w_qkv.astype(jnp.float32), w_out.astype(jnp.float32), w_up.astype(jnp.float32), w_down.astype(jnp.float32), biases.astype(jnp.float32), up_bias.astype(jnp.float32), norm_gains.astype(jnp.float32), norm_shifts.astype(jnp.float32), lead_table.astype(jnp.float32))

    def forward(tensor, weights):
        return lax.map(partial(group_forward, weights), (tensor, segment_ids, key_mask, lead_index))
    outputs, pull = jax.vjp(forward, inputs.astype(jnp.float32), params)
    input_grad, grads = pull((cotangent_first.astype(jnp.float32), cotangent_second.astype(jnp.float32)))
    return (outputs[0].astype(jnp.bfloat16), outputs[1].astype(jnp.bfloat16), input_grad, grads[0], grads[1], grads[2], grads[3], grads[4], grads[5], grads[6], grads[7], grads[8])
```

```python
from functools import partial
import math

import jax
import jax.numpy as jnp
import numpy as np
from jax import lax
from jax.experimental import pallas as pl
from jax.experimental.pallas import tpu as pltpu
from jax.sharding import Mesh, PartitionSpec as P

HEAD = 64
SCALE = 0.125
EPSILON = 1e-06
NEGATIVE = -1e30
ACROSS = (((0,), (0,)), ((), ()))
WITHIN = (((1,), (1,)), ((), ()))
BF = jnp.bfloat16
F32 = jnp.float32


def layer_norm(tensor, gain_row, shift_row):
    average = jnp.mean(tensor, axis=-1, keepdims=True)
    centred = tensor - average
    variance = jnp.mean(centred * centred, axis=-1, keepdims=True)
    return centred * lax.rsqrt(variance + EPSILON) * gain_row + shift_row


def product(left_side, right_side):
    return jnp.dot(left_side, right_side, preferred_element_type=F32)


def outer_sum(left_side, right_side):
    return lax.dot_general(left_side, right_side, ACROSS, preferred_element_type=F32)


def back_product(left_side, right_side):
    return lax.dot_general(left_side, right_side, WITHIN, preferred_element_type=F32)


def by_heads(tensor):
    return tensor.reshape(tensor.shape[0], tensor.shape[1] // HEAD, HEAD)


def permitted(query_seg, query_pos, key_seg, key_open, key_pos):
    matching = query_seg[:, None] == key_seg[None, :]
    return matching & ((key_open[None, :] == 1) | (query_pos[:, None] == key_pos[None, :]))


def scores(query_heads, key_heads):
    return (
        jnp.einsum("bhd,khd->hbk", query_heads, key_heads, preferred_element_type=F32) * SCALE
    )


def sweep(length, visitor, initial):
    stride = math.gcd(length, 512)
    return lax.fori_loop(
        0,
        length // stride,
        lambda position, running: visitor(position * stride, stride, running),
        initial,
    )


class Grid:
    def __init__(self, sizes):
        self.size = dict(sizes)
        self.at = {name: lax.axis_index(name) for name in sizes}
        self.places = jnp.stack([self.at[name] for name in sizes]).astype(jnp.int32)
        self.shards = math.prod(sizes.values())
        index = 0
        for name in sizes:
            index = index * sizes[name] + self.at[name]
        self.shard = index

    def shift(self, tensor, axis, step):
        n = self.size[axis]
        return lax.ppermute(tensor, axis, [(i, (i + step) % n) for i in range(n)])

    def far_steps(self):
        return [(a, b) for a in range(self.size["h"]) for b in range(self.size["z"])]

    def far_shift(self, tensor, step):
        high, deep = self.size["h"], self.size["z"]
        pairs = [
            (a * deep + b, ((a + step[0]) % high) * deep + (b + step[1]) % deep)
            for a in range(high)
            for b in range(deep)
        ]
        return lax.ppermute(tensor, ("h", "z"), pairs)

    def swap(self, tensor):
        return lax.ppermute(tensor, ("x", "c"), [(0, 0), (1, 2), (2, 1), (3, 3)])

    def rows(self, tensor):
        if self.size["h"] > 1:
            tensor = lax.all_gather(tensor, "h", axis=0, tiled=False)
        else:
            tensor = tensor[None]
        other = self.shift(tensor, "c", 1)
        first = self.at["c"] == 0
        both = jnp.stack([jnp.where(first, tensor, other), jnp.where(first, other, tensor)], axis=1)
        return both.reshape((-1,) + tensor.shape[2:])


def place(places, pieces, out_shapes, moves):
    def kernel(at_ref, *refs):
        ins, outs, sems = refs[: len(pieces)], refs[len(pieces) : -1], refs[-1]
        copies = [
            pltpu.make_async_copy(source, target, sems.at[i])
            for i, (source, target) in enumerate(moves(at_ref, ins, outs))
        ]
        for copy in copies:
            copy.start()
        for copy in copies:
            copy.wait()

    count = 2 * len(pieces)
    moved = sum(math.prod(s.shape) * 2 for s in out_shapes)
    return pl.pallas_call(
        kernel,
        out_shape=out_shapes,
        in_specs=[pl.BlockSpec(memory_space=pltpu.SMEM)]
        + [pl.BlockSpec(memory_space=pl.ANY)] * len(pieces),
        out_specs=[pl.BlockSpec(memory_space=pl.ANY)] * len(out_shapes),
        scratch_shapes=[pltpu.SemaphoreType.DMA((count,))],
        cost_estimate=pl.CostEstimate(flops=0, transcendentals=0, bytes_accessed=2 * moved),
        name="place",
    )(places, *pieces)


def gather_weights(grid, shard, widths):
    high, wide, deep, tall = (grid.size[name] for name in "hxzy")
    rows, columns = shard.shape
    half = rows // 2
    steps = grid.far_steps()
    pieces = [shard if step == (0, 0) else grid.far_shift(shard, step) for step in steps]

    def far_moves(at, ins, outs):
        listed = []
        for step, ref in zip(steps, ins):
            a = lax.rem(at[0] - step[0] + high, high)
            b = lax.rem(at[2] - step[1] + deep, deep)
            for colour in range(2):
                listed.append((ref.at[pl.ds(colour * half, half)], outs[colour].at[a, b]))
        return listed

    lines = place(
        grid.places,
        pieces,
        [jax.ShapeDtypeStruct((high, deep, half, columns), shard.dtype)] * 2,
        far_moves,
    )
    tagged = []
    first_a = [grid.shift(lines[0], "x", k) for k in range(1, wide)]
    first_b = [grid.shift(lines[1], "y", k) for k in range(1, tall)]
    tagged.append((lines[0], 0, 0, 0))
    tagged.append((lines[1], 0, 0, 1))
    tagged += [(t, k + 1, 0, 0) for k, t in enumerate(first_a)]
    tagged += [(t, 0, k + 1, 1) for k, t in enumerate(first_b)]
    held_a = [(lines[0], 0)] + [(t, k + 1) for k, t in enumerate(first_a)]
    held_b = [(lines[1], 0)] + [(t, k + 1) for k, t in enumerate(first_b)]
    for (ta, ka), (tb, kb) in zip(held_a, held_b):
        tagged += [(grid.shift(ta, "y", k), ka, k, 0) for k in range(1, tall)]
        tagged += [(grid.shift(tb, "x", k), k, kb, 1) for k in range(1, wide)]
    if len(held_b) > len(held_a):
        for tb, kb in held_b[len(held_a) :]:
            tagged += [(grid.shift(tb, "x", k), k, kb, 1) for k in range(1, wide)]
    pairs = [t + (0,) for t in tagged] + [(grid.shift(t[0], "c", 1),) + t[1:] + (1,) for t in tagged]
    offsets = [sum(widths[:i]) for i in range(len(widths))]

    def last_moves(at, ins, outs):
        listed = []
        for ref, (_, kx, ky, colour, kc) in zip(ins, pairs):
            px = lax.rem(at[1] - kx + wide, wide)
            py = lax.rem(at[3] - ky + tall, tall)
            pc = lax.rem(at[4] - kc + 2, 2)
            for out, offset, width in zip(outs, offsets, widths):
                listed.append(
                    (
                        ref.at[:, :, :, pl.ds(offset, width)],
                        out.at[:, px, :, py, pc, pl.ds(colour * half, half)],
                    )
                )
        return listed

    full = place(
        grid.places,
        [t[0] for t in pairs],
        [
            jax.ShapeDtypeStruct((high, wide, deep, tall, 2, rows, width), shard.dtype)
            for width in widths
        ],
        last_moves,
    )
    return [t.reshape(-1, width) for t, width in zip(full, widths)]


def pick(tensor, index, axis):
    return lax.dynamic_index_in_dim(tensor, index, axis, keepdims=False)


def total(parts):
    result = parts[0].astype(F32)
    for part in parts[1:]:
        result = result + part.astype(F32)
    return result


def scatter_sum(grid, term):
    high, wide, deep, tall = (grid.size[name] for name in "hxzy")
    rows, columns = term.shape[0] // grid.shards, term.shape[1]
    half = rows // 2
    view = term.reshape(high, wide, deep, tall, 2, rows, columns)
    pair_at = grid.at["c"]
    sent = grid.shift(pick(view, 1 - pair_at, 4), "c", 1)
    kept = pick(view, pair_at, 4)
    parts = []
    for colour, order in enumerate(("xy", "yx")):
        held = [t[..., colour * half : (colour + 1) * half, :] for t in (kept, sent)]
        axes = ["h", "x", "z", "y"]
        for name in order:
            n, own, axis = grid.size[name], grid.at[name], axes.index(name)
            arrived = [
                grid.shift(
                    total([pick(t, lax.rem(own + k, n), axis) for t in held]).astype(BF), name, k
                )
                for k in range(1, n)
            ]
            held = [pick(t, own, axis) for t in held] + arrived
            axes.remove(name)
        parts.append(held)

    def at_far(step):
        a = lax.rem(grid.at["h"] + step[0], high)
        b = lax.rem(grid.at["z"] + step[1], deep)
        return jnp.concatenate(
            [total([pick(pick(t, a, 0), b, 0) for t in held]) for held in parts], axis=0
        )

    arrived = [
        grid.far_shift(at_far(step).astype(BF), step) for step in grid.far_steps() if step != (0, 0)
    ]
    return total([at_far((0, 0))] + arrived)


def everywhere(grid, tensor):
    for name in "cxy":
        tensor = total([tensor] + [grid.shift(tensor, name, k) for k in range(1, grid.size[name])]).astype(
            tensor.dtype
        )
    return total(
        [tensor] + [grid.far_shift(tensor, s) for s in grid.far_steps() if s != (0, 0)]
    ).astype(tensor.dtype)


def body(
    sizes,
    inputs,
    segment_ids,
    key_mask,
    lead_index,
    cotangent_first,
    cotangent_second,
    w_qkv,
    w_out,
    w_up,
    w_down,
    biases,
    up_bias,
    norm_gains,
    norm_shifts,
    lead_table,
):
    grid = Grid(sizes)
    tokens, model = inputs.shape[1], inputs.shape[2]
    heads = model // HEAD
    shards = grid.shards
    share = model // shards

    small = jnp.concatenate(
        [t.reshape(-1) for t in (biases, up_bias, norm_gains, norm_shifts, lead_table)]
    )
    mine = jnp.arange(shards, dtype=jnp.int32)[:, None] == grid.shard
    small = everywhere(grid, jnp.where(mine, small[None, :], jnp.zeros((), BF)))
    lengths = [t.shape[0] for t in (biases, norm_gains, norm_shifts, lead_table)]

    def unpack(start, count):
        block = small[:, start : start + count * share].reshape(shards, count, share)
        return block.transpose(1, 0, 2).reshape(count, model).astype(F32)

    own_up = up_bias.shape[0]
    bias_full = unpack(0, lengths[0])
    bias_up = small[:, lengths[0] * share : lengths[0] * share + own_up].reshape(-1).astype(F32)
    begin = lengths[0] * share + own_up
    gains = unpack(begin, lengths[1])
    shifts = unpack(begin + lengths[1] * share, lengths[2])
    lead_rows = unpack(begin + (lengths[1] + lengths[2]) * share, lengths[3])

    labels = grid.swap(
        jnp.concatenate([segment_ids, key_mask, jnp.broadcast_to(lead_index.reshape(2, 1), (2, tokens))])
    )
    own_seg, own_open = labels[0], labels[1]
    leads = (labels[2, 0], labels[3, 0])
    start_low = grid.swap(inputs[0])
    seed_first = grid.swap(cotangent_first[0])
    seed_second = grid.swap(cotangent_second[0])
    every = grid.rows(labels[:2].T)
    all_seg, all_open = every[:, 0], every[:, 1]
    own_pos = (grid.at["h"] * 2 + grid.at["c"]) * tokens + jnp.arange(tokens, dtype=jnp.int32)

    (weight_qkv,) = gather_weights(grid, w_qkv, [w_qkv.shape[1]])
    weight_up, weight_out = gather_weights(
        grid, jnp.concatenate([w_up, w_out], axis=1), [w_up.shape[1], w_out.shape[1]]
    )
    (weight_down,) = gather_weights(grid, w_down, [w_down.shape[1]])

    def key_labels(row_start, stride):
        key_seg = lax.dynamic_slice_in_dim(all_seg, row_start, stride, 0)
        key_open = lax.dynamic_slice_in_dim(all_open, row_start, stride, 0)
        key_pos = row_start + jnp.arange(stride, dtype=jnp.int32)
        return permitted(own_seg, own_pos, key_seg, key_open, key_pos)

    def forward(start_in, lead_id):
        chooser = (jnp.arange(lead_rows.shape[0], dtype=jnp.int32) == lead_id).astype(F32)
        lead_vec = jnp.sum(chooser[:, None] * lead_rows, axis=0)
        hidden = start_in + lead_vec[None, :]
        normed = layer_norm(hidden, gains[0], shifts[0]).astype(BF)
        mixed = product(normed, weight_qkv)
        query = (mixed[:, :model] + bias_full[0]).astype(BF)
        keys = mixed[:, model : 2 * model].astype(BF)
        values = (mixed[:, 2 * model :] + bias_full[1]).astype(BF)
        query_heads = by_heads(query)
        start_stats = (
            jnp.full((heads, tokens), NEGATIVE, F32),
            jnp.zeros((heads, tokens), F32),
        )
        both_part = grid.rows(jnp.concatenate([keys, values], axis=1))
        key_part, value_part = both_part[:, :model], both_part[:, model:]

        def visitor(offset, stride, inner):
            highest, denominator = inner
            key_block = by_heads(lax.dynamic_slice_in_dim(key_part, offset, stride, 0))
            allowed = key_labels(offset, stride)
            masked = jnp.where(allowed[None], scores(query_heads, key_block), NEGATIVE)
            new_high = jnp.maximum(highest, jnp.max(masked, axis=-1))
            weights = jnp.where(allowed[None], jnp.exp(masked - new_high[..., None]), 0.0)
            return (new_high, denominator * jnp.exp(highest - new_high) + jnp.sum(weights, axis=-1))

        highest, denominator = sweep(key_part.shape[0], visitor, start_stats)
        log_total = highest + jnp.log(denominator)
        start_out = jnp.zeros((tokens, heads, HEAD), F32)

        def visitor(offset, stride, inner):
            key_block = by_heads(lax.dynamic_slice_in_dim(key_part, offset, stride, 0))
            value_block = by_heads(lax.dynamic_slice_in_dim(value_part, offset, stride, 0))
            allowed = key_labels(offset, stride)
            masked = jnp.where(allowed[None], scores(query_heads, key_block), NEGATIVE)
            probs = jnp.exp(masked - log_total[..., None]).astype(BF)
            return inner + jnp.einsum(
                "hbk,khd->bhd", probs, value_block, preferred_element_type=F32
            )

        attn = sweep(key_part.shape[0], visitor, start_out).reshape(tokens, model)
        attn_low = attn.astype(BF)
        middle = hidden + product(attn_low, weight_out) + bias_full[2]
        normed_mid = layer_norm(middle, gains[1], shifts[1]).astype(BF)
        gate_in = product(normed_mid, weight_up) + bias_up
        activated = jax.nn.gelu(gate_in, approximate=False).astype(BF)
        result = middle + product(activated, weight_down) + bias_full[3]
        saved = (
            hidden,
            normed,
            query,
            keys,
            values,
            key_part,
            value_part,
            log_total,
            attn,
            attn_low,
            middle,
            normed_mid,
            gate_in,
            activated,
            chooser,
        )
        return (result, saved)

    def backward(saved, grad_res, earlier, close):
        (
            hidden,
            normed,
            query,
            keys,
            values,
            key_part,
            value_part,
            log_total,
            attn,
            attn_low,
            middle,
            normed_mid,
            gate_in,
            activated,
            chooser,
        ) = saved

        def join(name, left_side, right_side):
            term = outer_sum(left_side, right_side)
            if earlier is not None:
                term = earlier[name].astype(F32) + term
            return close(term.astype(BF))

        terms = {}
        grad_low = grad_res.astype(BF)
        terms["down"] = join("down", activated, grad_low)
        bias_down = jnp.sum(grad_low.astype(F32), axis=0)
        gate_pull = jax.vjp(partial(jax.nn.gelu, approximate=False), gate_in)[1]
        grad_gate = gate_pull(back_product(grad_low, weight_down))[0].astype(BF)
        terms["up"] = join("up", normed_mid, grad_gate)
        bias_gate = jnp.sum(grad_gate.astype(F32), axis=0)
        mid_pull = jax.vjp(layer_norm, middle, gains[1], shifts[1])[1]
        grad_mid_part, gain_mid, shift_mid = mid_pull(back_product(grad_gate, weight_up))
        grad_mid = grad_res + grad_mid_part
        grad_branch = grad_mid.astype(BF)
        terms["out"] = join("out", attn_low, grad_branch)
        bias_attn = jnp.sum(grad_branch.astype(F32), axis=0)
        grad_attn = back_product(grad_branch, weight_out).astype(BF)
        grad_attn_heads = by_heads(grad_attn)
        delta = jnp.sum(by_heads(grad_attn.astype(F32)) * by_heads(attn), axis=-1).T
        query_heads = by_heads(query)
        keys_heads = by_heads(keys)
        values_heads = by_heads(values)
        start_query = jnp.zeros((tokens, heads, HEAD), F32)

        def visitor(offset, stride, inner):
            key_block = by_heads(lax.dynamic_slice_in_dim(key_part, offset, stride, 0))
            value_block = by_heads(lax.dynamic_slice_in_dim(value_part, offset, stride, 0))
            allowed = key_labels(offset, stride)
            masked = jnp.where(allowed[None], scores(query_heads, key_block), NEGATIVE)
            probs = jnp.exp(masked - log_total[..., None])
            grad_probs = jnp.einsum(
                "bhd,khd->hbk", grad_attn_heads, value_block, preferred_element_type=F32
            )
            grad_logits = (probs * (grad_probs - delta[..., None])).astype(BF)
            return inner + jnp.einsum(
                "hbk,khd->bhd", grad_logits, key_block, preferred_element_type=F32
            )

        grad_query = sweep(key_part.shape[0], visitor, start_query)
        stats = grid.rows(jnp.concatenate([log_total, delta]).T).T
        all_lse, all_delta = stats[:heads], stats[heads:]
        start_keys = (
            jnp.zeros((tokens, heads, HEAD), F32),
            jnp.zeros((tokens, heads, HEAD), F32),
        )
        both_part = grid.rows(jnp.concatenate([query, grad_attn], axis=1))
        query_part, grad_part = both_part[:, :model], both_part[:, model:]

        def visitor(offset, stride, inner):
            grad_keys, grad_values = inner
            query_block = by_heads(lax.dynamic_slice_in_dim(query_part, offset, stride, 0))
            grad_block = by_heads(lax.dynamic_slice_in_dim(grad_part, offset, stride, 0))
            query_seg = lax.dynamic_slice_in_dim(all_seg, offset, stride, 0)
            query_pos = offset + jnp.arange(stride, dtype=jnp.int32)
            allowed = permitted(query_seg, query_pos, own_seg, own_open, own_pos)
            lse_block = lax.dynamic_slice_in_dim(all_lse, offset, stride, 1)
            delta_block = lax.dynamic_slice_in_dim(all_delta, offset, stride, 1)
            masked = jnp.where(allowed[None], scores(query_block, keys_heads), NEGATIVE)
            probs = jnp.exp(masked - lse_block[..., None])
            grad_probs = jnp.einsum(
                "bhd,khd->hbk", grad_block, values_heads, preferred_element_type=F32
            )
            grad_logits = (probs * (grad_probs - delta_block[..., None])).astype(BF)
            grad_values = grad_values + jnp.einsum(
                "hbk,bhd->khd", probs.astype(BF), grad_block, preferred_element_type=F32
            )
            grad_keys = grad_keys + jnp.einsum(
                "hbk,bhd->khd", grad_logits, query_block, preferred_element_type=F32
            )
            return (grad_keys, grad_values)

        grad_keys, grad_values = sweep(query_part.shape[0], visitor, start_keys)
        query_low = (grad_query * SCALE).reshape(tokens, model).astype(BF)
        keys_low = (grad_keys * SCALE).reshape(tokens, model).astype(BF)
        values_low = grad_values.reshape(tokens, model).astype(BF)
        grad_mixed = jnp.concatenate([query_low, keys_low, values_low], axis=1)
        terms["qkv"] = join("qkv", normed, grad_mixed)
        bias_query = jnp.sum(query_low.astype(F32), axis=0)
        bias_value = jnp.sum(values_low.astype(F32), axis=0)
        in_pull = jax.vjp(layer_norm, hidden, gains[0], shifts[0])[1]
        grad_in_part, gain_in, shift_in = in_pull(back_product(grad_mixed, weight_qkv))
        grad_start = grad_mid + grad_in_part
        lead_sum = jnp.sum(grad_start, axis=0)
        term_lead = chooser[:, None] * lead_sum[None, :]
        vectors = (
            jnp.stack([bias_query, bias_value, bias_attn, bias_down]),
            bias_gate,
            jnp.stack([gain_in, gain_mid]),
            jnp.stack([shift_in, shift_mid]),
            term_lead,
        )
        return (grad_start, terms, vectors)

    result_first, saved_first = forward(start_low.astype(F32), leads[0])
    first_low = result_first.astype(BF)
    result_second, saved_second = forward(first_low.astype(F32), leads[1])
    second_low = result_second.astype(BF)
    grad_between, terms_second, vectors_second = backward(
        saved_second, seed_second.astype(F32), None, lambda t: t
    )
    grad_first, shares, vectors_first = backward(
        saved_first, seed_first.astype(F32) + grad_between, terms_second, partial(scatter_sum, grid)
    )
    vectors = [a + b for a, b in zip(vectors_second, vectors_first)]

    def pack(block):
        return block.reshape(-1, shards, share).transpose(1, 0, 2).reshape(shards, -1)

    packed = jnp.concatenate(
        [
            pack(vectors[0]),
            vectors[1].reshape(shards, -1),
            pack(vectors[2]),
            pack(vectors[3]),
            pack(vectors[4]),
        ],
        axis=1,
    )
    own_row = pick(everywhere(grid, packed), grid.shard, 0)
    cuts = np.cumsum([lengths[0] * share, own_up, lengths[1] * share, lengths[2] * share])
    small_out = jnp.split(own_row, [int(cut) for cut in cuts])
    return (
        grid.swap(first_low)[None],
        grid.swap(second_low)[None],
        grid.swap(grad_first.astype(BF)).astype(F32)[None],
        shares["qkv"],
        shares["out"],
        shares["up"],
        shares["down"],
        small_out[0].reshape(lengths[0], share),
        small_out[1],
        small_out[2].reshape(lengths[1], share),
        small_out[3].reshape(lengths[2], share),
        small_out[4].reshape(lengths[3], share),
    )


def solution(mesh):
    dp, fsdp = mesh.shape["dp"], mesh.shape["fsdp"]
    tall = fsdp // 8
    sizes = {"h": dp // 2, "x": 2, "z": 4, "y": tall, "c": 2}
    fine = Mesh(np.asarray(mesh.devices).reshape(tuple(sizes.values())), tuple(sizes))
    one, two, every = ("z", "y", "c"), ("h", "x"), ("h", "x", "z", "y", "c")
    placed = (
        P(one, two, None),
        P(one, two),
        P(one, two),
        P(one, None),
        P(one, two, None),
        P(one, two, None),
        P(every, None),
        P(every, None),
        P(every, None),
        P(every, None),
        P(None, every),
        P(every),
        P(None, every),
        P(None, every),
        P(None, every),
    )
    return jax.shard_map(
        partial(body, sizes),
        mesh=fine,
        in_specs=placed,
        out_specs=(
            P(one, two, None),
            P(one, two, None),
            P(one, two, None),
            P(every, None),
            P(every, None),
            P(every, None),
            P(every, None),
            P(None, every),
            P(every),
            P(None, every),
            P(None, every),
            P(None, every),
        ),
        check_vma=False,
    )
```

```python
from functools import partial
import math

import jax
import jax.numpy as jnp
import numpy as np
from jax import lax
from jax.experimental import pallas as pl
from jax.experimental.pallas import tpu as pltpu
from jax.sharding import Mesh, PartitionSpec as P

HEAD = 64
PAIR = 2 * HEAD
SCALE = 0.125
EPSILON = 1e-06
NEGATIVE = -1e30
ACROSS = (((0,), (0,)), ((), ()))
WITHIN = (((1,), (1,)), ((), ()))
BF = jnp.bfloat16
F32 = jnp.float32


def layer_norm(tensor, gain_row, shift_row):
    average = jnp.mean(tensor, axis=-1, keepdims=True)
    centred = tensor - average
    variance = jnp.mean(centred * centred, axis=-1, keepdims=True)
    return centred * lax.rsqrt(variance + EPSILON) * gain_row + shift_row


def product(left_side, right_side):
    return jnp.dot(left_side, right_side, preferred_element_type=F32)


def outer_sum(left_side, right_side):
    return lax.dot_general(left_side, right_side, ACROSS, preferred_element_type=F32)


def back_product(left_side, right_side):
    return lax.dot_general(left_side, right_side, WITHIN, preferred_element_type=F32)


def fill_bias(bias_ref, query_seg, query_pos, key_seg, key_open, key_pos):
    allowed = (key_seg == query_seg) & ((key_open == 1) | (key_pos == query_pos))
    bias_ref[...] = jnp.where(allowed, 0.0, NEGATIVE)


def half_lanes(tensor, side):
    lane = lax.broadcasted_iota(jnp.int32, tensor.shape, 1)
    return jnp.where((lane < HEAD) == (side == 0), tensor, jnp.zeros((), tensor.dtype))


def attention_forward(query, keys, values, query_labels, key_labels):
    tokens, model = query.shape
    every = keys.shape[0]
    pairs = model // PAIR
    step = math.gcd(tokens, 256)

    def kernel(q_ref, k_ref, v_ref, ql_ref, kl_ref, attn_ref, lse_ref, bias_ref):
        @pl.when(pl.program_id(0) == 0)
        def _():
            fill_bias(
                bias_ref, ql_ref[:, 0:1], ql_ref[:, 1:2], kl_ref[0:1], kl_ref[1:2], kl_ref[2:3]
            )

        keys_pair, values_pair = k_ref[...], v_ref[...]
        for start in range(0, tokens, step):
            query_pair = q_ref[start : start + step, :]
            sides = []
            for side in range(2):
                logits = back_product(half_lanes(query_pair, side), keys_pair)
                logits = logits + bias_ref[start : start + step, :]
                highest = jnp.max(logits, axis=1, keepdims=True)
                weights = jnp.exp(logits - highest)
                denominator = jnp.sum(weights, axis=1, keepdims=True)
                across = jnp.broadcast_to(highest + jnp.log(denominator), (step, PAIR)).T
                lse_ref[0, side : side + 1, start : start + step] = across[0:1]
                sides.append(product(weights.astype(BF), values_pair) / denominator)
            lane = lax.broadcasted_iota(jnp.int32, (step, PAIR), 1)
            attn_ref[start : start + step, :] = jnp.where(lane < HEAD, sides[0], sides[1])

    work = 2 * tokens * every * model
    return pl.pallas_call(
        kernel,
        grid=(pairs,),
        in_specs=[
            pl.BlockSpec((tokens, PAIR), lambda i: (0, i)),
            pl.BlockSpec((every, PAIR), lambda i: (0, i)),
            pl.BlockSpec((every, PAIR), lambda i: (0, i)),
            pl.BlockSpec(query_labels.shape, lambda i: (0, 0)),
            pl.BlockSpec(key_labels.shape, lambda i: (0, 0)),
        ],
        out_specs=[
            pl.BlockSpec((tokens, PAIR), lambda i: (0, i)),
            pl.BlockSpec((1, 2, tokens), lambda i: (i, 0, 0)),
        ],
        out_shape=[
            jax.ShapeDtypeStruct((tokens, model), F32),
            jax.ShapeDtypeStruct((pairs, 2, tokens), F32),
        ],
        scratch_shapes=[pltpu.VMEM((tokens, every), F32)],
        compiler_params=pltpu.CompilerParams(
            dimension_semantics=("arbitrary",), vmem_limit_bytes=48 << 20
        ),
        cost_estimate=pl.CostEstimate(
            flops=2 * work, transcendentals=work // PAIR, bytes_accessed=10 * every * model
        ),
        name="attention_forward",
    )(query, keys, values, query_labels, key_labels)


def attention_backward(query, keys, values, grad, attn, lse, query_labels, key_labels, first, pairs):
    tokens = query.shape[0]
    every = keys.shape[0]
    model = pairs * PAIR
    step = math.gcd(every, 256)

    def kernel(q_ref, k_ref, v_ref, g_ref, a_ref, lse_ref, ql_ref, kl_ref, dq_ref, dk_ref, dv_ref, bias_ref):
        @pl.when(pl.program_id(0) == 0)
        def _():
            fill_bias(
                bias_ref, ql_ref[0:1], ql_ref[1:2], kl_ref[:, 0:1], kl_ref[:, 1:2], kl_ref[:, 2:3]
            )

        query_pair, grad_pair = q_ref[...], g_ref[...]
        overlap = (grad_pair.astype(F32) * a_ref[...].astype(F32)).T
        deltas = [
            jnp.sum(overlap[side * HEAD : (side + 1) * HEAD], axis=0, keepdims=True)
            for side in range(2)
        ]
        keys_across = k_ref[...].astype(F32).T.astype(BF)
        query_sides = [half_lanes(query_pair, side) for side in range(2)]
        grad_sides = [half_lanes(grad_pair, side) for side in range(2)]
        grad_query = [jnp.zeros((HEAD, tokens), F32), jnp.zeros((HEAD, tokens), F32)]
        for start in range(0, every, step):
            keys_pair, values_pair = k_ref[start : start + step, :], v_ref[start : start + step, :]
            grad_keys, grad_values = [], []
            for side in range(2):
                logits = back_product(keys_pair, query_sides[side])
                logits = logits + bias_ref[start : start + step, :]
                probs = jnp.exp(logits - lse_ref[0, side : side + 1, :])
                grad_probs = back_product(values_pair, grad_sides[side])
                grad_logits = (probs * (grad_probs - deltas[side])).astype(BF)
                grad_values.append(product(probs.astype(BF), grad_sides[side]))
                grad_keys.append(product(grad_logits, query_sides[side]))
                grad_query[side] = grad_query[side] + product(
                    keys_across[side * HEAD : (side + 1) * HEAD, start : start + step], grad_logits
                )
            dk_ref[start : start + step, :] = (grad_keys[0] + grad_keys[1]).astype(BF)
            dv_ref[start : start + step, :] = (grad_values[0] + grad_values[1]).astype(BF)
        dq_ref[...] = (jnp.concatenate(grad_query, axis=0).T * SCALE).astype(BF)

    work = 2 * tokens * every * model
    own, own_out = (
        pl.BlockSpec((tokens, PAIR), lambda i: (0, i + first)),
        pl.BlockSpec((tokens, PAIR), lambda i: (0, i)),
    )
    whole, whole_out = (
        pl.BlockSpec((every, PAIR), lambda i: (0, i + first)),
        pl.BlockSpec((every, PAIR), lambda i: (0, i)),
    )
    return pl.pallas_call(
        kernel,
        grid=(pairs,),
        in_specs=[
            own,
            whole,
            whole,
            own,
            own,
            pl.BlockSpec((1, 2, tokens), lambda i: (i + first, 0, 0)),
            pl.BlockSpec(query_labels.shape, lambda i: (0, 0)),
            pl.BlockSpec(key_labels.shape, lambda i: (0, 0)),
        ],
        out_specs=[own_out, whole_out, whole_out],
        out_shape=[
            jax.ShapeDtypeStruct((tokens, model), BF),
            jax.ShapeDtypeStruct((every, model), BF),
            jax.ShapeDtypeStruct((every, model), BF),
        ],
        scratch_shapes=[pltpu.VMEM((every, tokens), F32)],
        compiler_params=pltpu.CompilerParams(
            dimension_semantics=("arbitrary",), vmem_limit_bytes=48 << 20
        ),
        cost_estimate=pl.CostEstimate(
            flops=5 * work, transcendentals=work // PAIR, bytes_accessed=12 * every * model
        ),
        name="attention_backward",
    )(query, keys, values, grad, attn, lse, query_labels, key_labels)


class Grid:
    def __init__(self, sizes):
        self.size = dict(sizes)
        self.at = {name: lax.axis_index(name) for name in sizes}
        self.places = jnp.stack([self.at[name] for name in sizes]).astype(jnp.int32)
        self.shards = math.prod(sizes.values())
        index = 0
        for name in sizes:
            index = index * sizes[name] + self.at[name]
        self.shard = index

    def shift(self, tensor, axis, step):
        n = self.size[axis]
        return lax.ppermute(tensor, axis, [(i, (i + step) % n) for i in range(n)])

    def far_steps(self):
        return [(a, b) for a in range(self.size["h"]) for b in range(self.size["z"])]

    def far_shift(self, tensor, step):
        high, deep = self.size["h"], self.size["z"]
        pairs = [
            (a * deep + b, ((a + step[0]) % high) * deep + (b + step[1]) % deep)
            for a in range(high)
            for b in range(deep)
        ]
        return lax.ppermute(tensor, ("h", "z"), pairs)

    def swap(self, tensor):
        return lax.ppermute(tensor, ("x", "c"), [(0, 0), (1, 2), (2, 1), (3, 3)])

    def rows(self, tensor):
        if self.size["h"] > 1:
            tensor = lax.all_gather(tensor, "h", axis=0, tiled=False)
        else:
            tensor = tensor[None]
        other = self.shift(tensor, "c", 1)
        first = self.at["c"] == 0
        both = jnp.stack([jnp.where(first, tensor, other), jnp.where(first, other, tensor)], axis=1)
        return both.reshape((-1,) + tensor.shape[2:])


def place(places, pieces, out_shapes, moves):
    count = len(pieces)
    landed = [pltpu.VMEM(piece.shape, piece.dtype) for piece in pieces]

    def kernel(at_ref, *refs):
        ins, outs = refs[:count], refs[count : count + len(out_shapes)]
        held, load_sems, store_sems = refs[-2 - count : -2], refs[-2], refs[-1]
        loads = [
            pltpu.make_async_copy(source, target, load_sems.at[i])
            for i, (source, target) in enumerate(zip(ins, held))
        ]
        for load in loads:
            load.start()
        stores = []
        ready = -1
        for piece, source, target in moves(at_ref, held, outs):
            while ready < piece:
                ready += 1
                loads[ready].wait()
            store = pltpu.make_async_copy(source, target, store_sems.at[len(stores)])
            store.start()
            stores.append(store)
        for store in stores:
            store.wait()

    moved = sum(math.prod(s.shape) * 2 for s in out_shapes)
    return pl.pallas_call(
        kernel,
        out_shape=out_shapes,
        in_specs=[pl.BlockSpec(memory_space=pltpu.SMEM)]
        + [pl.BlockSpec(memory_space=pl.ANY)] * count,
        out_specs=[pl.BlockSpec(memory_space=pl.ANY)] * len(out_shapes),
        scratch_shapes=landed
        + [pltpu.SemaphoreType.DMA((count,)), pltpu.SemaphoreType.DMA((2 * count,))],
        compiler_params=pltpu.CompilerParams(vmem_limit_bytes=moved + (4 << 20)),
        cost_estimate=pl.CostEstimate(flops=0, transcendentals=0, bytes_accessed=2 * moved),
        name="place",
    )(places, *pieces)


def gather_weights(grid, shard, widths):
    high, wide, deep, tall = (grid.size[name] for name in "hxzy")
    rows, columns = shard.shape
    half = rows // 2
    steps = grid.far_steps()
    pieces = [shard if step == (0, 0) else grid.far_shift(shard, step) for step in steps]

    def far_moves(at, ins, outs):
        listed = []
        for i, (step, ref) in enumerate(zip(steps, ins)):
            a = lax.rem(at[0] - step[0] + high, high)
            b = lax.rem(at[2] - step[1] + deep, deep)
            for colour in range(2):
                listed.append((i, ref.at[pl.ds(colour * half, half)], outs[colour].at[a, b]))
        return listed

    lines = place(
        grid.places,
        pieces,
        [jax.ShapeDtypeStruct((high, deep, half, columns), shard.dtype)] * 2,
        far_moves,
    )
    tagged = []
    first_a = [grid.shift(lines[0], "x", k) for k in range(1, wide)]
    first_b = [grid.shift(lines[1], "y", k) for k in range(1, tall)]
    tagged.append((lines[0], 0, 0, 0))
    tagged.append((lines[1], 0, 0, 1))
    tagged += [(t, k + 1, 0, 0) for k, t in enumerate(first_a)]
    tagged += [(t, 0, k + 1, 1) for k, t in enumerate(first_b)]
    held_a = [(lines[0], 0)] + [(t, k + 1) for k, t in enumerate(first_a)]
    held_b = [(lines[1], 0)] + [(t, k + 1) for k, t in enumerate(first_b)]
    for (ta, ka), (tb, kb) in zip(held_a, held_b):
        tagged += [(grid.shift(ta, "y", k), ka, k, 0) for k in range(1, tall)]
        tagged += [(grid.shift(tb, "x", k), k, kb, 1) for k in range(1, wide)]
    if len(held_b) > len(held_a):
        for tb, kb in held_b[len(held_a) :]:
            tagged += [(grid.shift(tb, "x", k), k, kb, 1) for k in range(1, wide)]
    pairs = [t + (0,) for t in tagged] + [(grid.shift(t[0], "c", 1),) + t[1:] + (1,) for t in tagged]
    offsets = [sum(widths[:i]) for i in range(len(widths))]

    def last_moves(at, ins, outs):
        listed = []
        for i, (ref, (_, kx, ky, colour, kc)) in enumerate(zip(ins, pairs)):
            px = lax.rem(at[1] - kx + wide, wide)
            py = lax.rem(at[3] - ky + tall, tall)
            pc = lax.rem(at[4] - kc + 2, 2)
            for out, offset, width in zip(outs, offsets, widths):
                listed.append(
                    (
                        i,
                        ref.at[:, :, :, pl.ds(offset, width)],
                        out.at[:, px, :, py, pc, pl.ds(colour * half, half)],
                    )
                )
        return listed

    full = place(
        grid.places,
        [t[0] for t in pairs],
        [
            jax.ShapeDtypeStruct((high, wide, deep, tall, 2, rows, width), shard.dtype)
            for width in widths
        ],
        last_moves,
    )
    return [t.reshape(-1, width) for t, width in zip(full, widths)]


def pick(tensor, index, axis):
    return lax.dynamic_index_in_dim(tensor, index, axis, keepdims=False)


def total(parts):
    result = parts[0].astype(F32)
    for part in parts[1:]:
        result = result + part.astype(F32)
    return result


class Scatter:
    def __init__(self, grid, term):
        self.grid = grid
        sizes = [grid.size[name] for name in "hxzy"]
        rows, columns = term.shape[0] // grid.shards, term.shape[1]
        half = rows // 2
        self.cuts = (slice(0, half), slice(half, rows))
        view = term.reshape(*sizes, 2, rows, columns)
        self.held = [[pick(view, grid.at["c"], 4)[..., cut, :]] for cut in self.cuts]
        self.sends = [pick(view, 1 - grid.at["c"], 4)]
        self.axes = [list("hxzy"), list("hxzy")]
        self.stage = 0

    def go(self):
        if self.stage == 0:
            self.arrived = [self.grid.shift(self.sends[0], "c", 1)]
        elif self.stage < 3:
            self.arrived = [self.grid.shift(t, *route) for t, route in zip(self.sends, self.routes)]
        else:
            self.arrived = [self.grid.far_shift(t, route) for t, route in zip(self.sends, self.routes)]

    def prepare(self):
        grid = self.grid
        for i, cut in enumerate(self.cuts):
            if self.stage == 0:
                self.held[i].append(self.arrived[0][..., cut, :])
            else:
                self.held[i] += [t for t, owner in zip(self.arrived, self.owners) if owner == i]
        self.stage += 1
        if self.stage == 3:
            self.routes = [step for step in grid.far_steps() if step != (0, 0)]
            self.sends = [self.at_far(step).astype(BF) for step in self.routes]
            return
        self.sends, self.routes, self.owners = [], [], []
        for i, order in enumerate(("xy", "yx")):
            name = order[self.stage - 1]
            n, own, axis = grid.size[name], grid.at[name], self.axes[i].index(name)
            for k in range(1, n):
                parts = [pick(t, lax.rem(own + k, n), axis) for t in self.held[i]]
                self.sends.append(total(parts).astype(BF))
                self.routes.append((name, k))
                self.owners.append(i)
            self.held[i] = [pick(t, own, axis) for t in self.held[i]]
            self.axes[i].remove(name)

    def at_far(self, step):
        a = lax.rem(self.grid.at["h"] + step[0], self.grid.size["h"])
        b = lax.rem(self.grid.at["z"] + step[1], self.grid.size["z"])
        return jnp.concatenate(
            [total([pick(pick(t, a, 0), b, 0) for t in held]) for held in self.held], axis=0
        )

    def result(self):
        return total([self.at_far((0, 0))] + self.arrived)


def order(values, sent=(), got=()):
    values, sends, arrived = lax.optimization_barrier(
        (values, [s.sends for s in sent], [s.arrived for s in got])
    )
    for scatter, arrays in zip(sent, sends):
        scatter.sends = arrays
    for scatter, arrays in zip(got, arrived):
        scatter.arrived = arrays
    return values


def everywhere(grid, tensor):
    for name in "cxy":
        tensor = total([tensor] + [grid.shift(tensor, name, k) for k in range(1, grid.size[name])]).astype(
            tensor.dtype
        )
    return total(
        [tensor] + [grid.far_shift(tensor, s) for s in grid.far_steps() if s != (0, 0)]
    ).astype(tensor.dtype)


def body(
    sizes,
    inputs,
    segment_ids,
    key_mask,
    lead_index,
    cotangent_first,
    cotangent_second,
    w_qkv,
    w_out,
    w_up,
    w_down,
    biases,
    up_bias,
    norm_gains,
    norm_shifts,
    lead_table,
):
    grid = Grid(sizes)
    tokens, model = inputs.shape[1], inputs.shape[2]
    shards = grid.shards
    share = model // shards

    small = jnp.concatenate(
        [t.reshape(-1) for t in (biases, up_bias, norm_gains, norm_shifts, lead_table)]
    )
    mine = jnp.arange(shards, dtype=jnp.int32)[:, None] == grid.shard
    small = everywhere(grid, jnp.where(mine, small[None, :], jnp.zeros((), BF)))
    lengths = [t.shape[0] for t in (biases, norm_gains, norm_shifts, lead_table)]

    def unpack(start, count):
        block = small[:, start : start + count * share].reshape(shards, count, share)
        return block.transpose(1, 0, 2).reshape(count, model).astype(F32)

    own_up = up_bias.shape[0]
    bias_full = unpack(0, lengths[0])
    bias_up = small[:, lengths[0] * share : lengths[0] * share + own_up].reshape(-1).astype(F32)
    begin = lengths[0] * share + own_up
    gains = unpack(begin, lengths[1])
    shifts = unpack(begin + lengths[1] * share, lengths[2])
    lead_rows = unpack(begin + (lengths[1] + lengths[2]) * share, lengths[3])

    labels = grid.swap(
        jnp.concatenate([segment_ids, key_mask, jnp.broadcast_to(lead_index.reshape(2, 1), (2, tokens))])
    )
    own_seg, own_open = labels[0], labels[1]
    leads = (labels[2, 0], labels[3, 0])
    start_low = grid.swap(inputs[0])
    seed_first = grid.swap(cotangent_first[0])
    seed_second = grid.swap(cotangent_second[0])
    every = grid.rows(labels[:2].T)
    all_seg, all_open = every[:, 0], every[:, 1]
    own_pos = (grid.at["h"] * 2 + grid.at["c"]) * tokens + jnp.arange(tokens, dtype=jnp.int32)

    (weight_qkv,) = gather_weights(grid, w_qkv, [w_qkv.shape[1]])
    weight_up, weight_out = gather_weights(
        grid, jnp.concatenate([w_up, w_out], axis=1), [w_up.shape[1], w_out.shape[1]]
    )
    (weight_down,) = gather_weights(grid, w_down, [w_down.shape[1]])

    query_labels = jnp.stack([own_seg, own_pos])
    query_labels_across = query_labels.T
    all_pos = jnp.arange(all_seg.shape[0], dtype=jnp.int32)
    key_labels = jnp.stack([all_seg, all_open, all_pos])
    key_labels_across = key_labels.T
    high = grid.size["h"]

    def forward(start_in, lead_id):
        chooser = (jnp.arange(lead_rows.shape[0], dtype=jnp.int32) == lead_id).astype(F32)
        lead_vec = jnp.sum(chooser[:, None] * lead_rows, axis=0)
        hidden = start_in + lead_vec[None, :]
        normed = layer_norm(hidden, gains[0], shifts[0]).astype(BF)
        mixed = product(normed, weight_qkv)
        query = (mixed[:, :model] + bias_full[0]).astype(BF) * jnp.asarray(SCALE, BF)
        keys = mixed[:, model : 2 * model].astype(BF)
        values = (mixed[:, 2 * model :] + bias_full[1]).astype(BF)
        every_key, every_value = grid.rows(keys), grid.rows(values)
        attn, lse = attention_forward(query, every_key, every_value, query_labels_across, key_labels)
        attn_low = attn.astype(BF)
        middle = hidden + product(attn_low, weight_out) + bias_full[2]
        normed_mid = layer_norm(middle, gains[1], shifts[1]).astype(BF)
        gate_in = product(normed_mid, weight_up) + bias_up
        activated = jax.nn.gelu(gate_in, approximate=False).astype(BF)
        result = middle + product(activated, weight_down) + bias_full[3]
        saved = (
            hidden, normed, query, every_key, every_value, lse, attn, attn_low, middle,
            normed_mid, gate_in, activated, chooser,
        )
        return (result, saved)

    def backward(saved, grad_res, earlier):
        (
            hidden, normed, query, every_key, every_value, lse, attn, attn_low, middle,
            normed_mid, gate_in, activated, chooser,
        ) = saved
        last = earlier is not None
        kinds = ("down", "up", "out", "qkv0", "qkv1")
        sums = {}

        def join(name, left_side, right_side):
            term = outer_sum(left_side, right_side)
            if last:
                term = earlier[name].astype(F32) + term
            sums[name] = Scatter(grid, term.astype(BF)) if last else term.astype(BF)

        def then(values, sent=(), got=()):
            if not last:
                return values
            values = order(values, [sums[name] for name in sent], [sums[name] for name in got])
            for name in sent:
                sums[name].go()
            return values

        def prepare(*names):
            if last:
                for name in names:
                    sums[name].prepare()

        grad_low = grad_res.astype(BF)
        join("down", activated, grad_low)
        grad_low = then(grad_low, sent=["down"])
        bias_down = jnp.sum(grad_low.astype(F32), axis=0)
        gate_pull = jax.vjp(partial(jax.nn.gelu, approximate=False), gate_in)[1]
        grad_gate = gate_pull(back_product(grad_low, weight_down))[0].astype(BF)
        grad_gate = then(grad_gate, got=["down"])
        prepare("down")
        grad_gate = then(grad_gate, sent=["down"])
        join("up", normed_mid, grad_gate)
        grad_gate = then(grad_gate, sent=["up"])
        bias_gate = jnp.sum(grad_gate.astype(F32), axis=0)
        mid_pull = jax.vjp(layer_norm, middle, gains[1], shifts[1])[1]
        grad_mid_part, gain_mid, shift_mid = mid_pull(back_product(grad_gate, weight_up))
        grad_mid = grad_res + grad_mid_part
        grad_mid = then(grad_mid, got=["up", "down"])
        prepare("down", "up")
        grad_mid = then(grad_mid, sent=["down", "up"])
        grad_branch = grad_mid.astype(BF)
        grad_attn = back_product(grad_branch, weight_out).astype(BF)
        bias_attn = jnp.sum(grad_branch.astype(F32), axis=0)
        pairs = model // PAIR
        cuts = (0, pairs // 2, pairs)
        mixed_parts, back_parts = [], []
        for half in range(2):
            first, count = cuts[half], cuts[half + 1] - cuts[half]
            query_low, partial_keys, partial_values = attention_backward(
                query, every_key, every_value, grad_attn, attn, lse, query_labels, key_labels_across,
                first, count,
            )
            width = count * PAIR
            partial_both = jnp.stack([partial_keys, partial_values]).reshape(2, high, 2, tokens, width)
            sent = pick(partial_both, 1 - grid.at["c"], 2)
            if half == 0:
                sent = then(sent, got=["down", "up"])
                prepare("down", "up")
                sent = then(sent, sent=["down", "up"])
                join("out", attn_low, grad_branch)
                sent, grad_attn = then((sent, grad_attn), sent=["out"])
            else:
                sent = then(sent, got=["qkv0", "down", "up", "out"])
                prepare("qkv0", "up", "out")
                sent = then(sent, sent=["qkv0", "up", "out"])
            both = total([pick(partial_both, grid.at["c"], 2), grid.shift(sent, "c", 1)])
            if high > 1:
                both = lax.psum_scatter(both.astype(BF), "h", scatter_dimension=1, tiled=False)
            else:
                both = both[:, 0]
            both = both.astype(BF)
            query_low = (query_low.astype(F32)).astype(BF)
            mixed = jnp.concatenate([query_low, both[0], both[1]], axis=1)
            join(f"qkv{half}", normed, mixed)
            if half == 0:
                grad_attn, mixed = then((grad_attn, mixed), sent=["qkv0"])
            else:
                mixed = then(mixed, sent=["qkv1"])
            mixed_parts.append(mixed)
        if last:
            mixed_parts[1] = then(mixed_parts[1], got=["qkv1", "qkv0", "out"])
            prepare("qkv1", "qkv0", "out")
            mixed_parts[1] = then(mixed_parts[1], sent=["qkv1", "qkv0", "out"])
        grad_mixed = jnp.concatenate(
            [p[:, i * p.shape[1] // 3 : (i + 1) * p.shape[1] // 3] for i in range(3) for p in mixed_parts],
            axis=1,
        )
        bias_query = jnp.sum(grad_mixed[:, :model].astype(F32), axis=0)
        bias_value = jnp.sum(grad_mixed[:, 2 * model :].astype(F32), axis=0)
        in_pull = jax.vjp(layer_norm, hidden, gains[0], shifts[0])[1]
        grad_in_part, gain_in, shift_in = in_pull(back_product(grad_mixed, weight_qkv))
        grad_start = grad_mid + grad_in_part
        lead_sum = jnp.sum(grad_start, axis=0)
        term_lead = chooser[:, None] * lead_sum[None, :]
        vectors = (
            jnp.stack([bias_query, bias_value, bias_attn, bias_down]),
            bias_gate,
            jnp.stack([gain_in, gain_mid]),
            jnp.stack([shift_in, shift_mid]),
            term_lead,
        )
        return (grad_start, sums, vectors)

    result_first, saved_first = forward(start_low.astype(F32), leads[0])
    first_low = result_first.astype(BF)
    result_second, saved_second = forward(first_low.astype(F32), leads[1])
    second_low = result_second.astype(BF)
    grad_between, terms_second, vectors_second = backward(saved_second, seed_second.astype(F32), None)
    grad_first, sums, vectors_first = backward(
        saved_first, seed_first.astype(F32) + grad_between, terms_second
    )
    shares = {}
    for name, scatter in sums.items():
        while scatter.stage < 3:
            scatter.prepare()
            scatter.go()
        shares[name] = scatter.result()
    width = shares["qkv0"].shape[1] // 3
    shares["qkv"] = jnp.concatenate(
        [shares[f"qkv{half}"][:, i * width : (i + 1) * width] for i in range(3) for half in range(2)],
        axis=1,
    )
    vectors = [a + b for a, b in zip(vectors_second, vectors_first)]

    def pack(block):
        return block.reshape(-1, shards, share).transpose(1, 0, 2).reshape(shards, -1)

    packed = jnp.concatenate(
        [
            pack(vectors[0]),
            vectors[1].reshape(shards, -1),
            pack(vectors[2]),
            pack(vectors[3]),
            pack(vectors[4]),
        ],
        axis=1,
    )
    own_row = pick(everywhere(grid, packed), grid.shard, 0)
    cuts = np.cumsum([lengths[0] * share, own_up, lengths[1] * share, lengths[2] * share])
    small_out = jnp.split(own_row, [int(cut) for cut in cuts])
    return (
        grid.swap(first_low)[None],
        grid.swap(second_low)[None],
        grid.swap(grad_first.astype(BF)).astype(F32)[None],
        shares["qkv"],
        shares["out"],
        shares["up"],
        shares["down"],
        small_out[0].reshape(lengths[0], share),
        small_out[1],
        small_out[2].reshape(lengths[1], share),
        small_out[3].reshape(lengths[2], share),
        small_out[4].reshape(lengths[3], share),
    )


def solution(mesh):
    dp, fsdp = mesh.shape["dp"], mesh.shape["fsdp"]
    tall = fsdp // 8
    sizes = {"h": dp // 2, "x": 2, "z": 4, "y": tall, "c": 2}
    fine = Mesh(np.asarray(mesh.devices).reshape(tuple(sizes.values())), tuple(sizes))
    one, two, every = ("z", "y", "c"), ("h", "x"), ("h", "x", "z", "y", "c")
    placed = (
        P(one, two, None),
        P(one, two),
        P(one, two),
        P(one, None),
        P(one, two, None),
        P(one, two, None),
        P(every, None),
        P(every, None),
        P(every, None),
        P(every, None),
        P(None, every),
        P(every),
        P(None, every),
        P(None, every),
        P(None, every),
    )
    return jax.shard_map(
        partial(body, sizes),
        mesh=fine,
        in_specs=placed,
        out_specs=(
            P(one, two, None),
            P(one, two, None),
            P(one, two, None),
            P(every, None),
            P(every, None),
            P(every, None),
            P(every, None),
            P(None, every),
            P(every),
            P(None, every),
            P(None, every),
            P(None, every),
        ),
        check_vma=False,
    )
```

```python
from functools import partial
import math

import jax
import jax.numpy as jnp
import numpy as np
from jax import lax
from jax.experimental import pallas as pl
from jax.experimental.pallas import tpu as pltpu
from jax.sharding import Mesh, PartitionSpec as P

HEAD = 64
PAIR = 2 * HEAD
SCALE = 0.125
EPSILON = 1e-06
NEGATIVE = -1e30
ACROSS = (((0,), (0,)), ((), ()))
WITHIN = (((1,), (1,)), ((), ()))
BF = jnp.bfloat16
F32 = jnp.float32


def layer_norm(tensor, gain_row, shift_row):
    average = jnp.mean(tensor, axis=-1, keepdims=True)
    centred = tensor - average
    variance = jnp.mean(centred * centred, axis=-1, keepdims=True)
    return centred * lax.rsqrt(variance + EPSILON) * gain_row + shift_row


def product(left_side, right_side):
    return jnp.dot(left_side, right_side, preferred_element_type=F32)


def outer_sum(left_side, right_side):
    return lax.dot_general(left_side, right_side, ACROSS, preferred_element_type=F32)


def back_product(left_side, right_side):
    return lax.dot_general(left_side, right_side, WITHIN, preferred_element_type=F32)


def fill_bias(bias_ref, query_labels, key_labels):
    query_seg, _, query_pos = query_labels
    key_seg, key_open, key_pos = key_labels
    allowed = (key_seg == query_seg) & ((key_open == 1) | (key_pos == query_pos))
    bias_ref[...] = jnp.where(allowed, 0.0, NEGATIVE)


def columns_of(ref):
    return tuple(ref[:, i : i + 1] for i in range(3))


def rows_of(ref):
    return tuple(ref[i : i + 1, :] for i in range(3))


def half_lanes(tensor, side):
    lane = lax.broadcasted_iota(jnp.int32, tensor.shape, 1)
    return jnp.where((lane < HEAD) == (side == 0), tensor, jnp.zeros((), tensor.dtype))


def attention_forward(query, mates, query_labels, key_labels):
    tokens, model = query.shape
    part = mates[0].shape[0]
    every = 2 * part
    pairs = model // PAIR
    step = math.gcd(tokens, 256)

    def kernel(q_ref, k0_ref, k1_ref, v0_ref, v1_ref, ql_ref, kl_ref, attn_ref, lse_ref, bias_ref):
        @pl.when(pl.program_id(0) == 0)
        def _():
            fill_bias(bias_ref, columns_of(ql_ref), rows_of(kl_ref))

        keys_pair = jnp.concatenate([k0_ref[...], k1_ref[...]], axis=0)
        values_pair = jnp.concatenate([v0_ref[...], v1_ref[...]], axis=0)
        for start in range(0, tokens, step):
            query_pair = q_ref[start : start + step, :]
            sides = []
            for side in range(2):
                logits = back_product(half_lanes(query_pair, side), keys_pair)
                logits = logits + bias_ref[start : start + step, :]
                highest = jnp.max(logits, axis=1, keepdims=True)
                weights = jnp.exp(logits - highest)
                denominator = jnp.sum(weights, axis=1, keepdims=True)
                across = jnp.broadcast_to(highest + jnp.log(denominator), (step, PAIR)).T
                lse_ref[0, side : side + 1, start : start + step] = across[0:1]
                sides.append(product(weights.astype(BF), values_pair) / denominator)
            lane = lax.broadcasted_iota(jnp.int32, (step, PAIR), 1)
            attn_ref[start : start + step, :] = jnp.where(lane < HEAD, sides[0], sides[1]).astype(BF)

    work = 2 * tokens * every * model
    keys_at = pl.BlockSpec((part, PAIR), lambda i: (0, i))
    values_at = pl.BlockSpec((part, PAIR), lambda i: (0, i + pairs))
    return pl.pallas_call(
        kernel,
        grid=(pairs,),
        in_specs=[
            pl.BlockSpec((tokens, PAIR), lambda i: (0, i)),
            keys_at,
            keys_at,
            values_at,
            values_at,
            pl.BlockSpec(query_labels.shape, lambda i: (0, 0)),
            pl.BlockSpec(key_labels.shape, lambda i: (0, 0)),
        ],
        out_specs=[
            pl.BlockSpec((tokens, PAIR), lambda i: (0, i)),
            pl.BlockSpec((1, 2, tokens), lambda i: (i, 0, 0)),
        ],
        out_shape=[
            jax.ShapeDtypeStruct((tokens, model), BF),
            jax.ShapeDtypeStruct((pairs, 2, tokens), F32),
        ],
        scratch_shapes=[pltpu.VMEM((tokens, every), F32)],
        compiler_params=pltpu.CompilerParams(
            dimension_semantics=("arbitrary",), vmem_limit_bytes=40 << 20
        ),
        cost_estimate=pl.CostEstimate(
            flops=2 * work, transcendentals=work // PAIR, bytes_accessed=10 * every * model
        ),
        name="attention_forward",
    )(query, *mates, *mates, query_labels, key_labels)


def attention_backward(query, mates, grad, attn, lse, query_labels, key_labels, first, pairs):
    tokens = query.shape[0]
    part = mates[0].shape[0]
    every, total_pairs = 2 * part, query.shape[1] // PAIR
    model = pairs * PAIR
    step = math.gcd(part, 256)

    def kernel(q_ref, k0_ref, k1_ref, v0_ref, v1_ref, g_ref, a_ref, lse_ref, ql_ref, kl_ref,
               dq_ref, d0_ref, d1_ref, bias_ref):
        @pl.when(pl.program_id(0) == 0)
        def _():
            fill_bias(bias_ref, rows_of(ql_ref), columns_of(kl_ref))

        query_pair, grad_pair = q_ref[...], g_ref[...]
        overlap = (grad_pair.astype(F32) * a_ref[...].astype(F32)).T
        deltas = [
            jnp.sum(overlap[side * HEAD : (side + 1) * HEAD], axis=0, keepdims=True)
            for side in range(2)
        ]
        query_sides = [half_lanes(query_pair, side) for side in range(2)]
        grad_sides = [half_lanes(grad_pair, side) for side in range(2)]
        grad_query = [jnp.zeros((HEAD, tokens), F32), jnp.zeros((HEAD, tokens), F32)]
        for mate, (k_ref, v_ref, d_ref) in enumerate(((k0_ref, v0_ref, d0_ref), (k1_ref, v1_ref, d1_ref))):
            keys_across = k_ref[...].astype(F32).T.astype(BF)
            for start in range(0, part, step):
                rows = slice(start, start + step)
                grad_keys, grad_values = [], []
                for side in range(2):
                    logits = back_product(k_ref[rows, :], query_sides[side])
                    logits = logits + bias_ref[mate * part + start : mate * part + start + step, :]
                    probs = jnp.exp(logits - lse_ref[0, side : side + 1, :])
                    grad_probs = back_product(v_ref[rows, :], grad_sides[side])
                    grad_logits = (probs * (grad_probs - deltas[side])).astype(BF)
                    grad_values.append(product(probs.astype(BF), grad_sides[side]))
                    grad_keys.append(product(grad_logits, query_sides[side]))
                    grad_query[side] = grad_query[side] + product(
                        keys_across[side * HEAD : (side + 1) * HEAD, rows], grad_logits
                    )
                d_ref[0, rows, :] = (grad_keys[0] + grad_keys[1]).astype(BF)
                d_ref[1, rows, :] = (grad_values[0] + grad_values[1]).astype(BF)
        dq_ref[...] = (jnp.concatenate(grad_query, axis=0).T * SCALE).astype(BF)

    work = 2 * tokens * every * model
    own = pl.BlockSpec((tokens, PAIR), lambda i: (0, i + first))
    keys_at = pl.BlockSpec((part, PAIR), lambda i: (0, i + first))
    values_at = pl.BlockSpec((part, PAIR), lambda i: (0, i + first + total_pairs))
    mate_out = pl.BlockSpec((2, part, PAIR), lambda i: (0, 0, i))
    return pl.pallas_call(
        kernel,
        grid=(pairs,),
        in_specs=[
            own,
            keys_at,
            keys_at,
            values_at,
            values_at,
            own,
            own,
            pl.BlockSpec((1, 2, tokens), lambda i: (i + first, 0, 0)),
            pl.BlockSpec(query_labels.shape, lambda i: (0, 0)),
            pl.BlockSpec(key_labels.shape, lambda i: (0, 0)),
        ],
        out_specs=[pl.BlockSpec((tokens, PAIR), lambda i: (0, i)), mate_out, mate_out],
        out_shape=[
            jax.ShapeDtypeStruct((tokens, model), BF),
            jax.ShapeDtypeStruct((2, part, model), BF),
            jax.ShapeDtypeStruct((2, part, model), BF),
        ],
        scratch_shapes=[pltpu.VMEM((every, tokens), F32)],
        compiler_params=pltpu.CompilerParams(
            dimension_semantics=("arbitrary",), vmem_limit_bytes=40 << 20
        ),
        cost_estimate=pl.CostEstimate(
            flops=5 * work, transcendentals=work // PAIR, bytes_accessed=12 * every * model
        ),
        name="attention_backward",
    )(query, *mates, *mates, grad, attn, lse, query_labels, key_labels)


def gated(normed, weight, bias_rows):
    tokens, model = normed.shape
    hidden_units = weight.shape[1]
    width = math.gcd(bias_rows.shape[1], 512)
    per_row = bias_rows.shape[1] // width
    rows = math.gcd(tokens, 128)
    bias = bias_rows.reshape(-1, 1, width)

    def kernel(x_ref, w_ref, b_ref, act_ref, slope_ref):
        for start in range(0, tokens, rows):
            gate = jnp.dot(
                x_ref[start : start + rows, :], w_ref[...], preferred_element_type=F32
            ) + b_ref[0]
            share = 0.5 + 0.5 * lax.erf(gate * math.sqrt(0.5))
            density = jnp.exp(gate * gate * -0.5) * (1.0 / math.sqrt(2.0 * math.pi))
            act_ref[start : start + rows, :] = (gate * share).astype(BF)
            slope_ref[start : start + rows, :] = (share + gate * density).astype(BF)

    block = pl.BlockSpec((tokens, width), lambda i: (0, i))
    return pl.pallas_call(
        kernel,
        grid=(hidden_units // width,),
        in_specs=[
            pl.BlockSpec((tokens, model), lambda i: (0, 0)),
            pl.BlockSpec((model, width), lambda i: (0, i)),
            pl.BlockSpec((1, 1, width), lambda i: (i, 0, 0)),
        ],
        out_specs=[block, block],
        out_shape=[jax.ShapeDtypeStruct((tokens, hidden_units), BF)] * 2,
        compiler_params=pltpu.CompilerParams(
            dimension_semantics=("arbitrary",), vmem_limit_bytes=40 << 20
        ),
        cost_estimate=pl.CostEstimate(
            flops=2 * tokens * model * hidden_units,
            transcendentals=2 * tokens * hidden_units,
            bytes_accessed=2 * (model + 2 * tokens) * hidden_units,
        ),
        name="gated",
    )(normed, weight, bias)


def gated_backward(grad_low, slope, weight_down, weight_up):
    tokens, model = grad_low.shape
    hidden_units = slope.shape[1]
    width = math.gcd(hidden_units, 512)
    steps = hidden_units // width
    rows = math.gcd(tokens, 256)

    def kernel(g_ref, s_ref, down_ref, up_ref, gate_ref, bias_ref, out_ref, acc_ref):
        @pl.when(pl.program_id(0) == 0)
        def _():
            acc_ref[...] = jnp.zeros_like(acc_ref)

        column = jnp.zeros((1, width), F32)
        for start in range(0, tokens, rows):
            cut = slice(start, start + rows)
            pulled = back_product(g_ref[cut, :], down_ref[...]) * s_ref[cut, :].astype(F32)
            low = pulled.astype(BF)
            gate_ref[cut, :] = low
            column = column + jnp.sum(low.astype(F32), axis=0, keepdims=True)
            acc_ref[cut, :] += back_product(low, up_ref[...])
        bias_ref[0] = column

        @pl.when(pl.program_id(0) == steps - 1)
        def _():
            out_ref[...] = acc_ref[...]

    return pl.pallas_call(
        kernel,
        grid=(steps,),
        in_specs=[
            pl.BlockSpec((tokens, model), lambda i: (0, 0)),
            pl.BlockSpec((tokens, width), lambda i: (0, i)),
            pl.BlockSpec((width, model), lambda i: (i, 0)),
            pl.BlockSpec((model, width), lambda i: (0, i)),
        ],
        out_specs=[
            pl.BlockSpec((tokens, width), lambda i: (0, i)),
            pl.BlockSpec((1, 1, width), lambda i: (i, 0, 0)),
            pl.BlockSpec((tokens, model), lambda i: (0, 0)),
        ],
        out_shape=[
            jax.ShapeDtypeStruct((tokens, hidden_units), BF),
            jax.ShapeDtypeStruct((steps, 1, width), F32),
            jax.ShapeDtypeStruct((tokens, model), F32),
        ],
        scratch_shapes=[pltpu.VMEM((tokens, model), F32)],
        compiler_params=pltpu.CompilerParams(
            dimension_semantics=("arbitrary",), vmem_limit_bytes=40 << 20
        ),
        cost_estimate=pl.CostEstimate(
            flops=4 * tokens * model * hidden_units,
            transcendentals=0,
            bytes_accessed=4 * (model + tokens) * hidden_units,
        ),
        name="gated_backward",
    )(grad_low, slope, weight_down, weight_up)


def weight_terms(grid, jobs):
    tokens, height = jobs[0][0][0].shape
    shards = grid.shards
    rows = height // shards
    widths = [rights[0].shape[1] for _, rights in jobs]
    columns = sum(widths)
    if rows % 16:
        acc = jnp.concatenate(
            [sum(outer_sum(left, right) for left, right in zip(*job)) for job in jobs], axis=1
        )
        acc = acc.astype(BF).reshape(shards // 2, 2, rows, columns)
        return tuple(pick(acc, lax.rem(grid.at["c"] + k, 2), 1) for k in range(2))
    lefts = [left for job in jobs for left in job[0]]
    rights = [right for job in jobs for right in job[1]]
    count, depth = len(lefts), len(jobs[0][0])
    block = 256
    pairs = block // (2 * rows)

    def kernel(at_ref, *refs):
        left_refs, right_refs = refs[:count], refs[count : 2 * count]
        kept_ref, sent_ref = refs[2 * count :]
        upper = at_ref[4] == 1
        begin = 0
        for job, width in enumerate(widths):
            chunk = math.gcd(width, 1024) if width % 1024 == 0 else math.gcd(width, 512)
            turn = slice(job * depth, (job + 1) * depth)
            for start in range(0, width, chunk):
                acc = None
                for left, right in zip(left_refs[turn], right_refs[turn]):
                    part = outer_sum(left[...], right[:, start : start + chunk])
                    acc = part if acc is None else acc + part
                acc = acc.reshape(pairs, 2, rows, chunk)
                at = slice(begin + start, begin + start + chunk)
                kept_ref[:, :, at] = jnp.where(upper, acc[:, 1], acc[:, 0]).astype(BF)
                sent_ref[:, :, at] = jnp.where(upper, acc[:, 0], acc[:, 1]).astype(BF)
            begin += width

    out = pl.BlockSpec((pairs, rows, columns), lambda i: (i, 0, 0))
    return pl.pallas_call(
        kernel,
        grid=(height // block,),
        in_specs=[pl.BlockSpec(memory_space=pltpu.SMEM)]
        + [pl.BlockSpec((tokens, block), lambda i: (0, i))] * count
        + [
            pl.BlockSpec((tokens, right.shape[1]), lambda i: (0, 0), pipeline_mode=pl.Buffered(1))
            for right in rights
        ],
        out_specs=[out, out],
        out_shape=[jax.ShapeDtypeStruct((shards // 2, rows, columns), BF)] * 2,
        compiler_params=pltpu.CompilerParams(
            dimension_semantics=("arbitrary",), vmem_limit_bytes=48 << 20
        ),
        cost_estimate=pl.CostEstimate(
            flops=2 * depth * tokens * height * columns,
            transcendentals=0,
            bytes_accessed=2 * height * columns + 2 * depth * tokens * (height + columns),
        ),
        name="weight_terms",
    )(grid.places, *lefts, *rights)


class Grid:
    def __init__(self, sizes):
        self.size = dict(sizes)
        self.at = {name: lax.axis_index(name) for name in sizes}
        self.places = jnp.stack([self.at[name] for name in sizes]).astype(jnp.int32)
        self.shards = math.prod(sizes.values())
        index = 0
        for name in sizes:
            index = index * sizes[name] + self.at[name]
        self.shard = index

    def shift(self, tensor, axis, step):
        n = self.size[axis]
        return lax.ppermute(tensor, axis, [(i, (i + step) % n) for i in range(n)])

    def far_steps(self):
        return [(a, b) for a in range(self.size["h"]) for b in range(self.size["z"])]

    def far_shift(self, tensor, step):
        high, deep = self.size["h"], self.size["z"]
        pairs = [
            (a * deep + b, ((a + step[0]) % high) * deep + (b + step[1]) % deep)
            for a in range(high)
            for b in range(deep)
        ]
        return lax.ppermute(tensor, ("h", "z"), pairs)

    def swapped(self, tensor):
        return lax.ppermute(tensor, ("x", "c"), [(1, 2), (2, 1)])

    def choose(self, tensor, moved):
        return jnp.where(self.at["x"] == self.at["c"], tensor, moved)

    def mates(self, tensor):
        if self.size["h"] > 1:
            tensor = lax.all_gather(tensor, "h", axis=0, tiled=True)
        return tensor, self.shift(tensor, "c", 1)


def place(places, pieces, out_shapes, moves):
    count = len(pieces)
    landed = [pltpu.VMEM(piece.shape, piece.dtype) for piece in pieces]

    def kernel(at_ref, *refs):
        ins, outs = refs[:count], refs[count : count + len(out_shapes)]
        held, load_sems, store_sems = refs[-2 - count : -2], refs[-2], refs[-1]
        loads = [
            pltpu.make_async_copy(source, target, load_sems.at[i])
            for i, (source, target) in enumerate(zip(ins, held))
        ]
        for load in loads:
            load.start()
        stores = []
        ready = -1
        for piece, source, target in moves(at_ref, held, outs):
            while ready < piece:
                ready += 1
                loads[ready].wait()
            store = pltpu.make_async_copy(source, target, store_sems.at[len(stores)])
            store.start()
            stores.append(store)
        for store in stores:
            store.wait()

    moved = sum(math.prod(s.shape) * 2 for s in out_shapes)
    return pl.pallas_call(
        kernel,
        out_shape=out_shapes,
        in_specs=[pl.BlockSpec(memory_space=pltpu.SMEM)]
        + [pl.BlockSpec(memory_space=pl.ANY)] * count,
        out_specs=[pl.BlockSpec(memory_space=pl.ANY)] * len(out_shapes),
        scratch_shapes=landed
        + [pltpu.SemaphoreType.DMA((count,)), pltpu.SemaphoreType.DMA((8 * count,))],
        compiler_params=pltpu.CompilerParams(vmem_limit_bytes=moved + (4 << 20)),
        cost_estimate=pl.CostEstimate(flops=0, transcendentals=0, bytes_accessed=2 * moved),
        name="place",
    )(places, *pieces)


class Gather:
    def __init__(self, grid, chunks, widths):
        self.grid, self.widths = grid, widths
        self.chunks = list(chunks)
        self.half = chunks[0].shape[0] // 2
        self.columns = sum(chunk.shape[1] for chunk in chunks)
        self.kind = chunks[0].dtype
        self.far = [None] * len(chunks)

    def new(self, *lead):
        return jax.ShapeDtypeStruct((*lead, self.half, self.columns), self.kind)

    def go_far(self, i):
        self.far[i] = [self.grid.far_shift(self.chunks[i], step) for step in self.grid.far_steps()[1:]]

    def make_lines(self):
        high, deep = self.grid.size["h"], self.grid.size["z"]
        steps, half = self.grid.far_steps(), self.half

        widths = [chunk.shape[1] for chunk in self.chunks]
        pieces = [
            (tensor, step, sum(widths[:i]), widths[i])
            for i, chunk in enumerate(self.chunks)
            for tensor, step in zip([chunk] + self.far[i], steps)
        ]

        def moves(at, ins, outs):
            listed = []
            for i, (ref, (_, step, offset, width)) in enumerate(zip(ins, pieces)):
                a = lax.rem(at[0] - step[0] + high, high)
                b = lax.rem(at[2] - step[1] + deep, deep)
                for colour in range(2):
                    listed.append(
                        (
                            i,
                            ref.at[pl.ds(colour * half, half)],
                            outs[colour].at[a, b, :, pl.ds(offset, width)],
                        )
                    )
            return listed

        self.sends = place(
            self.grid.places, [p[0] for p in pieces], [self.new(high, deep)] * 2, moves
        )

    def go_first(self):
        self.own = self.sends
        self.arrived = [
            self.grid.shift(t, name, k)
            for t, name in zip(self.sends, "xy")
            for k in range(1, self.grid.size[name])
        ]

    def make_planes(self):
        high, wide, deep, tall = (self.grid.size[name] for name in "hxzy")
        spots = [(0, 0), (1, 0)] + [(0, k) for k in range(1, wide)] + [(1, k) for k in range(1, tall)]

        def moves(at, ins, outs):
            return [(i, ref, outs[c].at[k]) for i, (ref, (c, k)) in enumerate(zip(ins, spots))]

        self.sends = place(
            self.grid.places,
            list(self.own) + self.arrived,
            [self.new(wide, high, deep), self.new(tall, high, deep)],
            moves,
        )

    def go_second(self):
        self.near = [(self.sends[0], 0, 0), (self.sends[1], 1, 0)]
        self.arrived = [
            self.grid.shift(t, name, k)
            for t, name in zip(self.sends, "yx")
            for k in range(1, self.grid.size[name])
        ]

    def go_pair_near(self):
        self.pairs = [(self.grid.shift(t, "c", 1), colour, k) for t, colour, k in self.near]

    def go_pair_far(self):
        counts = [(c, k) for c, name in enumerate("yx") for k in range(1, self.grid.size[name])]
        distant = [(t, c, k) for t, (c, k) in zip(self.arrived, counts)]
        self.near += distant
        self.pairs += [(self.grid.shift(t, "c", 1), colour, k) for t, colour, k in distant]

    def result(self):
        high, wide, deep, tall = (self.grid.size[name] for name in "hxzy")
        half, widths = self.half, self.widths
        pieces = [t + (0,) for t in self.near] + [t + (1,) for t in self.pairs]
        offsets = [sum(widths[:i]) for i in range(len(widths))]

        def moves(at, ins, outs):
            listed = []
            for i, (ref, (_, colour, far, kc)) in enumerate(zip(ins, pieces)):
                pc = lax.rem(at[4] + kc, 2)
                for k in range(wide if colour == 0 else tall):
                    kx, ky = (k, far) if colour == 0 else (far, k)
                    px = lax.rem(at[1] - kx + wide, wide)
                    py = lax.rem(at[3] - ky + tall, tall)
                    for out, offset, width in zip(outs, offsets, widths):
                        listed.append(
                            (
                                i,
                                ref.at[k, :, :, :, pl.ds(offset, width)],
                                out.at[:, px, :, py, pc, pl.ds(colour * half, half)],
                            )
                        )
            return listed

        full = place(
            self.grid.places,
            [t[0] for t in pieces],
            [
                jax.ShapeDtypeStruct((high, wide, deep, tall, 2, 2 * half, width), self.kind)
                for width in widths
            ],
            moves,
        )
        return [t.reshape(-1, width) for t, width in zip(full, widths)]


def pick(tensor, index, axis):
    return lax.dynamic_index_in_dim(tensor, index, axis, keepdims=False)


def total(parts):
    result = parts[0].astype(F32)
    for part in parts[1:]:
        result = result + part.astype(F32)
    return result


def tie(*groups):
    return lax.optimization_barrier(groups)


class Scatter:
    def __init__(self, grid, kept, sent):
        self.grid = grid
        sizes = [grid.size[name] for name in "hxzy"]
        self.rows, self.columns = kept.shape[1:]
        self.half = self.rows // 2
        kept = kept.reshape(*sizes, self.rows, self.columns)
        self.held = [[(kept, "hxzy", i * self.half)] for i in range(2)]
        self.picked = [{}, {}]
        self.sends = [sent.reshape(*sizes, self.rows, self.columns)]
        self.stage = 0

    def go(self):
        if self.stage == 0:
            self.arrived = [self.grid.shift(self.sends[0], "c", 1)]
        elif self.stage < 3:
            self.arrived = [self.grid.shift(t, *route) for t, route in zip(self.sends, self.routes)]
        else:
            self.arrived = [self.grid.far_shift(t, route) for t, route in zip(self.sends, self.routes)]

    def slices(self, i, extra):
        places = {**self.picked[i], **extra}
        parts = []
        for tensor, axes, row in self.held[i]:
            starts = [places.get(name, 0) for name in axes] + [row, 0]
            sizes = [1 if name in places else self.grid.size[name] for name in axes]
            part = lax.dynamic_slice(tensor, starts, sizes + [self.half, self.columns])
            left = [self.grid.size[name] for name in axes if name not in places]
            parts.append(part.reshape(*left, self.half, self.columns))
        return total(parts)

    def prepare(self):
        grid = self.grid
        if self.stage == 0:
            for i in range(2):
                self.held[i].append((self.arrived[0], "hxzy", i * self.half))
        else:
            for tensor, i in zip(self.arrived, self.owners):
                axes = "".join(name for name in "hxzy" if name not in self.picked[i])
                self.held[i].append((tensor, axes, 0))
        self.stage += 1
        if self.stage == 3:
            self.routes = [step for step in grid.far_steps() if step != (0, 0)]
            self.sends = [self.at_far(step).astype(BF) for step in self.routes]
            return
        self.sends, self.routes, self.owners = [], [], []
        for i, order in enumerate(("xy", "yx")):
            name = order[self.stage - 1]
            n, own = grid.size[name], grid.at[name]
            for k in range(1, n):
                self.sends.append(self.slices(i, {name: lax.rem(own + k, n)}).astype(BF))
                self.routes.append((name, k))
                self.owners.append(i)
            self.picked[i][name] = own

    def at_far(self, step):
        place = {
            name: lax.rem(self.grid.at[name] + k, self.grid.size[name]) for name, k in zip("hz", step)
        }
        return jnp.concatenate([self.slices(i, place) for i in range(2)], axis=0)

    def result(self):
        return total([self.at_far((0, 0))] + self.arrived)


def order(values, sent=(), got=()):
    values, sends, arrived = lax.optimization_barrier(
        (values, [s.sends for s in sent], [s.arrived for s in got])
    )
    for scatter, arrays in zip(sent, sends):
        scatter.sends = arrays
    for scatter, arrays in zip(got, arrived):
        scatter.arrived = arrays
    return values


def sum_far(grid, tensor):
    arrived = [grid.far_shift(tensor, s) for s in grid.far_steps() if s != (0, 0)]
    return total([tensor] + arrived).astype(tensor.dtype)


def sum_near(grid, tensor, name):
    arrived = [grid.shift(tensor, name, k) for k in range(1, grid.size[name])]
    return total([tensor] + arrived).astype(tensor.dtype)


def body(
    sizes,
    inputs,
    segment_ids,
    key_mask,
    lead_index,
    cotangent_first,
    cotangent_second,
    w_qkv,
    w_out,
    w_up,
    w_down,
    biases,
    up_bias,
    norm_gains,
    norm_shifts,
    lead_table,
):
    grid = Grid(sizes)
    tokens, model = inputs.shape[1], inputs.shape[2]
    shards = grid.shards
    share = model // shards
    tie = lax.optimization_barrier

    middle_up, middle_down = w_up.shape[1] // 2, w_down.shape[1] // 2
    one = Gather(grid, [w_qkv], [w_qkv.shape[1]])
    two = Gather(
        grid,
        [w_up[:, :middle_up], jnp.concatenate([w_up[:, middle_up:], w_out], axis=1)],
        [w_up.shape[1], w_out.shape[1]],
    )
    three = Gather(grid, [w_down[:, :middle_down], w_down[:, middle_down:]], [w_down.shape[1]])
    rows_small = jnp.concatenate([biases, norm_gains, norm_shifts, lead_table])
    lengths = [t.shape[0] for t in (biases, norm_gains, norm_shifts, lead_table)]
    cuts = [sum(lengths[:i]) for i in range(5)]
    lane = jnp.arange(model, dtype=jnp.int32)[None, :]
    to_lane = (lane == grid.shard * share + jnp.arange(share, dtype=jnp.int32)[:, None]).astype(BF)
    own_up = up_bias.shape[0]
    per_row = model // own_up
    up_rows = shards // per_row
    up_lane = (
        lane == (grid.shard % per_row) * own_up + jnp.arange(own_up, dtype=jnp.int32)[:, None]
    ).astype(BF)
    up_row = jnp.arange(up_rows, dtype=jnp.int32)[:, None] == grid.shard // per_row
    small = jnp.concatenate(
        [
            product(rows_small, to_lane),
            product(jnp.where(up_row, up_bias[None, :], jnp.zeros((), BF)), up_lane),
        ]
    )
    labels = jnp.concatenate(
        [segment_ids, key_mask, jnp.broadcast_to(lead_index.reshape(2, 1), (2, tokens))]
    )
    one.go_far(0)
    start_moved = grid.swapped(inputs[0])
    labels_moved = grid.swapped(labels)
    small = sum_near(grid, sum_near(grid, small.astype(BF), "c"), "y")
    one.far, labels_moved, start_moved, small = tie((one.far, labels_moved, start_moved, small))
    labels = grid.choose(labels, labels_moved)
    start_low = grid.choose(inputs[0], start_moved)
    one.make_lines()
    one.sends, two.chunks[0], small = tie((one.sends, two.chunks[0], small))
    one.go_first()
    two.go_far(0)
    small = sum_far(grid, sum_near(grid, small, "x"))
    one.arrived, two.far[0], small, labels = tie((one.arrived, two.far[0], small, labels))
    small = small.astype(F32)
    bias_full, gains, shifts, lead_rows = (small[cuts[i] : cuts[i + 1]] for i in range(4))
    bias_up = small[cuts[4] :]
    leads = (labels[2, 0], labels[3, 0])
    own_pos = (grid.at["h"] * 2 + grid.at["c"]) * tokens + jnp.arange(tokens, dtype=jnp.int32)
    own_labels = jnp.stack([labels[0], labels[1], own_pos], axis=1)
    key_labels = jnp.concatenate(grid.mates(own_labels))
    own_labels_across, key_labels_across = own_labels.T, key_labels.T
    high = grid.size["h"]

    one.make_planes()
    one.sends, two.chunks[1] = tie((one.sends, two.chunks[1]))
    one.go_second()
    two.go_far(1)
    one.arrived, two.far[1] = tie((one.arrived, two.far[1]))
    one.go_pair_near()
    one.go_pair_far()
    two.make_lines()
    crossed = [t[0] for t in one.pairs]
    crossed, two.sends, three.chunks[0] = tie((crossed, two.sends, three.chunks[0]))
    one.pairs = [(t,) + pair[1:] for t, pair in zip(crossed, one.pairs)]
    two.go_first()
    three.go_far(0)
    (weight_qkv,) = one.result()
    weights = {"qkv": weight_qkv}

    def before_exchange(values):
        values, two.arrived, three.far[0] = tie((values, two.arrived, three.far[0]))
        two.make_planes()
        values, two.sends, three.chunks[1] = tie((values, two.sends, three.chunks[1]))
        two.go_second()
        three.go_far(1)
        return values

    def after_attention(values):
        values, two.arrived, three.far[1] = tie((values, two.arrived, three.far[1]))
        two.go_pair_near()
        two.go_pair_far()
        three.make_lines()
        crossed = [t[0] for t in two.pairs]
        values, crossed, three.sends = tie((values, crossed, three.sends))
        two.pairs = [(t,) + pair[1:] for t, pair in zip(crossed, two.pairs)]
        three.go_first()
        weights["up"], weights["out"] = two.result()
        return values

    def before_gate(values):
        values, three.arrived = tie((values, three.arrived))
        three.make_planes()
        values, three.sends = tie((values, three.sends))
        three.go_second()
        three.go_pair_near()
        return values

    def after_gate(values):
        values, three.arrived = tie((values, three.arrived))
        three.go_pair_far()
        (weights["down"],) = three.result()
        return values

    def keep(values):
        return values

    def forward(start_in, lead_id, hooks):
        chooser = (jnp.arange(lead_rows.shape[0], dtype=jnp.int32) == lead_id).astype(F32)
        lead_vec = jnp.sum(chooser[:, None] * lead_rows, axis=0)
        hidden = start_in + lead_vec[None, :]
        normed = layer_norm(hidden, gains[0], shifts[0]).astype(BF)
        mixed = product(normed, weights["qkv"])
        query = (mixed[:, :model] + bias_full[0]).astype(BF) * jnp.asarray(SCALE, BF)
        both_bias = jnp.concatenate([jnp.zeros((model,), F32), bias_full[1]])
        keys_values = (mixed[:, model:] + both_bias).astype(BF)
        query, keys_values = hooks[0]((query, keys_values))
        mates = grid.mates(keys_values)
        attn_low, lse = attention_forward(query, mates, own_labels, key_labels_across)
        attn_low, lse = hooks[1]((attn_low, lse))
        middle = hidden + product(attn_low, weights["out"]) + bias_full[2]
        normed_mid = layer_norm(middle, gains[1], shifts[1]).astype(BF)
        normed_mid = hooks[2](normed_mid)
        activated, slope = gated(normed_mid, weights["up"], bias_up)
        activated, slope = hooks[3]((activated, slope))
        result = middle + product(activated, weights["down"]) + bias_full[3]
        saved = (
            hidden, normed, query, mates, lse, attn_low, middle, normed_mid, slope, activated, chooser,
        )
        return (result, saved)

    def backward(saved, grad_res, earlier, hooks):
        hidden, normed, query, mates, lse, attn_low, middle, normed_mid, slope, activated, chooser = saved
        last = earlier is not None
        operands, sums = {}, {}

        def start(name, **joined):
            operands.update(joined)
            if last:
                jobs = [tuple(zip(operands[part], earlier[part])) for part in joined]
                sums[name] = Scatter(grid, *weight_terms(grid, jobs))

        def then(values, sent=(), got=()):
            if not last:
                return values
            values = order(values, [sums[name] for name in sent], [sums[name] for name in got])
            for name in sent:
                sums[name].go()
            return values

        def step(values, names, begin=(), got=()):
            if not last:
                return values
            ready = [sums[name] for name in begin]
            values = order(values, ready, [sums[name] for name in (*names, *got)])
            for name in names:
                sums[name].prepare()
            return then(values, sent=[*names, *begin])

        grad_low = grad_res.astype(BF)
        start("down", down=(activated, grad_low))
        grad_low = then(grad_low, sent=["down"])
        bias_down = jnp.sum(grad_low.astype(F32), axis=0)
        grad_low = hooks[0](grad_low)
        grad_gate, bias_gate, grad_normed_mid = gated_backward(
            grad_low, slope, weights["down"], weights["up"]
        )
        grad_gate, grad_normed_mid = hooks[1]((grad_gate, grad_normed_mid))
        grad_gate, grad_normed_mid = step((grad_gate, grad_normed_mid), ["down"])
        start("up", up=(normed_mid, grad_gate))
        mid_pull = jax.vjp(layer_norm, middle, gains[1], shifts[1])[1]
        grad_mid_part, gain_mid, shift_mid = mid_pull(grad_normed_mid)
        grad_mid = grad_res + grad_mid_part
        grad_branch = grad_mid.astype(BF)
        grad_attn = back_product(grad_branch, weights["out"]).astype(BF)
        bias_attn = jnp.sum(grad_branch.astype(F32), axis=0)
        grad_attn = hooks[2](grad_attn)
        grad_attn = step(grad_attn, ["down"], begin=["up"])
        pairs = model // PAIR
        halves = (0, pairs // 2, pairs)

        def attend_back(half):
            first, count = halves[half], halves[half + 1] - halves[half]
            return attention_backward(
                query, mates, grad_attn, attn_low, lse, own_labels_across, key_labels, first, count
            )

        def mix(query_low, near, far):
            both = total([near, far])
            if high > 1:
                both = lax.psum_scatter(both.astype(BF), "h", scatter_dimension=1, tiled=True)
            both = both.astype(BF)
            return jnp.concatenate([query_low, both[0], both[1]], axis=1)

        query_low, near, sent = hooks[3](attend_back(0))
        query_low, near, sent, grad_attn = step((query_low, near, sent, grad_attn), ["down", "up"])
        far = grid.shift(sent, "c", 1)
        other_low, other_near, sent = attend_back(1)
        mixed_low = mix(query_low, near, far)
        start("mix", qkv0=(normed, mixed_low), out=(attn_low, grad_branch))
        other_low, other_near, sent, mixed_low = step(
            (other_low, other_near, sent, mixed_low), ["up"], begin=["mix"], got=["down"]
        )
        far = grid.shift(sent, "c", 1)
        mixed_high = mix(other_low, other_near, far)
        start("qkv1", qkv1=(normed, mixed_high))
        mixed_low, mixed_high = step((mixed_low, mixed_high), ["up", "mix"], begin=["qkv1"])
        grad_mixed = jnp.concatenate(
            [
                p[:, i * p.shape[1] // 3 : (i + 1) * p.shape[1] // 3]
                for i in range(3)
                for p in (mixed_low, mixed_high)
            ],
            axis=1,
        )
        grad_normed = back_product(grad_mixed, weights["qkv"])
        bias_query = jnp.sum(grad_mixed[:, :model].astype(F32), axis=0)
        bias_value = jnp.sum(grad_mixed[:, 2 * model :].astype(F32), axis=0)
        in_pull = jax.vjp(layer_norm, hidden, gains[0], shifts[0])[1]
        grad_in_part, gain_in, shift_in = in_pull(grad_normed)
        grad_start = grad_mid + grad_in_part
        grad_start = step(grad_start, ["mix", "qkv1"], got=["up"])
        lead_sum = jnp.sum(grad_start, axis=0)
        vectors = jnp.concatenate(
            [
                jnp.stack([bias_query, bias_value, bias_attn, bias_down, gain_in, gain_mid, shift_in, shift_mid]),
                chooser[:, None] * lead_sum[None, :],
                bias_gate.reshape(-1, model),
            ]
        )
        return (grad_start, operands, sums, vectors)

    result_first, saved_first = forward(
        start_low.astype(F32), leads[0], [before_exchange, after_attention, before_gate, after_gate]
    )
    first_low = result_first.astype(BF)
    first_low, seed_first, seed_second = tie((first_low, cotangent_first[0], cotangent_second[0]))
    moved = {"second": grid.swapped(seed_second)}

    def moves(begin, *names):
        def hook(values):
            values, taken = tie((values, {name: moved[name] for name in names}))
            moved.update(taken)
            if begin is None:
                return values
            values, sent = tie((values, begin[1]))
            moved[begin[0]] = grid.swapped(sent)
            return values

        return hook

    result_second, saved_second = forward(
        first_low.astype(F32),
        leads[1],
        [keep, moves(("first", seed_first), "second"), keep, moves(None, "first")],
    )
    second_low = result_second.astype(BF)
    seed_second = grid.choose(seed_second, moved["second"])
    seed_second, second_low = tie((seed_second, second_low))
    grad_between, operands, _, vectors_second = backward(
        saved_second,
        seed_second.astype(F32),
        None,
        [
            moves(("first_out", first_low)),
            moves(None, "first_out"),
            moves(("second_out", second_low)),
            moves(None, "second_out"),
        ],
    )
    seed_first = grid.choose(seed_first, moved["first"])
    first_low = grid.choose(first_low, moved["first_out"])
    second_low = grid.choose(second_low, moved["second_out"])
    grad_first, _, sums, vectors_first = backward(
        saved_first, seed_first.astype(F32) + grad_between, operands, [keep] * 4
    )
    vectors = vectors_second + vectors_first
    grad_low = grad_first.astype(BF)

    def step(values, names):
        scatters = [sums[name] for name in names]
        values = order(values, (), scatters)
        for scatter in scatters:
            scatter.prepare()
        values = order(values, scatters, ())
        for scatter in scatters:
            scatter.go()
        return values

    vectors = sum_near(grid, vectors, "c")
    vectors, grad_low = step((vectors, grad_low), ["mix", "qkv1"])
    grad_moved = grid.swapped(grad_low)
    vectors = sum_near(grid, vectors, "y")
    vectors, grad_moved = step((vectors, grad_moved), ["qkv1"])
    vectors = sum_far(grid, sum_near(grid, vectors, "x"))
    input_grad = grid.choose(grad_low, grad_moved).astype(F32)
    shares = {name: sums[name].result() for name in ("down", "up", "mix", "qkv1")}
    width = shares["qkv1"].shape[1] // 3
    parts = [shares["mix"], shares["qkv1"]]
    own_columns = lax.dynamic_slice_in_dim(vectors, grid.shard * share, share, 1)
    small_out = [own_columns[cuts[i] : cuts[i + 1]] for i in range(4)]
    up_out = lax.dynamic_slice(
        vectors, (cuts[4] + grid.shard // per_row, (grid.shard % per_row) * own_up), (1, own_up)
    )[0]
    return (
        first_low[None],
        second_low[None],
        input_grad[None],
        jnp.concatenate([p[:, i * width : (i + 1) * width] for i in range(3) for p in parts], axis=1),
        shares["mix"][:, 3 * width :],
        shares["up"],
        shares["down"],
        small_out[0],
        up_out,
        small_out[1],
        small_out[2],
        small_out[3],
    )


def solution(mesh):
    dp, fsdp = mesh.shape["dp"], mesh.shape["fsdp"]
    tall = fsdp // 8
    sizes = {"h": dp // 2, "x": 2, "z": 4, "y": tall, "c": 2}
    fine = Mesh(np.asarray(mesh.devices).reshape(tuple(sizes.values())), tuple(sizes))
    one, two, every = ("z", "y", "c"), ("h", "x"), ("h", "x", "z", "y", "c")
    placed = (
        P(one, two, None),
        P(one, two),
        P(one, two),
        P(one, None),
        P(one, two, None),
        P(one, two, None),
        P(every, None),
        P(every, None),
        P(every, None),
        P(every, None),
        P(None, every),
        P(every),
        P(None, every),
        P(None, every),
        P(None, every),
    )
    return jax.shard_map(
        partial(body, sizes),
        mesh=fine,
        in_specs=placed,
        out_specs=(
            P(one, two, None),
            P(one, two, None),
            P(one, two, None),
            P(every, None),
            P(every, None),
            P(every, None),
            P(every, None),
            P(None, every),
            P(every),
            P(None, every),
            P(None, every),
            P(None, every),
        ),
        check_vma=False,
    )
```

```python
from functools import partial
import math

import jax
import jax.numpy as jnp
import numpy as np
from jax import lax
from jax.experimental import pallas as pl
from jax.experimental.pallas import tpu as pltpu
from jax.sharding import Mesh, PartitionSpec as P

HEAD = 64
PAIR = 2 * HEAD
LANES = 128
SCALE = 0.125
EPSILON = 1e-06
NEGATIVE = -1e30
ACROSS = (((0,), (0,)), ((), ()))
WITHIN = (((1,), (1,)), ((), ()))
BF = jnp.bfloat16
F32 = jnp.float32


def layer_norm(tensor, gain_row, shift_row):
    average = jnp.mean(tensor, axis=-1, keepdims=True)
    centred = tensor - average
    variance = jnp.mean(centred * centred, axis=-1, keepdims=True)
    return centred * lax.rsqrt(variance + EPSILON) * gain_row + shift_row


def product(left_side, right_side):
    return jnp.dot(left_side, right_side, preferred_element_type=F32)


def outer_sum(left_side, right_side):
    return lax.dot_general(left_side, right_side, ACROSS, preferred_element_type=F32)


def back_product(left_side, right_side):
    return lax.dot_general(left_side, right_side, WITHIN, preferred_element_type=F32)


def fill_bias(bias_ref, query_labels, key_labels):
    query_seg, _, query_pos = query_labels
    key_seg, key_open, key_pos = key_labels
    allowed = (key_seg == query_seg) & ((key_open == 1) | (key_pos == query_pos))
    bias_ref[...] = jnp.where(allowed, 0.0, NEGATIVE)


def columns_of(ref):
    return tuple(ref[:, i : i + 1] for i in range(3))


def rows_of(ref):
    return tuple(ref[i : i + 1, :] for i in range(3))


def half_lanes(tensor, side):
    lane = lax.broadcasted_iota(jnp.int32, tensor.shape, 1)
    return jnp.where((lane < HEAD) == (side == 0), tensor, jnp.zeros((), tensor.dtype))


def attention_forward(query, mates, query_labels, key_labels):
    tokens, model = query.shape
    part = mates[0].shape[0]
    every = 2 * part
    pairs = model // PAIR
    step = math.gcd(tokens, 512)

    def kernel(q_ref, k0_ref, k1_ref, v0_ref, v1_ref, ql_ref, kl_ref, attn_ref, low_ref, lse_ref, bias_ref):
        @pl.when(pl.program_id(0) == 0)
        def _():
            fill_bias(bias_ref, columns_of(ql_ref), rows_of(kl_ref))

        keys_pair = jnp.concatenate([k0_ref[...], k1_ref[...]], axis=0)
        values_pair = jnp.concatenate([v0_ref[...], v1_ref[...]], axis=0)
        for start in range(0, tokens, step):
            query_pair = q_ref[start : start + step, :]
            sides = []
            for side in range(2):
                logits = back_product(half_lanes(query_pair, side), keys_pair)
                logits = logits + bias_ref[start : start + step, :]
                highest = jnp.max(logits, axis=1, keepdims=True)
                weights = jnp.exp(logits - highest)
                denominator = jnp.sum(weights, axis=1, keepdims=True)
                across = jnp.broadcast_to(highest + jnp.log(denominator), (step, PAIR)).T
                lse_ref[0, side : side + 1, start : start + step] = across[0:1]
                sides.append(product(weights.astype(BF), values_pair) / denominator)
            lane = lax.broadcasted_iota(jnp.int32, (step, PAIR), 1)
            both = jnp.where(lane < HEAD, sides[0], sides[1])
            attn_ref[start : start + step, :] = both
            low_ref[start : start + step, :] = both.astype(BF)

    work = 2 * tokens * every * model
    keys_at = pl.BlockSpec((part, PAIR), lambda i: (0, i))
    values_at = pl.BlockSpec((part, PAIR), lambda i: (0, i + pairs))
    return pl.pallas_call(
        kernel,
        grid=(pairs,),
        in_specs=[
            pl.BlockSpec((tokens, PAIR), lambda i: (0, i)),
            keys_at,
            keys_at,
            values_at,
            values_at,
            pl.BlockSpec(query_labels.shape, lambda i: (0, 0)),
            pl.BlockSpec(key_labels.shape, lambda i: (0, 0)),
        ],
        out_specs=[
            pl.BlockSpec((tokens, PAIR), lambda i: (0, i)),
            pl.BlockSpec((tokens, PAIR), lambda i: (0, i)),
            pl.BlockSpec((1, 2, tokens), lambda i: (i, 0, 0)),
        ],
        out_shape=[
            jax.ShapeDtypeStruct((tokens, model), F32),
            jax.ShapeDtypeStruct((tokens, model), BF),
            jax.ShapeDtypeStruct((pairs, 2, tokens), F32),
        ],
        scratch_shapes=[pltpu.VMEM((tokens, every), F32)],
        compiler_params=pltpu.CompilerParams(
            dimension_semantics=("arbitrary",), vmem_limit_bytes=60 << 20
        ),
        cost_estimate=pl.CostEstimate(
            flops=2 * work, transcendentals=work // PAIR, bytes_accessed=10 * every * model
        ),
        name="attention_forward",
    )(query, *mates, *mates, query_labels, key_labels)


def attention_backward(query, mates, grad, attn, lse, query_labels, key_labels, first, pairs):
    tokens = query.shape[0]
    part = mates[0].shape[0]
    every, total_pairs = 2 * part, query.shape[1] // PAIR
    model = pairs * PAIR
    step = math.gcd(part, 512)

    def kernel(q_ref, k0_ref, k1_ref, v0_ref, v1_ref, g_ref, a_ref, lse_ref, ql_ref, kl_ref,
               dq_ref, d0_ref, d1_ref, bias_ref):
        @pl.when(pl.program_id(0) == 0)
        def _():
            fill_bias(bias_ref, rows_of(ql_ref), columns_of(kl_ref))

        query_pair, grad_pair = q_ref[...], g_ref[...]
        overlap = (grad_pair.astype(F32) * a_ref[...]).T
        deltas = [
            jnp.sum(overlap[side * HEAD : (side + 1) * HEAD], axis=0, keepdims=True)
            for side in range(2)
        ]
        query_sides = [half_lanes(query_pair, side) for side in range(2)]
        grad_sides = [half_lanes(grad_pair, side) for side in range(2)]
        grad_query = [jnp.zeros((HEAD, tokens), F32), jnp.zeros((HEAD, tokens), F32)]
        for mate, (k_ref, v_ref, d_ref) in enumerate(((k0_ref, v0_ref, d0_ref), (k1_ref, v1_ref, d1_ref))):
            keys_across = k_ref[...].astype(F32).T.astype(BF)
            for start in range(0, part, step):
                rows = slice(start, start + step)
                grad_keys, grad_values = [], []
                for side in range(2):
                    logits = back_product(k_ref[rows, :], query_sides[side])
                    logits = logits + bias_ref[mate * part + start : mate * part + start + step, :]
                    probs = jnp.exp(logits - lse_ref[0, side : side + 1, :])
                    grad_probs = back_product(v_ref[rows, :], grad_sides[side])
                    grad_logits = (probs * (grad_probs - deltas[side])).astype(BF)
                    grad_values.append(product(probs.astype(BF), grad_sides[side]))
                    grad_keys.append(product(grad_logits, query_sides[side]))
                    grad_query[side] = grad_query[side] + product(
                        keys_across[side * HEAD : (side + 1) * HEAD, rows], grad_logits
                    )
                d_ref[0, rows, :] = (grad_keys[0] + grad_keys[1]).astype(BF)
                d_ref[1, rows, :] = (grad_values[0] + grad_values[1]).astype(BF)
        dq_ref[...] = (jnp.concatenate(grad_query, axis=0).T * SCALE).astype(BF)

    work = 2 * tokens * every * model
    own = pl.BlockSpec((tokens, PAIR), lambda i: (0, i + first))
    keys_at = pl.BlockSpec((part, PAIR), lambda i: (0, i + first))
    values_at = pl.BlockSpec((part, PAIR), lambda i: (0, i + first + total_pairs))
    mate_out = pl.BlockSpec((2, part, PAIR), lambda i: (0, 0, i))
    return pl.pallas_call(
        kernel,
        grid=(pairs,),
        in_specs=[
            own,
            keys_at,
            keys_at,
            values_at,
            values_at,
            own,
            own,
            pl.BlockSpec((1, 2, tokens), lambda i: (i + first, 0, 0)),
            pl.BlockSpec(query_labels.shape, lambda i: (0, 0)),
            pl.BlockSpec(key_labels.shape, lambda i: (0, 0)),
        ],
        out_specs=[pl.BlockSpec((tokens, PAIR), lambda i: (0, i)), mate_out, mate_out],
        out_shape=[
            jax.ShapeDtypeStruct((tokens, model), BF),
            jax.ShapeDtypeStruct((2, part, model), BF),
            jax.ShapeDtypeStruct((2, part, model), BF),
        ],
        scratch_shapes=[pltpu.VMEM((every, tokens), F32)],
        compiler_params=pltpu.CompilerParams(
            dimension_semantics=("arbitrary",), vmem_limit_bytes=60 << 20
        ),
        cost_estimate=pl.CostEstimate(
            flops=5 * work, transcendentals=work // PAIR, bytes_accessed=12 * every * model
        ),
        name="attention_backward",
    )(query, *mates, *mates, grad, attn, lse, query_labels, key_labels)


def gated(normed, weight, bias_rows):
    tokens, model = normed.shape
    hidden_units = weight.shape[1]
    width = math.gcd(bias_rows.shape[1], 512)
    per_row = bias_rows.shape[1] // width
    rows = math.gcd(tokens, 128)
    bias = bias_rows.reshape(-1, 1, width)

    def kernel(x_ref, w_ref, b_ref, act_ref, slope_ref):
        for start in range(0, tokens, rows):
            gate = jnp.dot(
                x_ref[start : start + rows, :], w_ref[...], preferred_element_type=F32
            ) + b_ref[0]
            share = 0.5 + 0.5 * lax.erf(gate * math.sqrt(0.5))
            density = jnp.exp(gate * gate * -0.5) * (1.0 / math.sqrt(2.0 * math.pi))
            act_ref[start : start + rows, :] = (gate * share).astype(BF)
            slope_ref[start : start + rows, :] = (share + gate * density).astype(BF)

    block = pl.BlockSpec((tokens, width), lambda i: (0, i))
    return pl.pallas_call(
        kernel,
        grid=(hidden_units // width,),
        in_specs=[
            pl.BlockSpec((tokens, model), lambda i: (0, 0)),
            pl.BlockSpec((model, width), lambda i: (0, i)),
            pl.BlockSpec((1, 1, width), lambda i: (i, 0, 0)),
        ],
        out_specs=[block, block],
        out_shape=[jax.ShapeDtypeStruct((tokens, hidden_units), BF)] * 2,
        compiler_params=pltpu.CompilerParams(
            dimension_semantics=("arbitrary",), vmem_limit_bytes=40 << 20
        ),
        cost_estimate=pl.CostEstimate(
            flops=2 * tokens * model * hidden_units,
            transcendentals=2 * tokens * hidden_units,
            bytes_accessed=2 * (model + 2 * tokens) * hidden_units,
        ),
        name="gated",
    )(normed, weight, bias)


def gated_backward(grad_low, slope, weight_down, weight_up):
    tokens, model = grad_low.shape
    hidden_units = slope.shape[1]
    width = math.gcd(hidden_units, 1024)
    steps = hidden_units // width
    rows = math.gcd(tokens, 256)

    def kernel(g_ref, s_ref, down_ref, up_ref, gate_ref, bias_ref, out_ref, acc_ref):
        @pl.when(pl.program_id(0) == 0)
        def _():
            acc_ref[...] = jnp.zeros_like(acc_ref)

        column = jnp.zeros((1, width), F32)
        for start in range(0, tokens, rows):
            cut = slice(start, start + rows)
            pulled = back_product(g_ref[cut, :], down_ref[...]) * s_ref[cut, :].astype(F32)
            low = pulled.astype(BF)
            gate_ref[cut, :] = low
            column = column + jnp.sum(low.astype(F32), axis=0, keepdims=True)
            acc_ref[cut, :] += back_product(low, up_ref[...])
        bias_ref[0] = column

        @pl.when(pl.program_id(0) == steps - 1)
        def _():
            out_ref[...] = acc_ref[...]

    return pl.pallas_call(
        kernel,
        grid=(steps,),
        in_specs=[
            pl.BlockSpec((tokens, model), lambda i: (0, 0)),
            pl.BlockSpec((tokens, width), lambda i: (0, i)),
            pl.BlockSpec((width, model), lambda i: (i, 0)),
            pl.BlockSpec((model, width), lambda i: (0, i)),
        ],
        out_specs=[
            pl.BlockSpec((tokens, width), lambda i: (0, i)),
            pl.BlockSpec((1, 1, width), lambda i: (i, 0, 0)),
            pl.BlockSpec((tokens, model), lambda i: (0, 0)),
        ],
        out_shape=[
            jax.ShapeDtypeStruct((tokens, hidden_units), BF),
            jax.ShapeDtypeStruct((steps, 1, width), F32),
            jax.ShapeDtypeStruct((tokens, model), F32),
        ],
        scratch_shapes=[pltpu.VMEM((tokens, model), F32)],
        compiler_params=pltpu.CompilerParams(
            dimension_semantics=("arbitrary",), vmem_limit_bytes=40 << 20
        ),
        cost_estimate=pl.CostEstimate(
            flops=4 * tokens * model * hidden_units,
            transcendentals=0,
            bytes_accessed=4 * (model + tokens) * hidden_units,
        ),
        name="gated_backward",
    )(grad_low, slope, weight_down, weight_up)


def weight_terms(grid, jobs):
    tokens, height = jobs[0][0][0].shape
    shards = grid.shards
    rows = height // shards
    widths = [part[0][0].shape[-1] for _, parts in jobs for part in parts]
    columns = sum(widths)
    if rows % 16:
        acc = jnp.concatenate(
            [
                sum(
                    outer_sum(left, right if at is None else right[at])
                    for left, (right, at) in zip(lefts, part)
                )
                for lefts, parts in jobs
                for part in parts
            ],
            axis=1,
        )
        acc = acc.astype(BF).reshape(shards // 2, 2, rows, columns)
        return tuple(pick(acc, lax.rem(grid.at["c"] + k, 2), 1) for k in range(2))
    lefts = [left for job in jobs for left in job[0]]
    rights = [right for _, parts in jobs for part in parts for right in part]
    depth = len(jobs[0][0])
    left_of = [job for job, (_, parts) in enumerate(jobs) for _ in parts]
    block = 256
    pairs = block // (2 * rows)

    def kernel(at_ref, *refs):
        left_refs, right_refs = refs[: len(lefts)], refs[len(lefts) : len(lefts) + len(rights)]
        kept_ref, sent_ref = refs[len(lefts) + len(rights) :]
        upper = at_ref[4] == 1
        begin = 0
        for part, width in enumerate(widths):
            chunk = math.gcd(width, 1024)
            job = left_of[part]
            for start in range(0, width, chunk):
                acc = None
                for k in range(depth):
                    more = outer_sum(
                        left_refs[job * depth + k][...],
                        right_refs[part * depth + k][:, start : start + chunk],
                    )
                    acc = more if acc is None else acc + more
                acc = acc.reshape(pairs, 2, rows, chunk)
                at = slice(begin + start, begin + start + chunk)
                kept_ref[:, :, at] = jnp.where(upper, acc[:, 1], acc[:, 0]).astype(BF)
                sent_ref[:, :, at] = jnp.where(upper, acc[:, 0], acc[:, 1]).astype(BF)
            begin += width

    def whole(right, at):
        if at is None:
            return pl.BlockSpec(right.shape, lambda i: (0, 0), pipeline_mode=pl.Buffered(1))
        return pl.BlockSpec(
            (None,) + right.shape[1:], lambda i: (at, 0, 0), pipeline_mode=pl.Buffered(1)
        )

    out = pl.BlockSpec((pairs, rows, columns), lambda i: (i, 0, 0))
    return pl.pallas_call(
        kernel,
        grid=(height // block,),
        in_specs=[pl.BlockSpec(memory_space=pltpu.SMEM)]
        + [pl.BlockSpec((tokens, block), lambda i: (0, i))] * len(lefts)
        + [whole(*right) for right in rights],
        out_specs=[out, out],
        out_shape=[jax.ShapeDtypeStruct((shards // 2, rows, columns), BF)] * 2,
        compiler_params=pltpu.CompilerParams(
            dimension_semantics=("arbitrary",), vmem_limit_bytes=48 << 20
        ),
        cost_estimate=pl.CostEstimate(
            flops=2 * depth * tokens * height * columns,
            transcendentals=0,
            bytes_accessed=2 * height * columns + 2 * depth * tokens * (height + columns),
        ),
        name="weight_terms",
    )(grid.places, *lefts, *(right for right, _ in rights))


class Grid:
    def __init__(self, sizes):
        self.size = dict(sizes)
        self.at = {name: lax.axis_index(name) for name in sizes}
        self.places = jnp.stack([self.at[name] for name in sizes]).astype(jnp.int32)
        self.shards = math.prod(sizes.values())
        index = 0
        for name in sizes:
            index = index * sizes[name] + self.at[name]
        self.shard = index

    def shift(self, tensor, axis, step):
        n = self.size[axis]
        return lax.ppermute(tensor, axis, [(i, (i + step) % n) for i in range(n)])

    def far_steps(self):
        return [(a, b) for a in range(self.size["h"]) for b in range(self.size["z"])]

    def far_shift(self, tensor, step):
        high, deep = self.size["h"], self.size["z"]
        pairs = [
            (a * deep + b, ((a + step[0]) % high) * deep + (b + step[1]) % deep)
            for a in range(high)
            for b in range(deep)
        ]
        return lax.ppermute(tensor, ("h", "z"), pairs)

    def swapped(self, tensor):
        return lax.ppermute(tensor, ("x", "c"), [(1, 2), (2, 1)])

    def choose(self, tensor, moved):
        return jnp.where(self.at["x"] == self.at["c"], tensor, moved)

    def mates(self, tensor):
        if self.size["h"] > 1:
            tensor = lax.all_gather(tensor, "h", axis=0, tiled=True)
        return tensor, self.shift(tensor, "c", 1)


def place(places, pieces, out_shapes, moves, room=None):
    count = len(pieces)
    landed = [pltpu.VMEM(piece.shape, piece.dtype) for piece in pieces]

    def kernel(at_ref, *refs):
        ins, outs = refs[:count], refs[count : count + len(out_shapes)]
        held, load_sems, store_sems = refs[-2 - count : -2], refs[-2], refs[-1]
        loads = [
            pltpu.make_async_copy(source, target, load_sems.at[i])
            for i, (source, target) in enumerate(zip(ins, held))
        ]
        for load in loads:
            load.start()
        stores = []
        ready = -1
        for piece, source, target in moves(at_ref, held, outs):
            while ready < piece:
                ready += 1
                loads[ready].wait()
            store = pltpu.make_async_copy(source, target, store_sems.at[len(stores)])
            store.start()
            stores.append(store)
        for store in stores:
            store.wait()

    moved = sum(math.prod(s.shape) * 2 for s in out_shapes)
    return pl.pallas_call(
        kernel,
        out_shape=out_shapes,
        in_specs=[pl.BlockSpec(memory_space=pltpu.SMEM)]
        + [pl.BlockSpec(memory_space=pl.ANY)] * count,
        out_specs=[pl.BlockSpec(memory_space=pl.ANY)] * len(out_shapes),
        scratch_shapes=landed
        + [pltpu.SemaphoreType.DMA((count,)), pltpu.SemaphoreType.DMA((8 * count,))],
        compiler_params=pltpu.CompilerParams(vmem_limit_bytes=room or moved + (4 << 20)),
        cost_estimate=pl.CostEstimate(flops=0, transcendentals=0, bytes_accessed=2 * moved),
        name="place",
    )(places, *pieces)


class Gather:
    def __init__(self, grid, chunks, widths):
        self.grid, self.widths = grid, widths
        self.chunks = list(chunks)
        self.half = chunks[0].shape[0] // 2
        self.columns = sum(chunk.shape[1] for chunk in chunks)
        self.kind = chunks[0].dtype
        self.far = [None] * len(chunks)

    def new(self, *lead):
        return jax.ShapeDtypeStruct((*lead, self.half, self.columns), self.kind)

    def go_far(self, i):
        self.far[i] = [self.grid.far_shift(self.chunks[i], step) for step in self.grid.far_steps()[1:]]

    def make_lines(self):
        high, deep = self.grid.size["h"], self.grid.size["z"]
        steps, half = self.grid.far_steps(), self.half

        widths = [chunk.shape[1] for chunk in self.chunks]
        pieces = [
            (tensor, step, sum(widths[:i]), widths[i])
            for i, chunk in enumerate(self.chunks)
            for tensor, step in zip([chunk] + self.far[i], steps)
        ]

        def moves(at, ins, outs):
            listed = []
            for i, (ref, (_, step, offset, width)) in enumerate(zip(ins, pieces)):
                a = lax.rem(at[0] - step[0] + high, high)
                b = lax.rem(at[2] - step[1] + deep, deep)
                for colour in range(2):
                    listed.append(
                        (
                            i,
                            ref.at[pl.ds(colour * half, half)],
                            outs[colour].at[a, b, :, pl.ds(offset, width)],
                        )
                    )
            return listed

        self.sends = place(
            self.grid.places,
            [p[0] for p in pieces],
            [self.new(high, deep)] * 2,
            moves,
            (60 << 20) if len(self.chunks) > 1 else None,
        )

    def go_first(self):
        self.own = self.sends
        self.arrived = [
            self.grid.shift(t, name, k)
            for t, name in zip(self.sends, "xy")
            for k in range(1, self.grid.size[name])
        ]

    def make_planes(self):
        high, wide, deep, tall = (self.grid.size[name] for name in "hxzy")
        spots = [(0, 0), (1, 0)] + [(0, k) for k in range(1, wide)] + [(1, k) for k in range(1, tall)]

        def moves(at, ins, outs):
            return [(i, ref, outs[c].at[k]) for i, (ref, (c, k)) in enumerate(zip(ins, spots))]

        self.sends = place(
            self.grid.places,
            list(self.own) + self.arrived,
            [self.new(wide, high, deep), self.new(tall, high, deep)],
            moves,
        )

    def go_second(self):
        self.near = [(self.sends[0], 0, 0), (self.sends[1], 1, 0)]
        self.arrived = [
            self.grid.shift(t, name, k)
            for t, name in zip(self.sends, "yx")
            for k in range(1, self.grid.size[name])
        ]

    def go_pair_near(self):
        self.pairs = [(self.grid.shift(t, "c", 1), colour, k) for t, colour, k in self.near]

    def go_pair_far(self):
        counts = [(c, k) for c, name in enumerate("yx") for k in range(1, self.grid.size[name])]
        distant = [(t, c, k) for t, (c, k) in zip(self.arrived, counts)]
        self.near += distant
        self.pairs += [(self.grid.shift(t, "c", 1), colour, k) for t, colour, k in distant]

    def result(self):
        high, wide, deep, tall = (self.grid.size[name] for name in "hxzy")
        half, widths = self.half, self.widths
        pieces = [t + (0,) for t in self.near] + [t + (1,) for t in self.pairs]
        offsets = [sum(widths[:i]) for i in range(len(widths))]

        def moves(at, ins, outs):
            listed = []
            for i, (ref, (_, colour, far, kc)) in enumerate(zip(ins, pieces)):
                pc = lax.rem(at[4] + kc, 2)
                for k in range(wide if colour == 0 else tall):
                    kx, ky = (k, far) if colour == 0 else (far, k)
                    px = lax.rem(at[1] - kx + wide, wide)
                    py = lax.rem(at[3] - ky + tall, tall)
                    for out, offset, width in zip(outs, offsets, widths):
                        listed.append(
                            (
                                i,
                                ref.at[k, :, :, :, pl.ds(offset, width)],
                                out.at[:, px, :, py, pc, pl.ds(colour * half, half)],
                            )
                        )
            return listed

        full = place(
            self.grid.places,
            [t[0] for t in pieces],
            [
                jax.ShapeDtypeStruct((high, wide, deep, tall, 2, 2 * half, width), self.kind)
                for width in widths
            ],
            moves,
        )
        return [t.reshape(-1, width) for t, width in zip(full, widths)]


def pick(tensor, index, axis):
    return lax.dynamic_index_in_dim(tensor, index, axis, keepdims=False)


def total(parts):
    result = parts[0].astype(F32)
    for part in parts[1:]:
        result = result + part.astype(F32)
    return result


def tie(*groups):
    return lax.optimization_barrier(groups)


class Scatter:
    def __init__(self, grid, kept, sent):
        self.grid = grid
        sizes = [grid.size[name] for name in "hxzy"]
        self.rows, self.columns = kept.shape[1:]
        self.half = self.rows // 2
        kept = kept.reshape(*sizes, self.rows, self.columns)
        self.held = [[(kept, "hxzy", i * self.half)] for i in range(2)]
        self.picked = [{}, {}]
        self.sends = [sent.reshape(*sizes, self.rows, self.columns)]
        self.stage = 0

    def go(self, part=0):
        if self.stage == 0:
            self.arrived = [self.grid.shift(self.sends[0], "c", 1)]
        elif self.stage < 3:
            self.arrived = [self.grid.shift(t, *route) for t, route in zip(self.sends, self.routes)]
        else:
            now = list(zip(self.sends, self.routes))[part::2]
            held = self.arrived if part else []
            self.arrived = held + [self.grid.far_shift(t, route) for t, route in now]

    def slices(self, i, extra):
        places = {**self.picked[i], **extra}
        parts = []
        for tensor, axes, row in self.held[i]:
            starts = [places.get(name, 0) for name in axes] + [row, 0]
            sizes = [1 if name in places else self.grid.size[name] for name in axes]
            part = lax.dynamic_slice(tensor, starts, sizes + [self.half, self.columns])
            left = [self.grid.size[name] for name in axes if name not in places]
            parts.append(part.reshape(*left, self.half, self.columns))
        return total(parts)

    def prepare(self):
        grid = self.grid
        if self.stage == 0:
            for i in range(2):
                self.held[i].append((self.arrived[0], "hxzy", i * self.half))
        else:
            for tensor, i in zip(self.arrived, self.owners):
                axes = "".join(name for name in "hxzy" if name not in self.picked[i])
                self.held[i].append((tensor, axes, 0))
        self.stage += 1
        if self.stage == 3:
            self.routes = [step for step in grid.far_steps() if step != (0, 0)]
            self.sends = [self.at_far(step).astype(BF) for step in self.routes]
            return
        self.sends, self.routes, self.owners = [], [], []
        for i, order in enumerate(("xy", "yx")):
            name = order[self.stage - 1]
            n, own = grid.size[name], grid.at[name]
            for k in range(1, n):
                self.sends.append(self.slices(i, {name: lax.rem(own + k, n)}).astype(BF))
                self.routes.append((name, k))
                self.owners.append(i)
            self.picked[i][name] = own

    def at_far(self, step):
        place = {
            name: lax.rem(self.grid.at[name] + k, self.grid.size[name]) for name, k in zip("hz", step)
        }
        return jnp.concatenate([self.slices(i, place) for i in range(2)], axis=0)

    def result(self):
        return total([self.at_far((0, 0))] + self.arrived)


def order(values, sent=(), got=()):
    values, sends, arrived = lax.optimization_barrier(
        (values, [s.sends for s in sent], [s.arrived for s in got])
    )
    for scatter, arrays in zip(sent, sends):
        scatter.sends = arrays
    for scatter, arrays in zip(got, arrived):
        scatter.arrived = arrays
    return values


def advance(values, scatters, begin=(), got=(), rest=()):
    values = order(values, [*begin, *rest], [*scatters, *got])
    for scatter in scatters:
        scatter.prepare()
    values = order(values, [*scatters, *begin, *rest])
    for scatter in (*begin, *scatters):
        scatter.go()
    for scatter in rest:
        scatter.go(1)
    return values


def sum_far(grid, tensor):
    arrived = [grid.far_shift(tensor, s) for s in grid.far_steps() if s != (0, 0)]
    return total([tensor] + arrived).astype(tensor.dtype)


def sum_near(grid, tensor, name):
    arrived = [grid.shift(tensor, name, k) for k in range(1, grid.size[name])]
    return total([tensor] + arrived).astype(tensor.dtype)


def body(
    sizes,
    inputs,
    segment_ids,
    key_mask,
    lead_index,
    cotangent_first,
    cotangent_second,
    w_qkv,
    w_out,
    w_up,
    w_down,
    biases,
    up_bias,
    norm_gains,
    norm_shifts,
    lead_table,
):
    grid = Grid(sizes)
    tokens, model = inputs.shape[1], inputs.shape[2]
    shards = grid.shards
    share = model // shards
    tie = lax.optimization_barrier

    rows_small = jnp.concatenate([biases, norm_gains, norm_shifts, lead_table])
    lengths = [t.shape[0] for t in (biases, norm_gains, norm_shifts, lead_table)]
    cuts = [sum(lengths[:i]) for i in range(5)]
    own_up = up_bias.shape[0]
    per_row = model // own_up
    shard_rows = w_qkv.shape[0]
    tiles = -(-(cuts[4] + 1) // shard_rows)

    def to_lanes(rows, width):
        lane = jnp.arange(LANES, dtype=jnp.int32)[None, :]
        begin = (grid.shard % (LANES // width)) * width
        spread = lane == begin + jnp.arange(width, dtype=jnp.int32)[:, None]
        return product(rows, spread.astype(BF)).astype(BF)

    def from_lanes(tensor, width):
        groups = tensor.reshape(-1, LANES // width, *tensor.shape[1:])
        return jnp.sum(groups.astype(F32), axis=1)

    block = jnp.concatenate([to_lanes(rows_small, share), to_lanes(up_bias[None, :], own_up)])
    block = jnp.pad(block, ((0, tiles * shard_rows - block.shape[0]), (0, 0)))
    block = block.reshape(tiles, shard_rows, LANES).transpose(1, 0, 2).reshape(shard_rows, -1)

    middle_up, middle_down = w_up.shape[1] // 2, w_down.shape[1] // 2
    one = Gather(
        grid, [jnp.concatenate([w_qkv, block], axis=1)], [w_qkv.shape[1], tiles * LANES]
    )
    two = Gather(
        grid,
        [w_up[:, :middle_up], jnp.concatenate([w_up[:, middle_up:], w_out], axis=1)],
        [w_up.shape[1], w_out.shape[1]],
    )
    three = Gather(grid, [w_down[:, :middle_down], w_down[:, middle_down:]], [w_down.shape[1]])
    labels = jnp.concatenate(
        [segment_ids, key_mask, jnp.broadcast_to(lead_index.reshape(2, 1), (2, tokens))]
    )
    one.go_far(0)
    start_moved, labels_moved = grid.swapped(inputs[0]), grid.swapped(labels)
    one.far, labels_moved, start_moved = tie((one.far, labels_moved, start_moved))
    labels = grid.choose(labels, labels_moved)
    leads = (labels[2, 0], labels[3, 0])
    start_low = grid.choose(inputs[0], start_moved)
    own_pos = (grid.at["h"] * 2 + grid.at["c"]) * tokens + jnp.arange(tokens, dtype=jnp.int32)
    own_labels = jnp.stack([labels[0], labels[1], own_pos], axis=1)
    key_labels = jnp.concatenate(grid.mates(own_labels))
    own_labels_across, key_labels_across = own_labels.T, key_labels.T
    high = grid.size["h"]

    one.make_lines()
    one.sends, two.chunks[0] = tie((one.sends, two.chunks[0]))
    one.go_first()
    two.go_far(0)
    one.arrived, two.far[0] = tie((one.arrived, two.far[0]))
    one.make_planes()
    one.sends, two.chunks[1] = tie((one.sends, two.chunks[1]))
    one.go_second()
    two.go_far(1)
    one.arrived, two.far[1] = tie((one.arrived, two.far[1]))
    one.go_pair_near()
    one.go_pair_far()
    two.make_lines()
    crossed = [t[0] for t in one.pairs]
    crossed, two.sends, three.chunks[0] = tie((crossed, two.sends, three.chunks[0]))
    one.pairs = [(t,) + pair[1:] for t, pair in zip(crossed, one.pairs)]
    two.go_first()
    three.go_far(0)
    weight_qkv, small = one.result()
    weights = {"qkv": weight_qkv}
    small = small.reshape(shards, shard_rows, -1)
    up_row, up_lanes = cuts[4] % shard_rows, cuts[4] // shard_rows * LANES
    bias_up = from_lanes(small[:, up_row, up_lanes : up_lanes + LANES][:, None], own_up)
    bias_up = bias_up.reshape(-1, model)
    small = from_lanes(small, share).reshape(-1, shard_rows, tiles, LANES)
    small = small.transpose(2, 1, 0, 3).reshape(tiles * shard_rows, model)
    bias_full, gains, shifts, lead_rows = (small[cuts[i] : cuts[i + 1]] for i in range(4))

    def before_exchange(values):
        values, two.arrived, three.far[0] = tie((values, two.arrived, three.far[0]))
        two.make_planes()
        values, two.sends, three.chunks[1] = tie((values, two.sends, three.chunks[1]))
        two.go_second()
        three.go_far(1)
        return values

    def after_attention(values):
        values, two.arrived, three.far[1] = tie((values, two.arrived, three.far[1]))
        two.go_pair_near()
        two.go_pair_far()
        three.make_lines()
        crossed = [t[0] for t in two.pairs]
        values, crossed, three.sends = tie((values, crossed, three.sends))
        two.pairs = [(t,) + pair[1:] for t, pair in zip(crossed, two.pairs)]
        three.go_first()
        weights["up"], weights["out"] = two.result()
        return values

    def before_gate(values):
        values, three.arrived = tie((values, three.arrived))
        three.make_planes()
        values, three.sends = tie((values, three.sends))
        three.go_second()
        three.go_pair_near()
        return values

    def after_gate(values):
        values, three.arrived = tie((values, three.arrived))
        three.go_pair_far()
        (weights["down"],) = three.result()
        return values

    def keep(values):
        return values

    def forward(start_in, lead_id, hooks):
        chooser = (jnp.arange(lead_rows.shape[0], dtype=jnp.int32) == lead_id).astype(F32)
        lead_vec = jnp.sum(chooser[:, None] * lead_rows, axis=0)
        hidden = start_in + lead_vec[None, :]
        normed = layer_norm(hidden, gains[0], shifts[0]).astype(BF)
        mixed = product(normed, weights["qkv"])
        query = (mixed[:, :model] + bias_full[0]).astype(BF) * jnp.asarray(SCALE, BF)
        both_bias = jnp.concatenate([jnp.zeros((model,), F32), bias_full[1]])
        keys_values = (mixed[:, model:] + both_bias).astype(BF)
        query, keys_values = hooks[0]((query, keys_values))
        mates = grid.mates(keys_values)
        attn, attn_low, lse = attention_forward(query, mates, own_labels, key_labels_across)
        attn_low, lse = hooks[1]((attn_low, lse))
        middle = hidden + product(attn_low, weights["out"]) + bias_full[2]
        normed_mid = layer_norm(middle, gains[1], shifts[1]).astype(BF)
        normed_mid = hooks[2](normed_mid)
        activated, slope = gated(normed_mid, weights["up"], bias_up)
        activated, slope = hooks[3]((activated, slope))
        result = middle + product(activated, weights["down"]) + bias_full[3]
        saved = (
            hidden, normed, query, mates, lse, attn, attn_low, middle, normed_mid, slope, activated,
            chooser,
        )
        return (result, saved)

    def backward(saved, grad_res, earlier, hooks):
        (
            hidden, normed, query, mates, lse, attn, attn_low, middle, normed_mid, slope, activated,
            chooser,
        ) = saved
        last = earlier is not None
        operands, sums = {}, {}

        def start(name, **joined):
            operands.update(joined)
            if last:
                jobs = [
                    (
                        (joined[part][0], earlier[part][0]),
                        list(zip(joined[part][1], earlier[part][1])),
                    )
                    for part in joined
                ]
                sums[name] = Scatter(grid, *weight_terms(grid, jobs))

        def then(values, sent=(), got=()):
            if not last:
                return values
            values = order(values, [sums[name] for name in sent], [sums[name] for name in got])
            for name in sent:
                sums[name].go()
            return values

        def step(values, names, begin=(), got=(), rest=()):
            if not last:
                return values
            return advance(
                values, *([sums[name] for name in group] for group in (names, begin, got, rest))
            )

        grad_low = grad_res.astype(BF)
        start("down", down=(activated, [(grad_low, None)]))
        grad_low = then(grad_low, sent=["down"])
        bias_down = jnp.sum(grad_low.astype(F32), axis=0)
        grad_low = hooks[0](grad_low)
        grad_gate, bias_gate, grad_normed_mid = gated_backward(
            grad_low, slope, weights["down"], weights["up"]
        )
        grad_gate, grad_normed_mid = hooks[1]((grad_gate, grad_normed_mid))
        grad_gate, grad_normed_mid = step((grad_gate, grad_normed_mid), ["down"])
        mid_pull = jax.vjp(layer_norm, middle, gains[1], shifts[1])[1]
        grad_mid_part, gain_mid, shift_mid = mid_pull(grad_normed_mid)
        grad_mid = grad_res + grad_mid_part
        grad_branch = grad_mid.astype(BF)
        grad_attn = back_product(grad_branch, weights["out"]).astype(BF)
        bias_attn = jnp.sum(grad_branch.astype(F32), axis=0)
        start("up", up=(normed_mid, [(grad_gate, None)]), out=(attn_low, [(grad_branch, None)]))
        grad_attn = hooks[2](grad_attn)
        grad_attn = step(grad_attn, ["down"], begin=["up"])
        pairs = model // PAIR
        halves = (0, pairs // 2, pairs)

        def attend_back(half):
            first, count = halves[half], halves[half + 1] - halves[half]
            return attention_backward(
                query, mates, grad_attn, attn, lse, own_labels_across, key_labels, first, count
            )

        def add(near, far):
            both = total([near, far])
            if high > 1:
                both = lax.psum_scatter(both.astype(BF), "h", scatter_dimension=1, tiled=True)
            return both.astype(BF)

        def parts(query_low, both):
            return (normed, [(query_low, None), (both, 0), (both, 1)])

        query_low, near, sent = hooks[3](attend_back(0))
        query_low, near, sent, grad_attn = step((query_low, near, sent, grad_attn), ["down", "up"])
        far = grid.shift(sent, "c", 1)
        other_low, other_near, sent = attend_back(1)
        both = add(near, far)
        start("mix", qkv0=parts(query_low, both))
        other_low, other_near, sent, query_low, both = step(
            (other_low, other_near, sent, query_low, both),
            ["up"],
            begin=["mix"],
            got=["down"],
            rest=["down"],
        )
        far = grid.shift(sent, "c", 1)
        other_both = add(other_near, far)
        start("qkv1", qkv1=parts(other_low, other_both))
        query_low, both, other_low, other_both = step(
            (query_low, both, other_low, other_both), ["up", "mix"], begin=["qkv1"], got=["down"]
        )
        grad_mixed = jnp.concatenate(
            [query_low, other_low, both[0], other_both[0], both[1], other_both[1]], axis=1
        )
        grad_normed = back_product(grad_mixed, weights["qkv"])
        bias_query = jnp.sum(grad_mixed[:, :model].astype(F32), axis=0)
        bias_value = jnp.sum(grad_mixed[:, 2 * model :].astype(F32), axis=0)
        in_pull = jax.vjp(layer_norm, hidden, gains[0], shifts[0])[1]
        grad_in_part, gain_in, shift_in = in_pull(grad_normed)
        grad_start = grad_mid + grad_in_part
        grad_start = step(grad_start, ["mix", "qkv1"], got=["up"], rest=["up"])
        lead_sum = jnp.sum(grad_start, axis=0)
        vectors = jnp.concatenate(
            [
                jnp.stack([bias_query, bias_value, bias_attn, bias_down, gain_in, gain_mid, shift_in, shift_mid]),
                chooser[:, None] * lead_sum[None, :],
                bias_gate.reshape(-1, model),
            ]
        )
        return (grad_start, operands, sums, vectors)

    result_first, saved_first = forward(
        start_low.astype(F32), leads[0], [before_exchange, after_attention, before_gate, after_gate]
    )
    first_low = result_first.astype(BF)
    first_low, seed_first, seed_second = tie((first_low, cotangent_first[0], cotangent_second[0]))
    moved = {"second": grid.swapped(seed_second)}

    def moves(begin, *names):
        def hook(values):
            values, taken = tie((values, {name: moved[name] for name in names}))
            moved.update(taken)
            if begin is None:
                return values
            values, sent = tie((values, begin[1]))
            moved[begin[0]] = grid.swapped(sent)
            return values

        return hook

    result_second, saved_second = forward(
        first_low.astype(F32),
        leads[1],
        [keep, moves(("first", seed_first), "second"), keep, moves(None, "first")],
    )
    second_low = result_second.astype(BF)
    seed_second = grid.choose(seed_second, moved["second"])
    seed_second, second_low = tie((seed_second, second_low))
    grad_between, operands, _, vectors_second = backward(
        saved_second,
        seed_second.astype(F32),
        None,
        [
            moves(("first_out", first_low)),
            moves(None, "first_out"),
            moves(("second_out", second_low)),
            moves(None, "second_out"),
        ],
    )
    seed_first = grid.choose(seed_first, moved["first"])
    first_low = grid.choose(first_low, moved["first_out"])
    second_low = grid.choose(second_low, moved["second_out"])
    grad_first, _, sums, vectors_first = backward(
        saved_first, seed_first.astype(F32) + grad_between, operands, [keep] * 4
    )
    vectors = vectors_second + vectors_first
    grad_low = grad_first.astype(BF)

    mix, qkv1, up = (sums[name] for name in ("mix", "qkv1", "up"))
    vectors, grad_low = advance((vectors, grad_low), [mix, qkv1], got=[up])
    mix.go(1)
    vectors = sum_near(grid, sum_near(grid, vectors, "c"), "y")
    vectors, grad_low = advance((vectors, grad_low), [qkv1])
    qkv1.go(1)
    grad_moved = grid.swapped(grad_low)
    vectors = sum_far(grid, sum_near(grid, vectors, "x"))
    input_grad = grid.choose(grad_low, grad_moved).astype(F32)
    shares = {name: sums[name].result() for name in ("down", "up", "mix", "qkv1")}
    width = shares["qkv1"].shape[1] // 3
    sides = [shares["mix"], shares["qkv1"]]
    own_columns = lax.dynamic_slice_in_dim(vectors, grid.shard * share, share, 1)
    small_out = [own_columns[cuts[i] : cuts[i + 1]] for i in range(4)]
    up_out = lax.dynamic_slice(
        vectors, (cuts[4] + grid.shard // per_row, (grid.shard % per_row) * own_up), (1, own_up)
    )[0]
    return (
        first_low[None],
        second_low[None],
        input_grad[None],
        jnp.concatenate([p[:, i * width : (i + 1) * width] for i in range(3) for p in sides], axis=1),
        shares["up"][:, w_up.shape[1] :],
        shares["up"][:, : w_up.shape[1]],
        shares["down"],
        small_out[0],
        up_out,
        small_out[1],
        small_out[2],
        small_out[3],
    )


def solution(mesh):
    dp, fsdp = mesh.shape["dp"], mesh.shape["fsdp"]
    tall = fsdp // 8
    sizes = {"h": dp // 2, "x": 2, "z": 4, "y": tall, "c": 2}
    fine = Mesh(np.asarray(mesh.devices).reshape(tuple(sizes.values())), tuple(sizes))
    one, two, every = ("z", "y", "c"), ("h", "x"), ("h", "x", "z", "y", "c")
    placed = (
        P(one, two, None),
        P(one, two),
        P(one, two),
        P(one, None),
        P(one, two, None),
        P(one, two, None),
        P(every, None),
        P(every, None),
        P(every, None),
        P(every, None),
        P(None, every),
        P(every),
        P(None, every),
        P(None, every),
        P(None, every),
    )
    return jax.shard_map(
        partial(body, sizes),
        mesh=fine,
        in_specs=placed,
        out_specs=(
            P(one, two, None),
            P(one, two, None),
            P(one, two, None),
            P(every, None),
            P(every, None),
            P(every, None),
            P(every, None),
            P(None, every),
            P(every),
            P(None, every),
            P(None, every),
            P(None, every),
        ),
        check_vma=False,
    )
```

```python
from functools import partial
import math

import jax
import jax.numpy as jnp
import numpy as np
from jax import lax
from jax.experimental import pallas as pl
from jax.experimental.pallas import tpu as pltpu
from jax.sharding import Mesh, PartitionSpec as P

HEAD = 64
PAIR = 2 * HEAD
LANES = 128
SCALE = 0.125
EPSILON = 1e-06
NEGATIVE = -1e30
ACROSS = (((0,), (0,)), ((), ()))
WITHIN = (((1,), (1,)), ((), ()))
BF = jnp.bfloat16
F32 = jnp.float32


def layer_norm(tensor, gain_row, shift_row):
    average = jnp.mean(tensor, axis=-1, keepdims=True)
    centred = tensor - average
    variance = jnp.mean(centred * centred, axis=-1, keepdims=True)
    return centred * lax.rsqrt(variance + EPSILON) * gain_row + shift_row


def product(left_side, right_side):
    return jnp.dot(left_side, right_side, preferred_element_type=F32)


def outer_sum(left_side, right_side):
    return lax.dot_general(left_side, right_side, ACROSS, preferred_element_type=F32)


def back_product(left_side, right_side):
    return lax.dot_general(left_side, right_side, WITHIN, preferred_element_type=F32)


def fill_bias(bias_ref, query_labels, key_labels):
    query_seg, _, query_pos = query_labels
    key_seg, key_open, key_pos = key_labels
    allowed = (key_seg == query_seg) & ((key_open == 1) | (key_pos == query_pos))
    bias_ref[...] = jnp.where(allowed, 0.0, NEGATIVE)


def columns_of(ref):
    return tuple(ref[:, i : i + 1] for i in range(3))


def rows_of(ref):
    return tuple(ref[i : i + 1, :] for i in range(3))


def half_lanes(tensor, side):
    lane = lax.broadcasted_iota(jnp.int32, tensor.shape, 1)
    return jnp.where((lane < HEAD) == (side == 0), tensor, jnp.zeros((), tensor.dtype))


def attention_forward(query, mates, query_labels, key_labels):
    tokens, model = query.shape
    part = mates[0].shape[0]
    every = 2 * part
    pairs = model // PAIR
    step = math.gcd(tokens, 512)

    def kernel(q_ref, k0_ref, k1_ref, v0_ref, v1_ref, ql_ref, kl_ref, attn_ref, low_ref, lse_ref, bias_ref):
        @pl.when(pl.program_id(0) == 0)
        def _():
            fill_bias(bias_ref, columns_of(ql_ref), rows_of(kl_ref))

        keys_pair = jnp.concatenate([k0_ref[...], k1_ref[...]], axis=0)
        values_pair = jnp.concatenate([v0_ref[...], v1_ref[...]], axis=0)
        for start in range(0, tokens, step):
            query_pair = q_ref[start : start + step, :]
            sides = []
            for side in range(2):
                logits = back_product(half_lanes(query_pair, side), keys_pair)
                logits = logits + bias_ref[start : start + step, :]
                highest = jnp.max(logits, axis=1, keepdims=True)
                weights = jnp.exp(logits - highest)
                denominator = jnp.sum(weights, axis=1, keepdims=True)
                across = jnp.broadcast_to(highest + jnp.log(denominator), (step, PAIR)).T
                lse_ref[0, side : side + 1, start : start + step] = across[0:1]
                sides.append(product(weights.astype(BF), values_pair) / denominator)
            lane = lax.broadcasted_iota(jnp.int32, (step, PAIR), 1)
            both = jnp.where(lane < HEAD, sides[0], sides[1])
            attn_ref[start : start + step, :] = both
            low_ref[start : start + step, :] = both.astype(BF)

    work = 2 * tokens * every * model
    keys_at = pl.BlockSpec((part, PAIR), lambda i: (0, i))
    values_at = pl.BlockSpec((part, PAIR), lambda i: (0, i + pairs))
    return pl.pallas_call(
        kernel,
        grid=(pairs,),
        in_specs=[
            pl.BlockSpec((tokens, PAIR), lambda i: (0, i)),
            keys_at,
            keys_at,
            values_at,
            values_at,
            pl.BlockSpec(query_labels.shape, lambda i: (0, 0)),
            pl.BlockSpec(key_labels.shape, lambda i: (0, 0)),
        ],
        out_specs=[
            pl.BlockSpec((tokens, PAIR), lambda i: (0, i)),
            pl.BlockSpec((tokens, PAIR), lambda i: (0, i)),
            pl.BlockSpec((1, 2, tokens), lambda i: (i, 0, 0)),
        ],
        out_shape=[
            jax.ShapeDtypeStruct((tokens, model), F32),
            jax.ShapeDtypeStruct((tokens, model), BF),
            jax.ShapeDtypeStruct((pairs, 2, tokens), F32),
        ],
        scratch_shapes=[pltpu.VMEM((tokens, every), F32)],
        compiler_params=pltpu.CompilerParams(
            dimension_semantics=("arbitrary",), vmem_limit_bytes=60 << 20
        ),
        cost_estimate=pl.CostEstimate(
            flops=2 * work, transcendentals=work // PAIR, bytes_accessed=10 * every * model
        ),
        name="attention_forward",
    )(query, *mates, *mates, query_labels, key_labels)


def attention_backward(query, mates, grad, attn, lse, query_labels, key_labels, first, pairs):
    tokens = query.shape[0]
    part = mates[0].shape[0]
    every, total_pairs = 2 * part, query.shape[1] // PAIR
    model = pairs * PAIR
    step = math.gcd(part, 512)

    def kernel(q_ref, k0_ref, k1_ref, v0_ref, v1_ref, g_ref, a_ref, lse_ref, ql_ref, kl_ref,
               dq_ref, d0_ref, d1_ref, bias_ref):
        @pl.when(pl.program_id(0) == 0)
        def _():
            fill_bias(bias_ref, rows_of(ql_ref), columns_of(kl_ref))

        query_pair, grad_pair = q_ref[...], g_ref[...]
        overlap = (grad_pair.astype(F32) * a_ref[...]).T
        deltas = [
            jnp.sum(overlap[side * HEAD : (side + 1) * HEAD], axis=0, keepdims=True)
            for side in range(2)
        ]
        query_sides = [half_lanes(query_pair, side) for side in range(2)]
        grad_sides = [half_lanes(grad_pair, side) for side in range(2)]
        grad_query = [jnp.zeros((HEAD, tokens), F32), jnp.zeros((HEAD, tokens), F32)]
        for mate, (k_ref, v_ref, d_ref) in enumerate(((k0_ref, v0_ref, d0_ref), (k1_ref, v1_ref, d1_ref))):
            keys_across = k_ref[...].astype(F32).T.astype(BF)
            for start in range(0, part, step):
                rows = slice(start, start + step)
                grad_keys, grad_values = [], []
                for side in range(2):
                    logits = back_product(k_ref[rows, :], query_sides[side])
                    logits = logits + bias_ref[mate * part + start : mate * part + start + step, :]
                    probs = jnp.exp(logits - lse_ref[0, side : side + 1, :])
                    grad_probs = back_product(v_ref[rows, :], grad_sides[side])
                    grad_logits = (probs * (grad_probs - deltas[side])).astype(BF)
                    grad_values.append(product(probs.astype(BF), grad_sides[side]))
                    grad_keys.append(product(grad_logits, query_sides[side]))
                    grad_query[side] = grad_query[side] + product(
                        keys_across[side * HEAD : (side + 1) * HEAD, rows], grad_logits
                    )
                d_ref[0, rows, :] = (grad_keys[0] + grad_keys[1]).astype(BF)
                d_ref[1, rows, :] = (grad_values[0] + grad_values[1]).astype(BF)
        dq_ref[...] = (jnp.concatenate(grad_query, axis=0).T * SCALE).astype(BF)

    work = 2 * tokens * every * model
    own = pl.BlockSpec((tokens, PAIR), lambda i: (0, i + first))
    keys_at = pl.BlockSpec((part, PAIR), lambda i: (0, i + first))
    values_at = pl.BlockSpec((part, PAIR), lambda i: (0, i + first + total_pairs))
    mate_out = pl.BlockSpec((2, part, PAIR), lambda i: (0, 0, i))
    return pl.pallas_call(
        kernel,
        grid=(pairs,),
        in_specs=[
            own,
            keys_at,
            keys_at,
            values_at,
            values_at,
            own,
            own,
            pl.BlockSpec((1, 2, tokens), lambda i: (i + first, 0, 0)),
            pl.BlockSpec(query_labels.shape, lambda i: (0, 0)),
            pl.BlockSpec(key_labels.shape, lambda i: (0, 0)),
        ],
        out_specs=[pl.BlockSpec((tokens, PAIR), lambda i: (0, i)), mate_out, mate_out],
        out_shape=[
            jax.ShapeDtypeStruct((tokens, model), BF),
            jax.ShapeDtypeStruct((2, part, model), BF),
            jax.ShapeDtypeStruct((2, part, model), BF),
        ],
        scratch_shapes=[pltpu.VMEM((every, tokens), F32)],
        compiler_params=pltpu.CompilerParams(
            dimension_semantics=("arbitrary",), vmem_limit_bytes=60 << 20
        ),
        cost_estimate=pl.CostEstimate(
            flops=5 * work, transcendentals=work // PAIR, bytes_accessed=12 * every * model
        ),
        name="attention_backward",
    )(query, *mates, *mates, grad, attn, lse, query_labels, key_labels)


def gated(normed, weight, bias_rows):
    tokens, model = normed.shape
    hidden_units = weight.shape[1]
    width = math.gcd(bias_rows.shape[1], 512)
    per_row = bias_rows.shape[1] // width
    rows = math.gcd(tokens, 256)
    bias = bias_rows.reshape(-1, 1, width)

    def kernel(x_ref, w_ref, b_ref, act_ref, slope_ref):
        for start in range(0, tokens, rows):
            gate = jnp.dot(
                x_ref[start : start + rows, :], w_ref[...], preferred_element_type=F32
            ) + b_ref[0]
            share = 0.5 + 0.5 * lax.erf(gate * math.sqrt(0.5))
            density = jnp.exp(gate * gate * -0.5) * (1.0 / math.sqrt(2.0 * math.pi))
            act_ref[start : start + rows, :] = (gate * share).astype(BF)
            slope_ref[start : start + rows, :] = (share + gate * density).astype(BF)

    block = pl.BlockSpec((tokens, width), lambda i: (0, i))
    return pl.pallas_call(
        kernel,
        grid=(hidden_units // width,),
        in_specs=[
            pl.BlockSpec((tokens, model), lambda i: (0, 0)),
            pl.BlockSpec((model, width), lambda i: (0, i)),
            pl.BlockSpec((1, 1, width), lambda i: (i, 0, 0)),
        ],
        out_specs=[block, block],
        out_shape=[jax.ShapeDtypeStruct((tokens, hidden_units), BF)] * 2,
        compiler_params=pltpu.CompilerParams(
            dimension_semantics=("arbitrary",), vmem_limit_bytes=40 << 20
        ),
        cost_estimate=pl.CostEstimate(
            flops=2 * tokens * model * hidden_units,
            transcendentals=2 * tokens * hidden_units,
            bytes_accessed=2 * (model + 2 * tokens) * hidden_units,
        ),
        name="gated",
    )(normed, weight, bias)


def gated_backward(grad_low, slope, weight_down, weight_up):
    tokens, model = grad_low.shape
    hidden_units = slope.shape[1]
    width = math.gcd(hidden_units, 1024)
    steps = hidden_units // width
    rows = math.gcd(tokens, 256)

    def kernel(g_ref, s_ref, down_ref, up_ref, gate_ref, bias_ref, out_ref, acc_ref):
        @pl.when(pl.program_id(0) == 0)
        def _():
            acc_ref[...] = jnp.zeros_like(acc_ref)

        column = jnp.zeros((1, width), F32)
        for start in range(0, tokens, rows):
            cut = slice(start, start + rows)
            pulled = back_product(g_ref[cut, :], down_ref[...]) * s_ref[cut, :].astype(F32)
            low = pulled.astype(BF)
            gate_ref[cut, :] = low
            column = column + jnp.sum(low.astype(F32), axis=0, keepdims=True)
            acc_ref[cut, :] += back_product(low, up_ref[...])
        bias_ref[0] = column

        @pl.when(pl.program_id(0) == steps - 1)
        def _():
            out_ref[...] = acc_ref[...]

    return pl.pallas_call(
        kernel,
        grid=(steps,),
        in_specs=[
            pl.BlockSpec((tokens, model), lambda i: (0, 0)),
            pl.BlockSpec((tokens, width), lambda i: (0, i)),
            pl.BlockSpec((width, model), lambda i: (i, 0)),
            pl.BlockSpec((model, width), lambda i: (0, i)),
        ],
        out_specs=[
            pl.BlockSpec((tokens, width), lambda i: (0, i)),
            pl.BlockSpec((1, 1, width), lambda i: (i, 0, 0)),
            pl.BlockSpec((tokens, model), lambda i: (0, 0)),
        ],
        out_shape=[
            jax.ShapeDtypeStruct((tokens, hidden_units), BF),
            jax.ShapeDtypeStruct((steps, 1, width), F32),
            jax.ShapeDtypeStruct((tokens, model), F32),
        ],
        scratch_shapes=[pltpu.VMEM((tokens, model), F32)],
        compiler_params=pltpu.CompilerParams(
            dimension_semantics=("arbitrary",), vmem_limit_bytes=40 << 20
        ),
        cost_estimate=pl.CostEstimate(
            flops=4 * tokens * model * hidden_units,
            transcendentals=0,
            bytes_accessed=4 * (model + tokens) * hidden_units,
        ),
        name="gated_backward",
    )(grad_low, slope, weight_down, weight_up)


def weight_terms(grid, jobs):
    tokens, height = jobs[0][0][0].shape
    shards = grid.shards
    rows = height // shards
    widths = [part[0][0].shape[-1] for _, parts in jobs for part in parts]
    columns = sum(widths)
    if rows % 16:
        acc = jnp.concatenate(
            [
                sum(
                    outer_sum(left, right if at is None else right[at])
                    for left, (right, at) in zip(lefts, part)
                )
                for lefts, parts in jobs
                for part in parts
            ],
            axis=1,
        )
        acc = acc.astype(BF).reshape(shards // 2, 2, rows, columns)
        return tuple(pick(acc, lax.rem(grid.at["c"] + k, 2), 1) for k in range(2))
    lefts = [left for job in jobs for left in job[0]]
    rights = [right for _, parts in jobs for part in parts for right in part]
    depth = len(jobs[0][0])
    left_of = [job for job, (_, parts) in enumerate(jobs) for _ in parts]
    block = 1024 if height > 1024 else 256
    pairs = block // (2 * rows)

    def kernel(at_ref, *refs):
        left_refs, right_refs = refs[: len(lefts)], refs[len(lefts) : len(lefts) + len(rights)]
        kept_ref, sent_ref = refs[len(lefts) + len(rights) :]
        upper = at_ref[4] == 1
        begin = 0
        for part, width in enumerate(widths):
            chunk = math.gcd(width, 1024)
            job = left_of[part]
            for start in range(0, width, chunk):
                acc = None
                for k in range(depth):
                    more = outer_sum(
                        left_refs[job * depth + k][...],
                        right_refs[part * depth + k][:, start : start + chunk],
                    )
                    acc = more if acc is None else acc + more
                acc = acc.reshape(pairs, 2, rows, chunk)
                at = slice(begin + start, begin + start + chunk)
                kept_ref[:, :, at] = jnp.where(upper, acc[:, 1], acc[:, 0]).astype(BF)
                sent_ref[:, :, at] = jnp.where(upper, acc[:, 0], acc[:, 1]).astype(BF)
            begin += width

    def whole(right, at):
        if at is None:
            return pl.BlockSpec(right.shape, lambda i: (0, 0), pipeline_mode=pl.Buffered(1))
        return pl.BlockSpec(
            (None,) + right.shape[1:], lambda i: (at, 0, 0), pipeline_mode=pl.Buffered(1)
        )

    out = pl.BlockSpec((pairs, rows, columns), lambda i: (i, 0, 0))
    return pl.pallas_call(
        kernel,
        grid=(height // block,),
        in_specs=[pl.BlockSpec(memory_space=pltpu.SMEM)]
        + [pl.BlockSpec((tokens, block), lambda i: (0, i))] * len(lefts)
        + [whole(*right) for right in rights],
        out_specs=[out, out],
        out_shape=[jax.ShapeDtypeStruct((shards // 2, rows, columns), BF)] * 2,
        compiler_params=pltpu.CompilerParams(
            dimension_semantics=("arbitrary",), vmem_limit_bytes=(60 if height > 1024 else 48) << 20
        ),
        cost_estimate=pl.CostEstimate(
            flops=2 * depth * tokens * height * columns,
            transcendentals=0,
            bytes_accessed=2 * height * columns + 2 * depth * tokens * (height + columns),
        ),
        name="weight_terms",
    )(grid.places, *lefts, *(right for right, _ in rights))


class Grid:
    def __init__(self, sizes):
        self.size = dict(sizes)
        self.at = {name: lax.axis_index(name) for name in sizes}
        self.places = jnp.stack([self.at[name] for name in sizes]).astype(jnp.int32)
        self.shards = math.prod(sizes.values())
        index = 0
        for name in sizes:
            index = index * sizes[name] + self.at[name]
        self.shard = index

    def shift(self, tensor, axis, step):
        n = self.size[axis]
        return lax.ppermute(tensor, axis, [(i, (i + step) % n) for i in range(n)])

    def far_steps(self):
        return [(a, b) for a in range(self.size["h"]) for b in range(self.size["z"])]

    def far_shift(self, tensor, step):
        high, deep = self.size["h"], self.size["z"]
        pairs = [
            (a * deep + b, ((a + step[0]) % high) * deep + (b + step[1]) % deep)
            for a in range(high)
            for b in range(deep)
        ]
        return lax.ppermute(tensor, ("h", "z"), pairs)

    def swapped(self, tensor):
        return lax.ppermute(tensor, ("x", "c"), [(1, 2), (2, 1)])

    def choose(self, tensor, moved):
        return jnp.where(self.at["x"] == self.at["c"], tensor, moved)

    def mates(self, tensor):
        if self.size["h"] > 1:
            tensor = lax.all_gather(tensor, "h", axis=0, tiled=True)
        return tensor, self.shift(tensor, "c", 1)


def place(places, pieces, out_shapes, moves, room=None):
    count = len(pieces)
    landed = [pltpu.VMEM(piece.shape, piece.dtype) for piece in pieces]

    def kernel(at_ref, *refs):
        ins, outs = refs[:count], refs[count : count + len(out_shapes)]
        held, load_sems, store_sems = refs[-2 - count : -2], refs[-2], refs[-1]
        loads = [
            pltpu.make_async_copy(source, target, load_sems.at[i])
            for i, (source, target) in enumerate(zip(ins, held))
        ]
        for load in loads:
            load.start()
        stores = []
        ready = -1
        for piece, source, target in moves(at_ref, held, outs):
            while ready < piece:
                ready += 1
                loads[ready].wait()
            store = pltpu.make_async_copy(source, target, store_sems.at[len(stores)])
            store.start()
            stores.append(store)
        for store in stores:
            store.wait()

    moved = sum(math.prod(s.shape) * 2 for s in out_shapes)
    return pl.pallas_call(
        kernel,
        out_shape=out_shapes,
        in_specs=[pl.BlockSpec(memory_space=pltpu.SMEM)]
        + [pl.BlockSpec(memory_space=pl.ANY)] * count,
        out_specs=[pl.BlockSpec(memory_space=pl.ANY)] * len(out_shapes),
        scratch_shapes=landed
        + [pltpu.SemaphoreType.DMA((count,)), pltpu.SemaphoreType.DMA((8 * count,))],
        compiler_params=pltpu.CompilerParams(vmem_limit_bytes=room or moved + (4 << 20)),
        cost_estimate=pl.CostEstimate(flops=0, transcendentals=0, bytes_accessed=2 * moved),
        name="place",
    )(places, *pieces)


class Gather:
    def __init__(self, grid, chunks, widths):
        self.grid, self.widths = grid, widths
        self.chunks = list(chunks)
        self.half = chunks[0].shape[0] // 2
        self.columns = sum(chunk.shape[1] for chunk in chunks)
        self.kind = chunks[0].dtype
        self.far = [None] * len(chunks)
        self.roomy = len(widths) > 1 or len(chunks) > 1

    def new(self, *lead):
        return jax.ShapeDtypeStruct((*lead, self.half, self.columns), self.kind)

    def go_far(self, i):
        self.far[i] = [self.grid.far_shift(self.chunks[i], step) for step in self.grid.far_steps()[1:]]

    def make_lines(self):
        high, deep = self.grid.size["h"], self.grid.size["z"]
        steps, half = self.grid.far_steps(), self.half

        widths = [chunk.shape[1] for chunk in self.chunks]
        pieces = [
            (tensor, step, sum(widths[:i]), widths[i])
            for i, chunk in enumerate(self.chunks)
            for tensor, step in zip([chunk] + self.far[i], steps)
        ]

        def moves(at, ins, outs):
            listed = []
            for i, (ref, (_, step, offset, width)) in enumerate(zip(ins, pieces)):
                a = lax.rem(at[0] - step[0] + high, high)
                b = lax.rem(at[2] - step[1] + deep, deep)
                for colour in range(2):
                    listed.append(
                        (
                            i,
                            ref.at[pl.ds(colour * half, half)],
                            outs[colour].at[a, b, :, pl.ds(offset, width)],
                        )
                    )
            return listed

        self.sends = place(
            self.grid.places,
            [p[0] for p in pieces],
            [self.new(high, deep)] * 2,
            moves,
            (60 << 20) if self.roomy else None,
        )

    def go_first(self):
        self.own = self.sends
        self.arrived = [
            self.grid.shift(t, name, k)
            for t, name in zip(self.sends, "xy")
            for k in range(1, self.grid.size[name])
        ]

    def make_planes(self):
        high, wide, deep, tall = (self.grid.size[name] for name in "hxzy")
        spots = [(0, 0), (1, 0)] + [(0, k) for k in range(1, wide)] + [(1, k) for k in range(1, tall)]

        def moves(at, ins, outs):
            return [(i, ref, outs[c].at[k]) for i, (ref, (c, k)) in enumerate(zip(ins, spots))]

        self.sends = place(
            self.grid.places,
            list(self.own) + self.arrived,
            [self.new(wide, high, deep), self.new(tall, high, deep)],
            moves,
        )

    def go_second(self):
        self.near = [(self.sends[0], 0, 0), (self.sends[1], 1, 0)]
        self.arrived = [
            self.grid.shift(t, name, k)
            for t, name in zip(self.sends, "yx")
            for k in range(1, self.grid.size[name])
        ]

    def go_pair_near(self):
        self.pairs = [(self.grid.shift(t, "c", 1), colour, k) for t, colour, k in self.near]

    def go_pair_far(self):
        counts = [(c, k) for c, name in enumerate("yx") for k in range(1, self.grid.size[name])]
        distant = [(t, c, k) for t, (c, k) in zip(self.arrived, counts)]
        self.near += distant
        self.pairs += [(self.grid.shift(t, "c", 1), colour, k) for t, colour, k in distant]

    def result(self):
        high, wide, deep, tall = (self.grid.size[name] for name in "hxzy")
        half, widths = self.half, self.widths
        pieces = [t + (0,) for t in self.near] + [t + (1,) for t in self.pairs]
        offsets = [sum(widths[:i]) for i in range(len(widths))]

        def moves(at, ins, outs):
            listed = []
            for i, (ref, (_, colour, far, kc)) in enumerate(zip(ins, pieces)):
                pc = lax.rem(at[4] + kc, 2)
                for k in range(wide if colour == 0 else tall):
                    kx, ky = (k, far) if colour == 0 else (far, k)
                    px = lax.rem(at[1] - kx + wide, wide)
                    py = lax.rem(at[3] - ky + tall, tall)
                    for out, offset, width in zip(outs, offsets, widths):
                        listed.append(
                            (
                                i,
                                ref.at[k, :, :, :, pl.ds(offset, width)],
                                out.at[:, px, :, py, pc, pl.ds(colour * half, half)],
                            )
                        )
            return listed

        full = place(
            self.grid.places,
            [t[0] for t in pieces],
            [
                jax.ShapeDtypeStruct((high, wide, deep, tall, 2, 2 * half, width), self.kind)
                for width in widths
            ],
            moves,
        )
        return [t.reshape(-1, width) for t, width in zip(full, widths)]


def pick(tensor, index, axis):
    return lax.dynamic_index_in_dim(tensor, index, axis, keepdims=False)


def total(parts):
    result = parts[0].astype(F32)
    for part in parts[1:]:
        result = result + part.astype(F32)
    return result


def tie(*groups):
    return lax.optimization_barrier(groups)


class Scatter:
    def __init__(self, grid, kept, sent):
        self.grid = grid
        sizes = [grid.size[name] for name in "hxzy"]
        self.rows, self.columns = kept.shape[1:]
        self.half = self.rows // 2
        kept = kept.reshape(*sizes, self.rows, self.columns)
        self.held = [[(kept, "hxzy", i * self.half)] for i in range(2)]
        self.picked = [{}, {}]
        self.sends = [sent.reshape(*sizes, self.rows, self.columns)]
        self.stage = 0

    def go(self, part=0):
        if self.stage == 0:
            self.arrived = [self.grid.shift(self.sends[0], "c", 1)]
        elif self.stage < 3:
            self.arrived = [self.grid.shift(t, *route) for t, route in zip(self.sends, self.routes)]
        else:
            now = list(zip(self.sends, self.routes))[part::2]
            held = self.arrived if part else []
            self.arrived = held + [self.grid.far_shift(t, route) for t, route in now]

    def slices(self, i, extra):
        places = {**self.picked[i], **extra}
        parts = []
        for tensor, axes, row in self.held[i]:
            starts = [places.get(name, 0) for name in axes] + [row, 0]
            sizes = [1 if name in places else self.grid.size[name] for name in axes]
            part = lax.dynamic_slice(tensor, starts, sizes + [self.half, self.columns])
            left = [self.grid.size[name] for name in axes if name not in places]
            parts.append(part.reshape(*left, self.half, self.columns))
        return total(parts)

    def prepare(self):
        grid = self.grid
        if self.stage == 0:
            for i in range(2):
                self.held[i].append((self.arrived[0], "hxzy", i * self.half))
        else:
            for tensor, i in zip(self.arrived, self.owners):
                axes = "".join(name for name in "hxzy" if name not in self.picked[i])
                self.held[i].append((tensor, axes, 0))
        self.stage += 1
        if self.stage == 3:
            self.routes = [step for step in grid.far_steps() if step != (0, 0)]
            self.sends = [self.at_far(step).astype(BF) for step in self.routes]
            return
        self.sends, self.routes, self.owners = [], [], []
        for i, order in enumerate(("xy", "yx")):
            name = order[self.stage - 1]
            n, own = grid.size[name], grid.at[name]
            for k in range(1, n):
                self.sends.append(self.slices(i, {name: lax.rem(own + k, n)}).astype(BF))
                self.routes.append((name, k))
                self.owners.append(i)
            self.picked[i][name] = own

    def at_far(self, step):
        place = {
            name: lax.rem(self.grid.at[name] + k, self.grid.size[name]) for name, k in zip("hz", step)
        }
        return jnp.concatenate([self.slices(i, place) for i in range(2)], axis=0)

    def result(self):
        return total([self.at_far((0, 0))] + self.arrived)


def order(values, sent=(), got=()):
    values, sends, arrived = lax.optimization_barrier(
        (values, [s.sends for s in sent], [s.arrived for s in got])
    )
    for scatter, arrays in zip(sent, sends):
        scatter.sends = arrays
    for scatter, arrays in zip(got, arrived):
        scatter.arrived = arrays
    return values


def advance(values, scatters, begin=(), got=(), rest=()):
    values = order(values, [*begin, *rest], [*scatters, *got])
    for scatter in scatters:
        scatter.prepare()
    values = order(values, [*scatters, *begin, *rest])
    for scatter in (*begin, *scatters):
        scatter.go()
    for scatter in rest:
        scatter.go(1)
    return values


def sum_far(grid, tensor):
    arrived = [grid.far_shift(tensor, s) for s in grid.far_steps() if s != (0, 0)]
    return total([tensor] + arrived).astype(tensor.dtype)


def sum_near(grid, tensor, name):
    arrived = [grid.shift(tensor, name, k) for k in range(1, grid.size[name])]
    return total([tensor] + arrived).astype(tensor.dtype)


def body(
    sizes,
    inputs,
    segment_ids,
    key_mask,
    lead_index,
    cotangent_first,
    cotangent_second,
    w_qkv,
    w_out,
    w_up,
    w_down,
    biases,
    up_bias,
    norm_gains,
    norm_shifts,
    lead_table,
):
    grid = Grid(sizes)
    tokens, model = inputs.shape[1], inputs.shape[2]
    shards = grid.shards
    share = model // shards
    tie = lax.optimization_barrier

    rows_small = jnp.concatenate([biases, norm_gains, norm_shifts, lead_table])
    lengths = [t.shape[0] for t in (biases, norm_gains, norm_shifts, lead_table)]
    cuts = [sum(lengths[:i]) for i in range(5)]
    own_up = up_bias.shape[0]
    per_row = model // own_up
    shard_rows = w_qkv.shape[0]
    tiles = -(-(cuts[4] + 1) // shard_rows)

    def to_lanes(rows, width):
        lane = jnp.arange(LANES, dtype=jnp.int32)[None, :]
        begin = (grid.shard % (LANES // width)) * width
        spread = lane == begin + jnp.arange(width, dtype=jnp.int32)[:, None]
        return product(rows, spread.astype(BF)).astype(BF)

    def from_lanes(tensor, width):
        groups = tensor.reshape(-1, LANES // width, *tensor.shape[1:])
        return jnp.sum(groups.astype(F32), axis=1)

    block = jnp.concatenate([to_lanes(rows_small, share), to_lanes(up_bias[None, :], own_up)])
    block = jnp.pad(block, ((0, tiles * shard_rows - block.shape[0]), (0, 0)))
    block = block.reshape(tiles, shard_rows, LANES).transpose(1, 0, 2).reshape(shard_rows, -1)

    middle_up = w_up.shape[1] // 2
    one = Gather(
        grid, [jnp.concatenate([w_qkv, block], axis=1)], [w_qkv.shape[1], tiles * LANES]
    )
    two = Gather(
        grid,
        [w_up[:, :middle_up], jnp.concatenate([w_up[:, middle_up:], w_out], axis=1)],
        [w_up.shape[1], w_out.shape[1]],
    )
    three = Gather(grid, [w_down], [w_down.shape[1]])
    labels = jnp.concatenate(
        [segment_ids, key_mask, jnp.broadcast_to(lead_index.reshape(2, 1), (2, tokens))]
    )
    one.go_far(0)
    start_moved, labels_moved = grid.swapped(inputs[0]), grid.swapped(labels)
    one.far, labels_moved, start_moved = tie((one.far, labels_moved, start_moved))
    labels = grid.choose(labels, labels_moved)
    leads = (labels[2, 0], labels[3, 0])
    start_low = grid.choose(inputs[0], start_moved)
    own_pos = (grid.at["h"] * 2 + grid.at["c"]) * tokens + jnp.arange(tokens, dtype=jnp.int32)
    own_labels = jnp.stack([labels[0], labels[1], own_pos], axis=1)
    key_labels = jnp.concatenate(grid.mates(own_labels))
    own_labels_across, key_labels_across = own_labels.T, key_labels.T
    high = grid.size["h"]
    blocks = high * grid.size["x"] * grid.size["z"]

    one.make_lines()
    one.sends, two.chunks[0] = tie((one.sends, two.chunks[0]))
    one.go_first()
    two.go_far(0)
    one.arrived, two.far[0] = tie((one.arrived, two.far[0]))
    one.make_planes()
    one.sends, two.chunks[1] = tie((one.sends, two.chunks[1]))
    one.go_second()
    two.go_far(1)
    one.arrived, two.far[1] = tie((one.arrived, two.far[1]))
    one.go_pair_near()
    one.go_pair_far()
    two.make_lines()
    crossed = [t[0] for t in one.pairs]
    crossed, two.sends = tie((crossed, two.sends))
    one.pairs = [(t,) + pair[1:] for t, pair in zip(crossed, one.pairs)]
    two.go_first()
    weight_qkv, small = one.result()
    weights = {"qkv": weight_qkv}
    small = small.reshape(shards, shard_rows, -1)
    up_row, up_lanes = cuts[4] % shard_rows, cuts[4] // shard_rows * LANES
    bias_up = from_lanes(small[:, up_row, up_lanes : up_lanes + LANES][:, None], own_up)
    bias_up = bias_up.reshape(-1, model)
    small = from_lanes(small, share).reshape(-1, shard_rows, tiles, LANES)
    small = small.transpose(2, 1, 0, 3).reshape(tiles * shard_rows, model)
    bias_full, gains, shifts, lead_rows = (small[cuts[i] : cuts[i + 1]] for i in range(4))

    def before_exchange(values):
        values, two.arrived, three.chunks[0] = tie((values, two.arrived, three.chunks[0]))
        two.make_planes()
        values, two.sends, three.chunks[0] = tie((values, two.sends, three.chunks[0]))
        two.go_second()
        three.go_far(0)
        return values

    def after_attention(values):
        values, two.arrived, three.far[0] = tie((values, two.arrived, three.far[0]))
        two.go_pair_near()
        two.go_pair_far()
        three.make_lines()
        crossed = [t[0] for t in two.pairs]
        values, crossed, three.sends = tie((values, crossed, three.sends))
        two.pairs = [(t,) + pair[1:] for t, pair in zip(crossed, two.pairs)]
        three.go_first()
        placed = two.result()
        values, three.arrived, placed = tie((values, three.arrived, placed))
        three.make_planes()
        values, three.sends, placed = tie((values, three.sends, placed))
        weights["up"], weights["out"] = placed
        three.go_second()
        three.go_pair_near()
        return values

    def after_gate(values):
        values, three.arrived = tie((values, three.arrived))
        three.go_pair_far()
        (weights["down"],) = three.result()
        return values

    def keep(values):
        return values

    def forward(start_in, lead_id, hooks):
        chooser = (jnp.arange(lead_rows.shape[0], dtype=jnp.int32) == lead_id).astype(F32)
        lead_vec = jnp.sum(chooser[:, None] * lead_rows, axis=0)
        hidden = start_in + lead_vec[None, :]
        normed = layer_norm(hidden, gains[0], shifts[0]).astype(BF)
        mixed = product(normed, weights["qkv"])
        query = (mixed[:, :model] + bias_full[0]).astype(BF) * jnp.asarray(SCALE, BF)
        both_bias = jnp.concatenate([jnp.zeros((model,), F32), bias_full[1]])
        keys_values = (mixed[:, model:] + both_bias).astype(BF)
        query, keys_values = hooks[0]((query, keys_values))
        mates = grid.mates(keys_values)
        attn, attn_low, lse = attention_forward(query, mates, own_labels, key_labels_across)
        attn_low, lse = hooks[1]((attn_low, lse))
        middle = hidden + product(attn_low, weights["out"]) + bias_full[2]
        normed_mid = layer_norm(middle, gains[1], shifts[1]).astype(BF)
        normed_mid = hooks[2](normed_mid)
        activated, slope = gated(normed_mid, weights["up"], bias_up)
        activated, slope = hooks[3]((activated, slope))
        result = middle + product(activated, weights["down"]) + bias_full[3]
        saved = (
            hidden, normed, query, mates, lse, attn, attn_low, middle, normed_mid, slope, activated,
            chooser,
        )
        return (result, saved)

    def backward(saved, grad_res, earlier, hooks):
        (
            hidden, normed, query, mates, lse, attn, attn_low, middle, normed_mid, slope, activated,
            chooser,
        ) = saved
        last = earlier is not None
        operands, sums = {}, {}

        def start(name, **joined):
            operands.update(joined)
            if last:
                jobs = [
                    (
                        (joined[part][0], earlier[part][0]),
                        list(zip(joined[part][1], earlier[part][1])),
                    )
                    for part in joined
                ]
                sums[name] = Scatter(grid, *weight_terms(grid, jobs))

        def then(values, sent=(), got=()):
            if not last:
                return values
            values = order(values, [sums[name] for name in sent], [sums[name] for name in got])
            for name in sent:
                sums[name].go()
            return values

        def step(values, names, begin=(), got=(), rest=()):
            if not last:
                return values
            return advance(
                values, *([sums[name] for name in group] for group in (names, begin, got, rest))
            )

        grad_low = grad_res.astype(BF)
        start("down", down=(activated, [(grad_low, None)]))
        grad_low = then(grad_low, sent=["down"])
        bias_down = jnp.sum(grad_low.astype(F32), axis=0)
        grad_low = hooks[0](grad_low)
        grad_gate, bias_gate, grad_normed_mid = gated_backward(
            grad_low, slope, weights["down"], weights["up"]
        )
        grad_gate, grad_normed_mid = hooks[1]((grad_gate, grad_normed_mid))
        grad_gate, grad_normed_mid = step((grad_gate, grad_normed_mid), ["down"])
        mid_pull = jax.vjp(layer_norm, middle, gains[1], shifts[1])[1]
        grad_mid_part, gain_mid, shift_mid = mid_pull(grad_normed_mid)
        grad_mid = grad_res + grad_mid_part
        grad_branch = grad_mid.astype(BF)
        grad_attn = back_product(grad_branch, weights["out"]).astype(BF)
        bias_attn = jnp.sum(grad_branch.astype(F32), axis=0)
        start("up", up=(normed_mid, [(grad_gate, None)]), out=(attn_low, [(grad_branch, None)]))
        grad_attn = hooks[2](grad_attn)
        grad_attn = step(grad_attn, ["down"], begin=["up"])
        pairs = model // PAIR
        halves = (0, pairs // 2, pairs)

        def attend_back(half):
            first, count = halves[half], halves[half + 1] - halves[half]
            return attention_backward(
                query, mates, grad_attn, attn, lse, own_labels_across, key_labels, first, count
            )

        def add(near, far):
            both = total([near, far])
            if high > 1:
                both = lax.psum_scatter(both.astype(BF), "h", scatter_dimension=1, tiled=True)
            return both.astype(BF)

        def parts(query_low, both):
            return (normed, [(query_low, None), (both, 0), (both, 1)])

        query_low, near, sent = hooks[3](attend_back(0))
        query_low, near, sent, grad_attn = step((query_low, near, sent, grad_attn), ["down", "up"])
        far = grid.shift(sent, "c", 1)
        other_low, other_near, sent = attend_back(1)
        both = add(near, far)
        start("mix", qkv0=parts(query_low, both))
        other_low, other_near, sent, query_low, both = step(
            (other_low, other_near, sent, query_low, both),
            ["up"],
            begin=["mix"],
            got=["down"],
            rest=["down"],
        )
        far = grid.shift(sent, "c", 1)
        other_both = add(other_near, far)
        start("qkv1", qkv1=parts(other_low, other_both))
        query_low, both, other_low, other_both = step(
            (query_low, both, other_low, other_both), ["up", "mix"], begin=["qkv1"], got=["down"]
        )
        grad_mixed = jnp.concatenate(
            [query_low, other_low, both[0], other_both[0], both[1], other_both[1]], axis=1
        )
        grad_normed = back_product(grad_mixed, weights["qkv"])
        bias_query = jnp.sum(grad_mixed[:, :model].astype(F32), axis=0)
        bias_value = jnp.sum(grad_mixed[:, 2 * model :].astype(F32), axis=0)
        in_pull = jax.vjp(layer_norm, hidden, gains[0], shifts[0])[1]
        grad_in_part, gain_in, shift_in = in_pull(grad_normed)
        grad_start = grad_mid + grad_in_part
        grad_start = step(grad_start, ["mix", "qkv1"], got=["up"], rest=["up"])
        lead_sum = jnp.sum(grad_start, axis=0)
        vectors = jnp.concatenate(
            [
                jnp.stack([bias_query, bias_value, bias_attn, bias_down, gain_in, gain_mid, shift_in, shift_mid]),
                chooser[:, None] * lead_sum[None, :],
                bias_gate.reshape(blocks, -1, model // blocks).transpose(1, 0, 2).reshape(-1, model),
            ]
        )
        return (grad_start, operands, sums, vectors)

    result_first, saved_first = forward(
        start_low.astype(F32), leads[0], [before_exchange, after_attention, keep, after_gate]
    )
    first_low = result_first.astype(BF)
    first_low, seed_first, seed_second = tie((first_low, cotangent_first[0], cotangent_second[0]))
    moved = {"second": grid.swapped(seed_second)}

    def moves(begin, *names):
        def hook(values):
            values, taken = tie((values, {name: moved[name] for name in names}))
            moved.update(taken)
            if begin is None:
                return values
            values, sent = tie((values, begin[1]))
            moved[begin[0]] = grid.swapped(sent)
            return values

        return hook

    result_second, saved_second = forward(
        first_low.astype(F32),
        leads[1],
        [keep, moves(("first", seed_first), "second"), keep, moves(None, "first")],
    )
    second_low = result_second.astype(BF)
    seed_second = grid.choose(seed_second, moved["second"])
    seed_second, second_low = tie((seed_second, second_low))
    grad_between, operands, _, vectors_second = backward(
        saved_second,
        seed_second.astype(F32),
        None,
        [
            moves(("first_out", first_low)),
            moves(None, "first_out"),
            moves(("second_out", second_low)),
            moves(None, "second_out"),
        ],
    )
    seed_first = grid.choose(seed_first, moved["first"])
    first_low = grid.choose(first_low, moved["first_out"])
    second_low = grid.choose(second_low, moved["second_out"])
    grad_first, _, sums, vectors_first = backward(
        saved_first, seed_first.astype(F32) + grad_between, operands, [keep] * 4
    )
    vectors = vectors_second + vectors_first
    grad_low = grad_first.astype(BF)

    mix, qkv1, up = (sums[name] for name in ("mix", "qkv1", "up"))
    vectors, grad_low = advance((vectors, grad_low), [mix, qkv1], got=[up])
    mix.go(1)
    vectors = sum_near(grid, sum_near(grid, vectors, "c"), "y")
    vectors, grad_low = advance((vectors, grad_low), [qkv1])
    qkv1.go(1)
    grad_moved = grid.swapped(grad_low)
    vectors = sum_near(grid, vectors, "x")

    def block_at(step):
        place = {
            name: lax.rem(grid.at[name] + k, grid.size[name]) for name, k in zip("hz", step)
        }
        at = (place["h"] * grid.size["x"] + grid.at["x"]) * grid.size["z"] + place["z"]
        return lax.dynamic_slice_in_dim(vectors, at * (model // blocks), model // blocks, 1)

    vectors = total(
        [block_at((0, 0))]
        + [grid.far_shift(block_at(step), step) for step in grid.far_steps() if step != (0, 0)]
    )
    input_grad = grid.choose(grad_low, grad_moved).astype(F32)
    shares = {name: sums[name].result() for name in ("down", "up", "mix", "qkv1")}
    width = shares["qkv1"].shape[1] // 3
    sides = [shares["mix"], shares["qkv1"]]
    within = grid.at["y"] * 2 + grid.at["c"]
    own_columns = lax.dynamic_slice_in_dim(vectors, within * share, share, 1)
    small_out = [own_columns[cuts[i] : cuts[i + 1]] for i in range(4)]
    up_at = within * own_up
    up_width = model // blocks
    up_out = lax.dynamic_slice(
        vectors, (cuts[4] + up_at // up_width, up_at % up_width), (1, own_up)
    )[0]
    return (
        first_low[None],
        second_low[None],
        input_grad[None],
        jnp.concatenate([p[:, i * width : (i + 1) * width] for i in range(3) for p in sides], axis=1),
        shares["up"][:, w_up.shape[1] :],
        shares["up"][:, : w_up.shape[1]],
        shares["down"],
        small_out[0],
        up_out,
        small_out[1],
        small_out[2],
        small_out[3],
    )


def solution(mesh):
    dp, fsdp = mesh.shape["dp"], mesh.shape["fsdp"]
    tall = fsdp // 8
    sizes = {"h": dp // 2, "x": 2, "z": 4, "y": tall, "c": 2}
    fine = Mesh(np.asarray(mesh.devices).reshape(tuple(sizes.values())), tuple(sizes))
    one, two, every = ("z", "y", "c"), ("h", "x"), ("h", "x", "z", "y", "c")
    placed = (
        P(one, two, None),
        P(one, two),
        P(one, two),
        P(one, None),
        P(one, two, None),
        P(one, two, None),
        P(every, None),
        P(every, None),
        P(every, None),
        P(every, None),
        P(None, every),
        P(every),
        P(None, every),
        P(None, every),
        P(None, every),
    )
    return jax.shard_map(
        partial(body, sizes),
        mesh=fine,
        in_specs=placed,
        out_specs=(
            P(one, two, None),
            P(one, two, None),
            P(one, two, None),
            P(every, None),
            P(every, None),
            P(every, None),
            P(every, None),
            P(None, every),
            P(every),
            P(None, every),
            P(None, every),
            P(None, every),
        ),
        check_vma=False,
    )
```

```python
from functools import partial
import math

import jax
import jax.numpy as jnp
import numpy as np
from jax import lax
from jax.experimental import pallas as pl
from jax.experimental.pallas import tpu as pltpu
from jax.sharding import Mesh, PartitionSpec as P

HEAD = 64
PAIR = 2 * HEAD
LANES = 128
SCALE = 0.125
EPSILON = 1e-06
NEGATIVE = -1e30
ACROSS = (((0,), (0,)), ((), ()))
WITHIN = (((1,), (1,)), ((), ()))
BF = jnp.bfloat16
F32 = jnp.float32


def layer_norm(tensor, gain_row, shift_row):
    average = jnp.mean(tensor, axis=-1, keepdims=True)
    centred = tensor - average
    variance = jnp.mean(centred * centred, axis=-1, keepdims=True)
    return centred * lax.rsqrt(variance + EPSILON) * gain_row + shift_row


def product(left_side, right_side):
    return jnp.dot(left_side, right_side, preferred_element_type=F32)


def outer_sum(left_side, right_side):
    return lax.dot_general(left_side, right_side, ACROSS, preferred_element_type=F32)


def back_product(left_side, right_side):
    return lax.dot_general(left_side, right_side, WITHIN, preferred_element_type=F32)


def fill_bias(bias_ref, query_labels, key_labels):
    query_seg, _, query_pos = query_labels
    key_seg, key_open, key_pos = key_labels
    allowed = (key_seg == query_seg) & ((key_open == 1) | (key_pos == query_pos))
    bias_ref[...] = jnp.where(allowed, 0.0, NEGATIVE)


def columns_of(ref):
    return tuple(ref[:, i : i + 1] for i in range(3))


def rows_of(ref):
    return tuple(ref[i : i + 1, :] for i in range(3))


def half_lanes(tensor, side):
    lane = lax.broadcasted_iota(jnp.int32, tensor.shape, 1)
    return jnp.where((lane < HEAD) == (side == 0), tensor, jnp.zeros((), tensor.dtype))


def attention_forward(query, mates, query_labels, key_labels):
    tokens, model = query.shape
    part = mates[0].shape[0]
    every = 2 * part
    pairs = model // PAIR
    step = math.gcd(tokens, 512)

    def kernel(q_ref, k0_ref, k1_ref, v0_ref, v1_ref, ql_ref, kl_ref, attn_ref, low_ref, lse_ref, bias_ref):
        @pl.when(pl.program_id(0) == 0)
        def _():
            fill_bias(bias_ref, columns_of(ql_ref), rows_of(kl_ref))

        keys_pair = jnp.concatenate([k0_ref[...], k1_ref[...]], axis=0)
        values_pair = jnp.concatenate([v0_ref[...], v1_ref[...]], axis=0)
        for start in range(0, tokens, step):
            query_pair = q_ref[start : start + step, :]
            sides = []
            for side in range(2):
                logits = back_product(half_lanes(query_pair, side), keys_pair)
                logits = logits + bias_ref[start : start + step, :]
                highest = jnp.max(logits, axis=1, keepdims=True)
                weights = jnp.exp(logits - highest)
                denominator = jnp.sum(weights, axis=1, keepdims=True)
                across = jnp.broadcast_to(highest + jnp.log(denominator), (step, PAIR)).T
                lse_ref[0, side : side + 1, start : start + step] = across[0:1]
                sides.append(product(weights.astype(BF), values_pair) / denominator)
            lane = lax.broadcasted_iota(jnp.int32, (step, PAIR), 1)
            both = jnp.where(lane < HEAD, sides[0], sides[1])
            attn_ref[start : start + step, :] = both
            low_ref[start : start + step, :] = both.astype(BF)

    work = 2 * tokens * every * model
    keys_at = pl.BlockSpec((part, PAIR), lambda i: (0, i))
    values_at = pl.BlockSpec((part, PAIR), lambda i: (0, i + pairs))
    return pl.pallas_call(
        kernel,
        grid=(pairs,),
        in_specs=[
            pl.BlockSpec((tokens, PAIR), lambda i: (0, i)),
            keys_at,
            keys_at,
            values_at,
            values_at,
            pl.BlockSpec(query_labels.shape, lambda i: (0, 0)),
            pl.BlockSpec(key_labels.shape, lambda i: (0, 0)),
        ],
        out_specs=[
            pl.BlockSpec((tokens, PAIR), lambda i: (0, i)),
            pl.BlockSpec((tokens, PAIR), lambda i: (0, i)),
            pl.BlockSpec((1, 2, tokens), lambda i: (i, 0, 0)),
        ],
        out_shape=[
            jax.ShapeDtypeStruct((tokens, model), F32),
            jax.ShapeDtypeStruct((tokens, model), BF),
            jax.ShapeDtypeStruct((pairs, 2, tokens), F32),
        ],
        scratch_shapes=[pltpu.VMEM((tokens, every), F32)],
        compiler_params=pltpu.CompilerParams(
            dimension_semantics=("arbitrary",), vmem_limit_bytes=60 << 20
        ),
        cost_estimate=pl.CostEstimate(
            flops=2 * work, transcendentals=work // PAIR, bytes_accessed=10 * every * model
        ),
        name="attention_forward",
    )(query, *mates, *mates, query_labels, key_labels)


def attention_backward(query, mates, grad, attn, lse, query_labels, key_labels, first, pairs):
    tokens = query.shape[0]
    part = mates[0].shape[0]
    every, total_pairs = 2 * part, query.shape[1] // PAIR
    model = pairs * PAIR
    step = math.gcd(part, 512)

    def kernel(q_ref, k0_ref, k1_ref, v0_ref, v1_ref, g_ref, a_ref, lse_ref, ql_ref, kl_ref,
               dq_ref, d0_ref, d1_ref, bias_ref):
        @pl.when(pl.program_id(0) == 0)
        def _():
            fill_bias(bias_ref, rows_of(ql_ref), columns_of(kl_ref))

        query_pair, grad_pair = q_ref[...], g_ref[...]
        overlap = (grad_pair.astype(F32) * a_ref[...]).T
        deltas = [
            jnp.sum(overlap[side * HEAD : (side + 1) * HEAD], axis=0, keepdims=True)
            for side in range(2)
        ]
        query_sides = [half_lanes(query_pair, side) for side in range(2)]
        grad_sides = [half_lanes(grad_pair, side) for side in range(2)]
        grad_query = [jnp.zeros((HEAD, tokens), F32), jnp.zeros((HEAD, tokens), F32)]
        for mate, (k_ref, v_ref, d_ref) in enumerate(((k0_ref, v0_ref, d0_ref), (k1_ref, v1_ref, d1_ref))):
            keys_across = k_ref[...].astype(F32).T.astype(BF)
            for start in range(0, part, step):
                rows = slice(start, start + step)
                grad_keys, grad_values = [], []
                for side in range(2):
                    logits = back_product(k_ref[rows, :], query_sides[side])
                    logits = logits + bias_ref[mate * part + start : mate * part + start + step, :]
                    probs = jnp.exp(logits - lse_ref[0, side : side + 1, :])
                    grad_probs = back_product(v_ref[rows, :], grad_sides[side])
                    grad_logits = (probs * (grad_probs - deltas[side])).astype(BF)
                    grad_values.append(product(probs.astype(BF), grad_sides[side]))
                    grad_keys.append(product(grad_logits, query_sides[side]))
                    grad_query[side] = grad_query[side] + product(
                        keys_across[side * HEAD : (side + 1) * HEAD, rows], grad_logits
                    )
                d_ref[0, rows, :] = (grad_keys[0] + grad_keys[1]).astype(BF)
                d_ref[1, rows, :] = (grad_values[0] + grad_values[1]).astype(BF)
        dq_ref[...] = (jnp.concatenate(grad_query, axis=0).T * SCALE).astype(BF)

    work = 2 * tokens * every * model
    own = pl.BlockSpec((tokens, PAIR), lambda i: (0, i + first))
    keys_at = pl.BlockSpec((part, PAIR), lambda i: (0, i + first))
    values_at = pl.BlockSpec((part, PAIR), lambda i: (0, i + first + total_pairs))
    mate_out = pl.BlockSpec((2, part, PAIR), lambda i: (0, 0, i))
    return pl.pallas_call(
        kernel,
        grid=(pairs,),
        in_specs=[
            own,
            keys_at,
            keys_at,
            values_at,
            values_at,
            own,
            own,
            pl.BlockSpec((1, 2, tokens), lambda i: (i + first, 0, 0)),
            pl.BlockSpec(query_labels.shape, lambda i: (0, 0)),
            pl.BlockSpec(key_labels.shape, lambda i: (0, 0)),
        ],
        out_specs=[pl.BlockSpec((tokens, PAIR), lambda i: (0, i)), mate_out, mate_out],
        out_shape=[
            jax.ShapeDtypeStruct((tokens, model), BF),
            jax.ShapeDtypeStruct((2, part, model), BF),
            jax.ShapeDtypeStruct((2, part, model), BF),
        ],
        scratch_shapes=[pltpu.VMEM((every, tokens), F32)],
        compiler_params=pltpu.CompilerParams(
            dimension_semantics=("arbitrary",), vmem_limit_bytes=60 << 20
        ),
        cost_estimate=pl.CostEstimate(
            flops=5 * work, transcendentals=work // PAIR, bytes_accessed=12 * every * model
        ),
        name="attention_backward",
    )(query, *mates, *mates, grad, attn, lse, query_labels, key_labels)


def gated(normed, weight, bias_rows):
    tokens, model = normed.shape
    hidden_units = weight.shape[1]
    width = math.gcd(bias_rows.shape[1], 512)
    per_row = bias_rows.shape[1] // width
    rows = math.gcd(tokens, 256)
    bias = bias_rows.reshape(-1, 1, width)

    def kernel(x_ref, w_ref, b_ref, act_ref, slope_ref):
        for start in range(0, tokens, rows):
            gate = jnp.dot(
                x_ref[start : start + rows, :], w_ref[...], preferred_element_type=F32
            ) + b_ref[0]
            share = 0.5 + 0.5 * lax.erf(gate * math.sqrt(0.5))
            density = jnp.exp(gate * gate * -0.5) * (1.0 / math.sqrt(2.0 * math.pi))
            act_ref[start : start + rows, :] = (gate * share).astype(BF)
            slope_ref[start : start + rows, :] = (share + gate * density).astype(BF)

    block = pl.BlockSpec((tokens, width), lambda i: (0, i))
    return pl.pallas_call(
        kernel,
        grid=(hidden_units // width,),
        in_specs=[
            pl.BlockSpec((tokens, model), lambda i: (0, 0)),
            pl.BlockSpec((model, width), lambda i: (0, i)),
            pl.BlockSpec((1, 1, width), lambda i: (i, 0, 0)),
        ],
        out_specs=[block, block],
        out_shape=[jax.ShapeDtypeStruct((tokens, hidden_units), BF)] * 2,
        compiler_params=pltpu.CompilerParams(
            dimension_semantics=("arbitrary",), vmem_limit_bytes=40 << 20
        ),
        cost_estimate=pl.CostEstimate(
            flops=2 * tokens * model * hidden_units,
            transcendentals=2 * tokens * hidden_units,
            bytes_accessed=2 * (model + 2 * tokens) * hidden_units,
        ),
        name="gated",
    )(normed, weight, bias)


def gated_backward(grad_low, slope, weight_down, weight_up):
    tokens, model = grad_low.shape
    hidden_units = slope.shape[1]
    width = math.gcd(hidden_units, 1024)
    steps = hidden_units // width
    rows = math.gcd(tokens, 256)

    def kernel(g_ref, s_ref, down_ref, up_ref, gate_ref, bias_ref, out_ref, acc_ref):
        @pl.when(pl.program_id(0) == 0)
        def _():
            acc_ref[...] = jnp.zeros_like(acc_ref)

        column = jnp.zeros((1, width), F32)
        for start in range(0, tokens, rows):
            cut = slice(start, start + rows)
            pulled = back_product(g_ref[cut, :], down_ref[...]) * s_ref[cut, :].astype(F32)
            low = pulled.astype(BF)
            gate_ref[cut, :] = low
            column = column + jnp.sum(low.astype(F32), axis=0, keepdims=True)
            acc_ref[cut, :] += back_product(low, up_ref[...])
        bias_ref[0] = column

        @pl.when(pl.program_id(0) == steps - 1)
        def _():
            out_ref[...] = acc_ref[...]

    return pl.pallas_call(
        kernel,
        grid=(steps,),
        in_specs=[
            pl.BlockSpec((tokens, model), lambda i: (0, 0)),
            pl.BlockSpec((tokens, width), lambda i: (0, i)),
            pl.BlockSpec((width, model), lambda i: (i, 0)),
            pl.BlockSpec((model, width), lambda i: (0, i)),
        ],
        out_specs=[
            pl.BlockSpec((tokens, width), lambda i: (0, i)),
            pl.BlockSpec((1, 1, width), lambda i: (i, 0, 0)),
            pl.BlockSpec((tokens, model), lambda i: (0, 0)),
        ],
        out_shape=[
            jax.ShapeDtypeStruct((tokens, hidden_units), BF),
            jax.ShapeDtypeStruct((steps, 1, width), F32),
            jax.ShapeDtypeStruct((tokens, model), F32),
        ],
        scratch_shapes=[pltpu.VMEM((tokens, model), F32)],
        compiler_params=pltpu.CompilerParams(
            dimension_semantics=("arbitrary",), vmem_limit_bytes=40 << 20
        ),
        cost_estimate=pl.CostEstimate(
            flops=4 * tokens * model * hidden_units,
            transcendentals=0,
            bytes_accessed=4 * (model + tokens) * hidden_units,
        ),
        name="gated_backward",
    )(grad_low, slope, weight_down, weight_up)


def weight_terms(grid, jobs):
    tokens, height = jobs[0][0][0].shape
    shards = grid.shards
    rows = height // shards
    widths = [part[0][0].shape[-1] for _, parts in jobs for part in parts]
    columns = sum(widths)
    if rows % 16:
        acc = jnp.concatenate(
            [
                sum(
                    outer_sum(left, right if at is None else right[at])
                    for left, (right, at) in zip(lefts, part)
                )
                for lefts, parts in jobs
                for part in parts
            ],
            axis=1,
        )
        acc = acc.astype(BF).reshape(shards // 2, 2, rows, columns)
        return tuple(pick(acc, lax.rem(grid.at["c"] + k, 2), 1) for k in range(2))
    lefts = [left for job in jobs for left in job[0]]
    rights = [right for _, parts in jobs for part in parts for right in part]
    depth = len(jobs[0][0])
    left_of = [job for job, (_, parts) in enumerate(jobs) for _ in parts]
    block = 1024 if height > 1024 else 256
    pairs = block // (2 * rows)

    def kernel(at_ref, *refs):
        left_refs, right_refs = refs[: len(lefts)], refs[len(lefts) : len(lefts) + len(rights)]
        kept_ref, sent_ref = refs[len(lefts) + len(rights) :]
        upper = at_ref[4] == 1
        begin = 0
        for part, width in enumerate(widths):
            chunk = math.gcd(width, 1024)
            job = left_of[part]
            for start in range(0, width, chunk):
                acc = None
                for k in range(depth):
                    more = outer_sum(
                        left_refs[job * depth + k][...],
                        right_refs[part * depth + k][:, start : start + chunk],
                    )
                    acc = more if acc is None else acc + more
                acc = acc.reshape(pairs, 2, rows, chunk)
                at = slice(begin + start, begin + start + chunk)
                kept_ref[:, :, at] = jnp.where(upper, acc[:, 1], acc[:, 0]).astype(BF)
                sent_ref[:, :, at] = jnp.where(upper, acc[:, 0], acc[:, 1]).astype(BF)
            begin += width

    def whole(right, at):
        if at is None:
            return pl.BlockSpec(right.shape, lambda i: (0, 0), pipeline_mode=pl.Buffered(1))
        return pl.BlockSpec(
            (None,) + right.shape[1:], lambda i: (at, 0, 0), pipeline_mode=pl.Buffered(1)
        )

    out = pl.BlockSpec((pairs, rows, columns), lambda i: (i, 0, 0))
    return pl.pallas_call(
        kernel,
        grid=(height // block,),
        in_specs=[pl.BlockSpec(memory_space=pltpu.SMEM)]
        + [pl.BlockSpec((tokens, block), lambda i: (0, i))] * len(lefts)
        + [whole(*right) for right in rights],
        out_specs=[out, out],
        out_shape=[jax.ShapeDtypeStruct((shards // 2, rows, columns), BF)] * 2,
        compiler_params=pltpu.CompilerParams(
            dimension_semantics=("arbitrary",), vmem_limit_bytes=(60 if height > 1024 else 48) << 20
        ),
        cost_estimate=pl.CostEstimate(
            flops=2 * depth * tokens * height * columns,
            transcendentals=0,
            bytes_accessed=2 * height * columns + 2 * depth * tokens * (height + columns),
        ),
        name="weight_terms",
    )(grid.places, *lefts, *(right for right, _ in rights))


class Grid:
    def __init__(self, sizes):
        self.size = dict(sizes)
        self.at = {name: lax.axis_index(name) for name in sizes}
        self.places = jnp.stack([self.at[name] for name in sizes]).astype(jnp.int32)
        self.shards = math.prod(sizes.values())
        index = 0
        for name in sizes:
            index = index * sizes[name] + self.at[name]
        self.shard = index

    def shift(self, tensor, axis, step):
        n = self.size[axis]
        return lax.ppermute(tensor, axis, [(i, (i + step) % n) for i in range(n)])

    def far_steps(self):
        return [(a, b) for a in range(self.size["h"]) for b in range(self.size["z"])]

    def far_shift(self, tensor, step):
        high, deep = self.size["h"], self.size["z"]
        pairs = [
            (a * deep + b, ((a + step[0]) % high) * deep + (b + step[1]) % deep)
            for a in range(high)
            for b in range(deep)
        ]
        return lax.ppermute(tensor, ("h", "z"), pairs)

    def swapped(self, tensor):
        return lax.ppermute(tensor, ("x", "c"), [(1, 2), (2, 1)])

    def choose(self, tensor, moved):
        return jnp.where(self.at["x"] == self.at["c"], tensor, moved)

    def mates(self, tensor):
        if self.size["h"] > 1:
            tensor = lax.all_gather(tensor, "h", axis=0, tiled=True)
        return tensor, self.shift(tensor, "c", 1)


def place(places, pieces, out_shapes, moves, room=None):
    count = len(pieces)
    landed = [pltpu.VMEM(piece.shape, piece.dtype) for piece in pieces]

    def kernel(at_ref, *refs):
        ins, outs = refs[:count], refs[count : count + len(out_shapes)]
        held, load_sems, store_sems = refs[-2 - count : -2], refs[-2], refs[-1]
        loads = [
            pltpu.make_async_copy(source, target, load_sems.at[i])
            for i, (source, target) in enumerate(zip(ins, held))
        ]
        for load in loads:
            load.start()
        stores = []
        ready = -1
        for piece, source, target in moves(at_ref, held, outs):
            while ready < piece:
                ready += 1
                loads[ready].wait()
            store = pltpu.make_async_copy(source, target, store_sems.at[len(stores)])
            store.start()
            stores.append(store)
        for store in stores:
            store.wait()

    moved = sum(math.prod(s.shape) * 2 for s in out_shapes)
    return pl.pallas_call(
        kernel,
        out_shape=out_shapes,
        in_specs=[pl.BlockSpec(memory_space=pltpu.SMEM)]
        + [pl.BlockSpec(memory_space=pl.ANY)] * count,
        out_specs=[pl.BlockSpec(memory_space=pl.ANY)] * len(out_shapes),
        scratch_shapes=landed
        + [pltpu.SemaphoreType.DMA((count,)), pltpu.SemaphoreType.DMA((8 * count,))],
        compiler_params=pltpu.CompilerParams(vmem_limit_bytes=room or moved + (4 << 20)),
        cost_estimate=pl.CostEstimate(flops=0, transcendentals=0, bytes_accessed=2 * moved),
        name="place",
    )(places, *pieces)


class Gather:
    def __init__(self, grid, chunks, widths):
        self.grid, self.widths = grid, widths
        self.chunks = list(chunks)
        self.half = chunks[0].shape[0] // 2
        self.columns = sum(chunk.shape[1] for chunk in chunks)
        self.kind = chunks[0].dtype
        self.far = [None] * len(chunks)
        self.roomy = len(widths) > 1 or len(chunks) > 1

    def new(self, *lead):
        return jax.ShapeDtypeStruct((*lead, self.half, self.columns), self.kind)

    def go_far(self, i):
        self.far[i] = [self.grid.far_shift(self.chunks[i], step) for step in self.grid.far_steps()[1:]]

    def make_lines(self):
        high, deep = self.grid.size["h"], self.grid.size["z"]
        steps, half = self.grid.far_steps(), self.half

        widths = [chunk.shape[1] for chunk in self.chunks]
        pieces = [
            (tensor, step, sum(widths[:i]), widths[i])
            for i, chunk in enumerate(self.chunks)
            for tensor, step in zip([chunk] + self.far[i], steps)
        ]

        def moves(at, ins, outs):
            listed = []
            for i, (ref, (_, step, offset, width)) in enumerate(zip(ins, pieces)):
                a = lax.rem(at[0] - step[0] + high, high)
                b = lax.rem(at[2] - step[1] + deep, deep)
                for colour in range(2):
                    listed.append(
                        (
                            i,
                            ref.at[pl.ds(colour * half, half)],
                            outs[colour].at[a, b, :, pl.ds(offset, width)],
                        )
                    )
            return listed

        self.sends = place(
            self.grid.places,
            [p[0] for p in pieces],
            [self.new(high, deep)] * 2,
            moves,
            (60 << 20) if self.roomy else None,
        )

    def go_first(self):
        self.own = self.sends
        self.arrived = [
            self.grid.shift(t, name, k)
            for t, name in zip(self.sends, "xy")
            for k in range(1, self.grid.size[name])
        ]

    def make_planes(self):
        high, wide, deep, tall = (self.grid.size[name] for name in "hxzy")
        spots = [(0, 0), (1, 0)] + [(0, k) for k in range(1, wide)] + [(1, k) for k in range(1, tall)]

        def moves(at, ins, outs):
            return [(i, ref, outs[c].at[k]) for i, (ref, (c, k)) in enumerate(zip(ins, spots))]

        self.sends = place(
            self.grid.places,
            list(self.own) + self.arrived,
            [self.new(wide, high, deep), self.new(tall, high, deep)],
            moves,
        )

    def go_second(self):
        self.near = [(self.sends[0], 0, 0), (self.sends[1], 1, 0)]
        self.arrived = [
            self.grid.shift(t, name, k)
            for t, name in zip(self.sends, "yx")
            for k in range(1, self.grid.size[name])
        ]

    def go_pair_near(self):
        self.pairs = [(self.grid.shift(t, "c", 1), colour, k) for t, colour, k in self.near]

    def go_pair_far(self):
        counts = [(c, k) for c, name in enumerate("yx") for k in range(1, self.grid.size[name])]
        distant = [(t, c, k) for t, (c, k) in zip(self.arrived, counts)]
        self.near += distant
        self.pairs += [(self.grid.shift(t, "c", 1), colour, k) for t, colour, k in distant]

    def result(self):
        high, wide, deep, tall = (self.grid.size[name] for name in "hxzy")
        half, widths = self.half, self.widths
        pieces = [t + (0,) for t in self.near] + [t + (1,) for t in self.pairs]
        offsets = [sum(widths[:i]) for i in range(len(widths))]

        def moves(at, ins, outs):
            listed = []
            for i, (ref, (_, colour, far, kc)) in enumerate(zip(ins, pieces)):
                pc = lax.rem(at[4] + kc, 2)
                for k in range(wide if colour == 0 else tall):
                    kx, ky = (k, far) if colour == 0 else (far, k)
                    px = lax.rem(at[1] - kx + wide, wide)
                    py = lax.rem(at[3] - ky + tall, tall)
                    for out, offset, width in zip(outs, offsets, widths):
                        listed.append(
                            (
                                i,
                                ref.at[k, :, :, :, pl.ds(offset, width)],
                                out.at[:, px, :, py, pc, pl.ds(colour * half, half)],
                            )
                        )
            return listed

        full = place(
            self.grid.places,
            [t[0] for t in pieces],
            [
                jax.ShapeDtypeStruct((high, wide, deep, tall, 2, 2 * half, width), self.kind)
                for width in widths
            ],
            moves,
        )
        return [t.reshape(-1, width) for t, width in zip(full, widths)]


def pick(tensor, index, axis):
    return lax.dynamic_index_in_dim(tensor, index, axis, keepdims=False)


def total(parts):
    result = parts[0].astype(F32)
    for part in parts[1:]:
        result = result + part.astype(F32)
    return result


def tie(*groups):
    return lax.optimization_barrier(groups)


class Scatter:
    def __init__(self, grid, kept, sent):
        self.grid = grid
        sizes = [grid.size[name] for name in "hxzy"]
        self.rows, self.columns = kept.shape[1:]
        self.half = self.rows // 2
        kept = kept.reshape(*sizes, self.rows, self.columns)
        self.held = [[(kept, "hxzy", i * self.half)] for i in range(2)]
        self.picked = [{}, {}]
        self.sends = [sent.reshape(*sizes, self.rows, self.columns)]
        self.stage = 0

    def go(self, part=0):
        if self.stage == 0:
            self.arrived = [self.grid.shift(self.sends[0], "c", 1)]
        elif self.stage < 3:
            self.arrived = [self.grid.shift(t, *route) for t, route in zip(self.sends, self.routes)]
        else:
            now = list(zip(self.sends, self.routes))[part::2]
            held = self.arrived if part else []
            self.arrived = held + [self.grid.far_shift(t, route) for t, route in now]

    def slices(self, i, extra):
        places = {**self.picked[i], **extra}
        parts = []
        for tensor, axes, row in self.held[i]:
            starts = [places.get(name, 0) for name in axes] + [row, 0]
            sizes = [1 if name in places else self.grid.size[name] for name in axes]
            part = lax.dynamic_slice(tensor, starts, sizes + [self.half, self.columns])
            left = [self.grid.size[name] for name in axes if name not in places]
            parts.append(part.reshape(*left, self.half, self.columns))
        return total(parts)

    def prepare(self):
        grid = self.grid
        if self.stage == 0:
            for i in range(2):
                self.held[i].append((self.arrived[0], "hxzy", i * self.half))
        else:
            for tensor, i in zip(self.arrived, self.owners):
                axes = "".join(name for name in "hxzy" if name not in self.picked[i])
                self.held[i].append((tensor, axes, 0))
        self.stage += 1
        if self.stage == 3:
            self.routes = [step for step in grid.far_steps() if step != (0, 0)]
            self.sends = [self.at_far(step).astype(BF) for step in self.routes]
            return
        self.sends, self.routes, self.owners = [], [], []
        for i, order in enumerate(("xy", "yx")):
            name = order[self.stage - 1]
            n, own = grid.size[name], grid.at[name]
            for k in range(1, n):
                self.sends.append(self.slices(i, {name: lax.rem(own + k, n)}).astype(BF))
                self.routes.append((name, k))
                self.owners.append(i)
            self.picked[i][name] = own

    def at_far(self, step):
        place = {
            name: lax.rem(self.grid.at[name] + k, self.grid.size[name]) for name, k in zip("hz", step)
        }
        return jnp.concatenate([self.slices(i, place) for i in range(2)], axis=0)

    def result(self):
        return total([self.at_far((0, 0))] + self.arrived)


def order(values, sent=(), got=()):
    values, sends, arrived = lax.optimization_barrier(
        (values, [s.sends for s in sent], [s.arrived for s in got])
    )
    for scatter, arrays in zip(sent, sends):
        scatter.sends = arrays
    for scatter, arrays in zip(got, arrived):
        scatter.arrived = arrays
    return values


def advance(values, scatters, begin=(), got=(), rest=()):
    values = order(values, [*begin, *rest], [*scatters, *got])
    for scatter in scatters:
        scatter.prepare()
    values = order(values, [*scatters, *begin, *rest])
    for scatter in (*begin, *scatters):
        scatter.go()
    for scatter in rest:
        scatter.go(1)
    return values


def sum_far(grid, tensor):
    arrived = [grid.far_shift(tensor, s) for s in grid.far_steps() if s != (0, 0)]
    return total([tensor] + arrived).astype(tensor.dtype)


def sum_near(grid, tensor, name):
    arrived = [grid.shift(tensor, name, k) for k in range(1, grid.size[name])]
    return total([tensor] + arrived).astype(tensor.dtype)


def body(
    sizes,
    inputs,
    segment_ids,
    key_mask,
    lead_index,
    cotangent_first,
    cotangent_second,
    w_qkv,
    w_out,
    w_up,
    w_down,
    biases,
    up_bias,
    norm_gains,
    norm_shifts,
    lead_table,
):
    grid = Grid(sizes)
    tokens, model = inputs.shape[1], inputs.shape[2]
    shards = grid.shards
    share = model // shards
    tie = lax.optimization_barrier

    rows_small = jnp.concatenate([biases, norm_gains, norm_shifts, lead_table])
    lengths = [t.shape[0] for t in (biases, norm_gains, norm_shifts, lead_table)]
    cuts = [sum(lengths[:i]) for i in range(5)]
    own_up = up_bias.shape[0]
    per_row = model // own_up
    shard_rows = w_qkv.shape[0]
    tiles = -(-(cuts[4] + 1) // shard_rows)

    def to_lanes(rows, width):
        lane = jnp.arange(LANES, dtype=jnp.int32)[None, :]
        begin = (grid.shard % (LANES // width)) * width
        spread = lane == begin + jnp.arange(width, dtype=jnp.int32)[:, None]
        return product(rows, spread.astype(BF)).astype(BF)

    def from_lanes(tensor, width):
        groups = tensor.reshape(-1, LANES // width, *tensor.shape[1:])
        return jnp.sum(groups.astype(F32), axis=1)

    block = jnp.concatenate([to_lanes(rows_small, share), to_lanes(up_bias[None, :], own_up)])
    block = jnp.pad(block, ((0, tiles * shard_rows - block.shape[0]), (0, 0)))
    block = block.reshape(tiles, shard_rows, LANES).transpose(1, 0, 2).reshape(shard_rows, -1)

    middle_up = w_up.shape[1] // 2
    one = Gather(
        grid, [jnp.concatenate([w_qkv, block], axis=1)], [w_qkv.shape[1], tiles * LANES]
    )
    two = Gather(
        grid,
        [w_up[:, :middle_up], jnp.concatenate([w_up[:, middle_up:], w_out], axis=1)],
        [w_up.shape[1], w_out.shape[1]],
    )
    three = Gather(grid, [w_down], [w_down.shape[1]])
    labels = jnp.concatenate(
        [segment_ids, key_mask, jnp.broadcast_to(lead_index.reshape(2, 1), (2, tokens))]
    )
    one.go_far(0)
    start_moved, labels_moved = grid.swapped(inputs[0]), grid.swapped(labels)
    one.far, labels_moved, start_moved = tie((one.far, labels_moved, start_moved))
    labels = grid.choose(labels, labels_moved)
    leads = (labels[2, 0], labels[3, 0])
    start_low = grid.choose(inputs[0], start_moved)
    own_pos = (grid.at["h"] * 2 + grid.at["c"]) * tokens + jnp.arange(tokens, dtype=jnp.int32)
    own_labels = jnp.stack([labels[0], labels[1], own_pos], axis=1)
    key_labels = jnp.concatenate(grid.mates(own_labels))
    own_labels_across, key_labels_across = own_labels.T, key_labels.T
    high = grid.size["h"]
    blocks = high * grid.size["x"] * grid.size["z"]

    one.make_lines()
    one.sends, two.chunks[0] = tie((one.sends, two.chunks[0]))
    one.go_first()
    two.go_far(0)
    one.arrived, two.far[0] = tie((one.arrived, two.far[0]))
    one.make_planes()
    one.sends, two.chunks[1] = tie((one.sends, two.chunks[1]))
    one.go_second()
    two.go_far(1)
    one.arrived, two.far[1] = tie((one.arrived, two.far[1]))
    one.go_pair_near()
    one.go_pair_far()
    two.make_lines()
    crossed = [t[0] for t in one.pairs]
    crossed, two.sends = tie((crossed, two.sends))
    one.pairs = [(t,) + pair[1:] for t, pair in zip(crossed, one.pairs)]
    two.go_first()
    weight_qkv, small = one.result()
    weights = {"qkv": weight_qkv}
    small = small.reshape(shards, shard_rows, -1)
    up_row, up_lanes = cuts[4] % shard_rows, cuts[4] // shard_rows * LANES
    bias_up = from_lanes(small[:, up_row, up_lanes : up_lanes + LANES][:, None], own_up)
    bias_up = bias_up.reshape(-1, model)
    small = from_lanes(small, share).reshape(-1, shard_rows, tiles, LANES)
    small = small.transpose(2, 1, 0, 3).reshape(tiles * shard_rows, model)
    bias_full, gains, shifts, lead_rows = (small[cuts[i] : cuts[i + 1]] for i in range(4))

    def before_exchange(values):
        values, two.arrived, three.chunks[0] = tie((values, two.arrived, three.chunks[0]))
        two.make_planes()
        values, two.sends, three.chunks[0] = tie((values, two.sends, three.chunks[0]))
        two.go_second()
        three.go_far(0)
        return values

    def after_attention(values):
        values, two.arrived, three.far[0] = tie((values, two.arrived, three.far[0]))
        two.go_pair_near()
        two.go_pair_far()
        three.make_lines()
        values, three.sends = tie((values, three.sends))
        three.go_first()
        placed = two.result()
        values, three.arrived, placed = tie((values, three.arrived, placed))
        three.make_planes()
        values, three.sends, placed = tie((values, three.sends, placed))
        weights["up"], weights["out"] = placed
        three.go_second()
        three.go_pair_near()
        return values

    def after_gate(values):
        values, three.arrived = tie((values, three.arrived))
        three.go_pair_far()
        (weights["down"],) = three.result()
        return values

    def keep(values):
        return values

    def forward(start_in, lead_id, hooks):
        chooser = (jnp.arange(lead_rows.shape[0], dtype=jnp.int32) == lead_id).astype(F32)
        lead_vec = jnp.sum(chooser[:, None] * lead_rows, axis=0)
        hidden = start_in + lead_vec[None, :]
        normed = layer_norm(hidden, gains[0], shifts[0]).astype(BF)
        mixed = product(normed, weights["qkv"])
        query = (mixed[:, :model] + bias_full[0]).astype(BF) * jnp.asarray(SCALE, BF)
        both_bias = jnp.concatenate([jnp.zeros((model,), F32), bias_full[1]])
        keys_values = (mixed[:, model:] + both_bias).astype(BF)
        query, keys_values = hooks[0]((query, keys_values))
        mates = grid.mates(keys_values)
        attn, attn_low, lse = attention_forward(query, mates, own_labels, key_labels_across)
        attn_low, lse = hooks[1]((attn_low, lse))
        middle = hidden + product(attn_low, weights["out"]) + bias_full[2]
        normed_mid = layer_norm(middle, gains[1], shifts[1]).astype(BF)
        normed_mid = hooks[2](normed_mid)
        activated, slope = gated(normed_mid, weights["up"], bias_up)
        activated, slope = hooks[3]((activated, slope))
        result = middle + product(activated, weights["down"]) + bias_full[3]
        saved = (
            hidden, normed, query, mates, lse, attn, attn_low, middle, normed_mid, slope, activated,
            chooser,
        )
        return (result, saved)

    def backward(saved, grad_res, earlier, hooks):
        (
            hidden, normed, query, mates, lse, attn, attn_low, middle, normed_mid, slope, activated,
            chooser,
        ) = saved
        last = earlier is not None
        operands, sums = {}, {}

        def start(name, **joined):
            operands.update(joined)
            if last:
                jobs = [
                    (
                        (joined[part][0], earlier[part][0]),
                        list(zip(joined[part][1], earlier[part][1])),
                    )
                    for part in joined
                ]
                sums[name] = Scatter(grid, *weight_terms(grid, jobs))

        def then(values, sent=(), got=()):
            if not last:
                return values
            values = order(values, [sums[name] for name in sent], [sums[name] for name in got])
            for name in sent:
                sums[name].go()
            return values

        def step(values, names, begin=(), got=(), rest=()):
            if not last:
                return values
            return advance(
                values, *([sums[name] for name in group] for group in (names, begin, got, rest))
            )

        grad_low = grad_res.astype(BF)
        start("down", down=(activated, [(grad_low, None)]))
        grad_low = then(grad_low, sent=["down"])
        bias_down = jnp.sum(grad_low.astype(F32), axis=0)
        grad_low = hooks[0](grad_low)
        grad_gate, bias_gate, grad_normed_mid = gated_backward(
            grad_low, slope, weights["down"], weights["up"]
        )
        grad_gate, grad_normed_mid = hooks[1]((grad_gate, grad_normed_mid))
        grad_gate, grad_normed_mid = step((grad_gate, grad_normed_mid), ["down"])
        mid_pull = jax.vjp(layer_norm, middle, gains[1], shifts[1])[1]
        grad_mid_part, gain_mid, shift_mid = mid_pull(grad_normed_mid)
        grad_mid = grad_res + grad_mid_part
        grad_branch = grad_mid.astype(BF)
        grad_attn = back_product(grad_branch, weights["out"]).astype(BF)
        bias_attn = jnp.sum(grad_branch.astype(F32), axis=0)
        start("up", up=(normed_mid, [(grad_gate, None)]), out=(attn_low, [(grad_branch, None)]))
        grad_attn = hooks[2](grad_attn)
        grad_attn = step(grad_attn, ["down"], begin=["up"])
        pairs = model // PAIR
        halves = (0, pairs // 2, pairs)

        def attend_back(half):
            first, count = halves[half], halves[half + 1] - halves[half]
            return attention_backward(
                query, mates, grad_attn, attn, lse, own_labels_across, key_labels, first, count
            )

        def add(near, far):
            both = total([near, far])
            if high > 1:
                both = lax.psum_scatter(both.astype(BF), "h", scatter_dimension=1, tiled=True)
            return both.astype(BF)

        def parts(query_low, both):
            return (normed, [(query_low, None), (both, 0), (both, 1)])

        query_low, near, sent = hooks[3](attend_back(0))
        query_low, near, sent, grad_attn = step((query_low, near, sent, grad_attn), ["down", "up"])
        far = grid.shift(sent, "c", 1)
        other_low, other_near, sent = attend_back(1)
        both = add(near, far)
        start("mix", qkv0=parts(query_low, both))
        other_low, other_near, sent, query_low, both = step(
            (other_low, other_near, sent, query_low, both),
            ["up"],
            begin=["mix"],
            got=["down"],
            rest=["down"],
        )
        far = grid.shift(sent, "c", 1)
        other_both = add(other_near, far)
        start("qkv1", qkv1=parts(other_low, other_both))
        query_low, both, other_low, other_both = step(
            (query_low, both, other_low, other_both), ["up", "mix"], begin=["qkv1"], got=["down"]
        )
        grad_mixed = jnp.concatenate(
            [query_low, other_low, both[0], other_both[0], both[1], other_both[1]], axis=1
        )
        grad_normed = back_product(grad_mixed, weights["qkv"])
        bias_query = jnp.sum(grad_mixed[:, :model].astype(F32), axis=0)
        bias_value = jnp.sum(grad_mixed[:, 2 * model :].astype(F32), axis=0)
        in_pull = jax.vjp(layer_norm, hidden, gains[0], shifts[0])[1]
        grad_in_part, gain_in, shift_in = in_pull(grad_normed)
        grad_start = grad_mid + grad_in_part
        grad_start = step(grad_start, ["mix", "qkv1"], got=["up"], rest=["up"])
        lead_sum = jnp.sum(grad_start, axis=0)
        vectors = jnp.concatenate(
            [
                jnp.stack([bias_query, bias_value, bias_attn, bias_down, gain_in, gain_mid, shift_in, shift_mid]),
                chooser[:, None] * lead_sum[None, :],
                bias_gate.reshape(blocks, -1, model // blocks).transpose(1, 0, 2).reshape(-1, model),
            ]
        )
        return (grad_start, operands, sums, vectors)

    result_first, saved_first = forward(
        start_low.astype(F32), leads[0], [before_exchange, after_attention, keep, after_gate]
    )
    first_low = result_first.astype(BF)
    first_low, seed_first, seed_second = tie((first_low, cotangent_first[0], cotangent_second[0]))
    moved = {"second": grid.swapped(seed_second)}

    def moves(begin, *names):
        def hook(values):
            values, taken = tie((values, {name: moved[name] for name in names}))
            moved.update(taken)
            if begin is None:
                return values
            values, sent = tie((values, begin[1]))
            moved[begin[0]] = grid.swapped(sent)
            return values

        return hook

    result_second, saved_second = forward(
        first_low.astype(F32),
        leads[1],
        [keep, moves(("first", seed_first), "second"), keep, moves(None, "first")],
    )
    second_low = result_second.astype(BF)
    seed_second = grid.choose(seed_second, moved["second"])
    seed_second, second_low = tie((seed_second, second_low))
    grad_between, operands, _, vectors_second = backward(
        saved_second,
        seed_second.astype(F32),
        None,
        [
            moves(("first_out", first_low)),
            moves(None, "first_out"),
            moves(("second_out", second_low)),
            moves(None, "second_out"),
        ],
    )
    seed_first = grid.choose(seed_first, moved["first"])
    first_low = grid.choose(first_low, moved["first_out"])
    second_low = grid.choose(second_low, moved["second_out"])
    grad_first, _, sums, vectors_first = backward(
        saved_first, seed_first.astype(F32) + grad_between, operands, [keep] * 4
    )
    vectors = vectors_second + vectors_first
    grad_low = grad_first.astype(BF)

    mix, qkv1, up = (sums[name] for name in ("mix", "qkv1", "up"))
    vectors, grad_low = advance((vectors, grad_low), [mix, qkv1], got=[up])
    mix.go(1)
    vectors = sum_near(grid, sum_near(grid, vectors, "c"), "y")
    vectors, grad_low = advance((vectors, grad_low), [qkv1])
    qkv1.go(1)
    grad_moved = grid.swapped(grad_low)
    vectors = sum_near(grid, vectors, "x")

    def block_at(step):
        place = {
            name: lax.rem(grid.at[name] + k, grid.size[name]) for name, k in zip("hz", step)
        }
        at = (place["h"] * grid.size["x"] + grid.at["x"]) * grid.size["z"] + place["z"]
        return lax.dynamic_slice_in_dim(vectors, at * (model // blocks), model // blocks, 1)

    vectors = total(
        [block_at((0, 0))]
        + [grid.far_shift(block_at(step), step) for step in grid.far_steps() if step != (0, 0)]
    )
    input_grad = grid.choose(grad_low, grad_moved).astype(F32)
    shares = {name: sums[name].result() for name in ("down", "up", "mix", "qkv1")}
    width = shares["qkv1"].shape[1] // 3
    sides = [shares["mix"], shares["qkv1"]]
    within = grid.at["y"] * 2 + grid.at["c"]
    own_columns = lax.dynamic_slice_in_dim(vectors, within * share, share, 1)
    small_out = [own_columns[cuts[i] : cuts[i + 1]] for i in range(4)]
    up_at = within * own_up
    up_width = model // blocks
    up_out = lax.dynamic_slice(
        vectors, (cuts[4] + up_at // up_width, up_at % up_width), (1, own_up)
    )[0]
    return (
        first_low[None],
        second_low[None],
        input_grad[None],
        jnp.concatenate([p[:, i * width : (i + 1) * width] for i in range(3) for p in sides], axis=1),
        shares["up"][:, w_up.shape[1] :],
        shares["up"][:, : w_up.shape[1]],
        shares["down"],
        small_out[0],
        up_out,
        small_out[1],
        small_out[2],
        small_out[3],
    )


def solution(mesh):
    dp, fsdp = mesh.shape["dp"], mesh.shape["fsdp"]
    tall = fsdp // 8
    sizes = {"h": dp // 2, "x": 2, "z": 4, "y": tall, "c": 2}
    fine = Mesh(np.asarray(mesh.devices).reshape(tuple(sizes.values())), tuple(sizes))
    one, two, every = ("z", "y", "c"), ("h", "x"), ("h", "x", "z", "y", "c")
    placed = (
        P(one, two, None),
        P(one, two),
        P(one, two),
        P(one, None),
        P(one, two, None),
        P(one, two, None),
        P(every, None),
        P(every, None),
        P(every, None),
        P(every, None),
        P(None, every),
        P(every),
        P(None, every),
        P(None, every),
        P(None, every),
    )
    return jax.shard_map(
        partial(body, sizes),
        mesh=fine,
        in_specs=placed,
        out_specs=(
            P(one, two, None),
            P(one, two, None),
            P(one, two, None),
            P(every, None),
            P(every, None),
            P(every, None),
            P(every, None),
            P(None, every),
            P(every),
            P(None, every),
            P(None, every),
            P(None, every),
        ),
        check_vma=False,
    )
```
